512 devices in a mesh: fsdp: 8 (over y_lo, x), ctx: 64 (over y_hi, z, core).
Axes of the slice: x: 4, y: 4 (y_hi: 2, y_lo: 2; y = y_hi * 2 + y_lo), z: 16, core: 2. Of those that a mesh axis runs over, the one named last changes fastest.
Arguments:
- latents: float32 [8192, 64], P('ctx'), may hold values from -15 to 15
- stream: bfloat16 [8192, 3072], P('ctx'), may hold values from -6 to 6
- queries: bfloat16 [8192, 2048], P('ctx', 'fsdp'), may hold values from -200 to 200
- key_rows: bfloat16 [8192, 2048], P('ctx', 'fsdp'), may hold values from -4 to 4
- value_rows: bfloat16 [8192, 2048], P('ctx', 'fsdp'), may hold values from -6 to 6
- w_mix: bfloat16 [2048, 3072], P('fsdp', 'ctx'), may hold values from -0.25 to 0.25
- w_head: bfloat16 [3072, 128], P('fsdp'), may hold values from -0.0390625 to 0.0390625
Outputs:
- flipped: float32 [8192, 64], P('ctx')
- head_grad: float32 [3072, 128], P('fsdp')
The draws below stay inside these ranges and needn't reach their ends.
All inputs are finite; a program needn't handle non-finite values.
Results may differ from the reference program's by a relative error of at most 0.003.
The reference program's roundings to bfloat16 on the way (of `attended`) count: a program that leaves them out, or rounds other values in their place, can miss the bound.
Values may be sent and summed in bfloat16 or wider, within the bound.
A program may use at most 64 MiB of HBM per device.

```python
import jax
import jax.numpy as jnp
from jax import lax

D = 3072
HEADS = 16
HD = 128
C = 64
TOK = 128
SEQ = 8192


def drawn_pair(key):
    width = HEADS * HD
    query_key = jax.random.fold_in(key, 101)
    keys_key = jax.random.fold_in(key, 102)
    queries = jnp.clip(jax.random.normal(query_key, (SEQ, width), jnp.float32), -4.0, 4.0) * 2.5
    key_rows = jnp.clip(jax.random.normal(keys_key, (SEQ, width), jnp.float32), -4.0, 4.0)
    return (queries, key_rows)


def draw_queries(key, part):
    return drawn_pair(key)[0].astype(jnp.bfloat16)


def draw_key_rows(key, part):
    return drawn_pair(key)[1].astype(jnp.bfloat16)


def draw_latents(key, part):
    base_key = jax.random.fold_in(key, 201)
    base = jnp.clip(jax.random.normal(base_key, (SEQ, C), jnp.float32), -6.0, 6.0)
    rows = jnp.arange(SEQ, dtype=jnp.int32)
    boost = jnp.where(rows % TOK == 0, 2.5, 1.0).astype(jnp.float32)
    return jnp.clip(base, -6.0, 6.0) * boost[:, None]


def level_of(own_key, dims, cuts, smallest, largest):
    gain, own = 1.0, jax.random.fold_in(own_key, 6)
    for axis_at, parts in cuts:
        draws = jnp.exp(jax.random.uniform(jax.random.fold_in(own, axis_at), (parts,), jnp.float32, smallest / len(cuts), largest / len(cuts)))
        gain = gain * jnp.repeat(draws, dims[axis_at] // parts).reshape([-1 if axis == axis_at else 1 for axis in range(len(dims))])
    return gain


def centred(rng, shape, deviation, bound, cuts=(), kind=jnp.bfloat16):
    entries = jax.random.normal(rng, shape, jnp.float32) * deviation
    if len(cuts) > 0:
        entries = level_of(rng, shape, cuts, -0.22, 0.18) * entries
    return jnp.clip(entries, min=-bound, max=bound).astype(kind)


def setup_inputs(seed: int = 0) -> dict:
    seeds = jax.random.split(jax.random.key(seed), 8)
    return {
        "latents": draw_latents(jax.random.fold_in(seeds[7], 71), 0),
        "stream": centred(seeds[1], (SEQ, D), 1.0, 6.0, ((0, 64),)),
        "queries": draw_queries(jax.random.fold_in(seeds[7], 71), 0),
        "key_rows": draw_key_rows(jax.random.fold_in(seeds[7], 71), 0),
        "value_rows": centred(seeds[4], (SEQ, HEADS * HD), 1.0, 6.0, ((0, 64), (1, 8))),
        "w_mix": centred(seeds[5], (HEADS * HD, D), (HEADS * HD // 4) ** -0.5, 0.25, ((0, 8), (1, 64))),
        "w_head": centred(seeds[6], (D, 2 * C), (8 * D) ** -0.5, 0.0390625, ((0, 8),)),
    }


def attend(queries, key_rows, value_rows):
    seq_len = queries.shape[0]
    block_len = min(512, seq_len)
    score_scale = HD ** -0.5
    key_heads = key_rows.astype(jnp.float32).reshape(seq_len, HEADS, HD)
    value_heads = value_rows.astype(jnp.float32).reshape(seq_len, HEADS, HD)
    key_pos = jnp.arange(seq_len, dtype=jnp.int32)

    def one_block(offset):
        picked = lax.dynamic_slice_in_dim(queries, offset, block_len, 0)
        query_heads = picked.astype(jnp.float32).reshape(block_len, HEADS, HD)
        scores = jnp.einsum("qhd,khd->hqk", query_heads, key_heads) * score_scale
        query_pos = offset + jnp.arange(block_len, dtype=jnp.int32)
        causal = key_pos[None, :] <= query_pos[:, None]
        scores = jnp.where(causal[None], scores, -1e30)
        row_max = jnp.max(scores, axis=-1, keepdims=True)
        weights = jnp.where(causal[None], jnp.exp(scores - row_max), 0.0)
        row_sum = jnp.sum(weights, axis=-1)
        rounded = lax.optimization_barrier(weights.astype(jnp.bfloat16)).astype(jnp.float32)
        numer = jnp.einsum("hqk,khd->hqd", rounded, value_heads)
        output = numer / row_sum[..., None]
        return jnp.transpose(output, (1, 0, 2)).reshape(block_len, HEADS * HD).astype(jnp.bfloat16)

    offsets = jnp.arange(0, seq_len, block_len, dtype=jnp.int32)
    blocks = lax.map(one_block, offsets)
    return blocks.reshape(seq_len, HEADS * HD)


def reference(latents, stream, queries, key_rows, value_rows, w_mix, w_head):
    attended = attend(queries, key_rows, value_rows)
    mixed = jnp.dot(attended, w_mix, preferred_element_type=jnp.float32)
    resid = stream.astype(jnp.float32) + mixed
    pred = jnp.dot(resid, w_head.astype(jnp.float32), precision=lax.Precision.HIGHEST)
    prior = jnp.concatenate([jnp.zeros((1, 2 * C), jnp.float32), pred[:-1]], axis=0)
    shift_part = prior[:, :C]
    log_scale = prior[:, C:]
    inverse = jnp.exp(-log_scale)
    white = (latents - shift_part) * inverse
    loss_scale = float(SEQ) ** -0.5
    d_prior = jnp.concatenate([-white * inverse, 1.0 - white * white], axis=1) * loss_scale
    d_pred = jnp.concatenate([d_prior[1:], jnp.zeros((1, 2 * C), jnp.float32)], axis=0)
    head_grad = jnp.dot(resid.T, d_pred, precision=lax.Precision.HIGHEST)
    return white[::-1], head_grad
```

```python
import functools
import math

import jax
import jax.numpy as jnp
from jax import lax
from jax.experimental import pallas as pl
from jax.experimental.pallas import tpu as pltpu
from jax.sharding import PartitionSpec as P

HD = 128
MESH = pl.DeviceIdType.MESH
F32, BF16 = jnp.float32, jnp.bfloat16
NT_DIMS = (((1,), (1,)), ((), ()))
SCALE = HD**-0.5 * math.log2(math.e)


def remote(src, dst, send, recv, f, c):
    return pltpu.make_async_remote_copy(
        src_ref=src, dst_ref=dst, send_sem=send, recv_sem=recv, device_id=(f, c), device_id_type=MESH
    )


def greet(barrier, f, c):
    pl.semaphore_signal(barrier, inc=1, device_id=(f, c), device_id_type=MESH)


class Place:
    def __init__(self, F, C):
        self.F, self.C, self.Z = F, C, C // 4
        self.f, self.c = lax.axis_index("fsdp"), lax.axis_index("ctx")
        self.row = self.f // (F // 2)
        self.half = self.c // (C // 2)
        self.z = lax.rem(self.c, C // 2) // 2
        self.k = lax.rem(self.c, 2)
        self.sib = self.c + 1 - 2 * self.k
        self.mate = lax.rem(self.c + C // 2, C)

    def at(self, half, z, k):
        return half * (self.C // 2) + z * 2 + k

    def zrel(self, by):
        return lax.rem(self.z + by + self.Z, self.Z)


def dot_nt(a, b):
    return lax.dot_general(a, b, NT_DIMS, preferred_element_type=F32)


def split3(x):
    a = x.astype(BF16)
    rest = x - a.astype(F32)
    b = rest.astype(BF16)
    return a, b, (rest - b.astype(F32)).astype(BF16)


def attend_kernel(
    F, C, q_ref, k_ref, v_ref, w_ref, att_ref, wt_ref,
    kbuf, vbuf, wbuf, q2, m_s, l_s, acc_s, o_in, st_out, st_in, tbuf,
    ring_send, ring_recv, sib_send, sib_recv, w_send, w_recv, w2_send, w2_recv, ws_sem, q_sem, o_send, o_recv,
):
    p = Place(F, C)
    f, z, k, half, Z = p.f, p.z, p.k, p.half, p.Z
    steps, groups = Z // 2, F // 2
    per = Z // groups
    tok = q_ref.shape[0]
    wide = w_ref.shape[1]
    above, below = p.at(half, p.zrel(1), k), p.at(half, p.zrel(-1), k)

    barrier = pltpu.get_barrier_semaphore()
    for c in (above, below, p.sib, p.mate):
        greet(barrier, f, c)
    mine = p.row == half
    for g in range(groups):
        for h in range(2):
            fd, cd = half * groups + g, p.at(h, z, k)

            @pl.when(jnp.logical_not(jnp.logical_and(fd == f, cd == p.c)))
            def _():
                greet(barrier, fd, cd)

    for fs in range(F):
        cs = p.at(p.row, z, k)

        @pl.when(jnp.logical_not(jnp.logical_and(fs == f, cs == p.c)))
        def _():
            greet(barrier, fs, cs)

    kbuf[z, k] = k_ref[...]
    vbuf[z, k] = v_ref[...]
    wbuf[z] = w_ref[...]
    m_s[...] = jnp.full_like(m_s, -1e30)
    l_s[...] = jnp.zeros_like(l_s)
    acc_s[...] = jnp.zeros_like(acc_s)
    pl.semaphore_wait(barrier, 4 + 2 * F - 2 * mine.astype(jnp.int32))

    def buf(kind):
        return kbuf if kind % 2 == 0 else vbuf

    def origin(kind, s):
        return p.zrel(-s) if kind < 2 else p.zrel(s)

    def ring(kind, s, o):
        return remote(
            buf(kind).at[o, k], buf(kind).at[o, k], ring_send.at[kind, s], ring_recv.at[kind, s],
            f, above if kind < 2 else below,
        )

    def beside(kind, s, core):
        o = origin(kind, s)
        return remote(
            buf(kind).at[o, core], buf(kind).at[o, core], sib_send.at[kind, s], sib_recv.at[kind, s], f, p.sib
        )

    def wring(up, s, o):
        return remote(
            wbuf.at[o], wbuf.at[o], w_send.at[up, s], w_recv.at[up, s], f, above if up == 0 else below
        )

    for kind in (0, 2, 1, 3):
        ring(kind, 1, z).start()
    for up in (0, 1):
        wring(up, 1, z).start()
    for kind in (0, 1):
        beside(kind, 0, k).start()
    to_mate = remote(q_ref, q2, q_sem.at[0], q_sem.at[1], f, p.mate)

    @pl.when(half == 1)
    def _():
        to_mate.start()

    def fold(who, o, masked=False):
        for h in range(2):
            cols = slice(h * HD, (h + 1) * HD)
            q = (q_ref if who == 0 else q2)[:, cols]
            kk = kbuf[o, :, :, cols].reshape(2 * tok, HD)
            vv = vbuf[o, :, :, cols].reshape(2 * tok, HD)
            s = dot_nt(q, kk)
            if masked:
                row = k * tok + lax.broadcasted_iota(jnp.int32, s.shape, 0)
                s = jnp.where(lax.broadcasted_iota(jnp.int32, s.shape, 1) <= row, s, -1e30)
            s0, s1 = s[:, :tok], s[:, tok:]
            m_old = m_s[who, h]
            top = jnp.max(jnp.maximum(s0, s1), axis=1, keepdims=True)
            m_new = jnp.maximum(m_old, top)
            keep = jnp.exp2((m_old - m_new) * SCALE)
            p0 = jnp.exp2((s0 - m_new) * SCALE)
            p1 = jnp.exp2((s1 - m_new) * SCALE)
            m_s[who, h] = m_new
            l_s[who, h] = l_s[who, h] * keep + (p0 + p1)
            both = jnp.concatenate([p0.astype(BF16), p1.astype(BF16)], axis=1)
            acc_s[who, h] = acc_s[who, h] * keep + jnp.dot(both, vv, preferred_element_type=F32)

    def arrive(kind, s):
        o = origin(kind, s)
        ring(kind, s, o).wait_recv()
        last = steps if kind < 2 else steps - 1

        @pl.when(s < last)
        def _():
            ring(kind, s + 1, o).start()

        beside(kind, s, k).start()

    def w_arrive(up, s):
        o = p.zrel(-s) if up == 0 else p.zrel(s)
        wring(up, s, o).wait_recv()
        last = steps if up == 0 else steps - 1

        @pl.when(s < last)
        def _():
            wring(up, s + 1, o).start()

    def first_fold():
        beside(0, 0, 1 - k).wait_recv()
        beside(1, 0, 1 - k).wait_recv()

        @pl.when(half == 0)
        def _():
            to_mate.wait_recv()
            fold(1, z)

        fold(0, z, masked=True)

    def fold_step(s):
        for base in (0, 2):
            o = origin(base, s)
            beside(base, s, 1 - k).wait_recv()
            beside(base + 1, s, 1 - k).wait_recv()

            @pl.when(half == 0)
            def _():
                fold(1, o)

            seen = z >= s if base == 0 else z + s >= Z

            @pl.when(seen)
            def _():
                fold(0, o)

    def to_plane(g, h):
        return remote(
            wbuf.at[pl.ds(g * per, per)], wt_ref.at[:, k, :, pl.ds(pl.multiple_of(f * wide, wide), wide)],
            w2_send.at[g, h], w2_recv.at[f], half * groups + g, p.at(h, z, k),
        )

    def elsewhere(g, h):
        return jnp.logical_not(jnp.logical_and(half * groups + g == f, half == h))

    def spread_w():
        for g in range(groups):
            for h in range(2):

                @pl.when(elsewhere(g, h))
                def _():
                    to_plane(g, h).start()

        @pl.when(mine)
        def _():
            g = f - half * groups
            wt_ref[:, k, :, pl.ds(pl.multiple_of(f * wide, wide), wide)] = wbuf[pl.ds(g * per, per)]

    @pl.loop(1, steps + 1)
    def _(s):
        arrive(0, s)

        @pl.when(s < steps)
        def _():
            arrive(2, s)

        arrive(1, s)

        @pl.when(s < steps)
        def _():
            arrive(3, s)

        @pl.when(s <= steps // 2)
        def _():
            w_arrive(0, 2 * s - 1)
            w_arrive(1, 2 * s - 1)

        @pl.when(s == 1)
        def _():
            first_fold()

        @pl.when(s > 1)
        def _():
            fold_step(s - 1)

        @pl.when(s <= steps // 2)
        def _():
            w_arrive(0, 2 * s)

            @pl.when(2 * s < steps)
            def _():
                w_arrive(1, 2 * s)

        @pl.when(s == steps // 2)
        def _():
            spread_w()

    far = origin(0, steps)
    beside(0, steps, 1 - k).wait_recv()
    beside(1, steps, 1 - k).wait_recv()
    lane = lax.broadcasted_iota(jnp.int32, (tok, 128), 1)
    back = [
        remote(acc_s.at[1], o_in, o_send.at[0], o_recv.at[0], f, p.mate),
        remote(st_out, st_in, o_send.at[1], o_recv.at[1], f, p.mate),
    ]

    @pl.when(half == 0)
    def _():
        fold(1, far)
        back[0].start()
        stats = jnp.zeros((tok, 128), F32)
        for h in range(2):
            stats = jnp.where(lane == h, m_s[1, h], stats)
            stats = jnp.where(lane == 2 + h, jnp.sum(l_s[1, h], axis=1, keepdims=True), stats)
        st_out[...] = stats.T[:8]
        back[1].start()

    @pl.when(z >= steps)
    def _():
        fold(0, far)

    def from_plane(fs):
        return remote(
            wbuf.at[pl.ds(0, per)], wt_ref.at[:, k, :, pl.ds(fs * wide, wide)],
            w2_send.at[0, 0], w2_recv.at[fs], fs, p.at(p.row, z, k),
        )

    for fs in range(F):

        @pl.when(jnp.logical_not(jnp.logical_and(mine, fs == f)))
        def _():
            from_plane(fs).wait_recv()

    across = remote(wt_ref.at[:, k], wt_ref.at[:, k], ws_sem.at[0], ws_sem.at[1], f, p.sib)
    across.start()

    def store(h, acc, total):
        att_ref[:, h * HD : (h + 1) * HD] = (acc / total).astype(BF16)

    @pl.when(half == 0)
    def _():
        for h in range(2):
            store(h, acc_s[0, h], jnp.sum(l_s[0, h], axis=1, keepdims=True))

    @pl.when(half == 1)
    def _():
        back[0].wait_recv()
        back[1].wait_recv()
        tbuf[...] = jnp.zeros_like(tbuf)
        tbuf[:8] = st_in[...]
        stats = tbuf[...].T
        for h in range(2):
            m_a, l_a = m_s[0, h], jnp.sum(l_s[0, h], axis=1, keepdims=True)
            m_b = jnp.max(jnp.where(lane == h, stats, -3e38), axis=1, keepdims=True)
            l_b = jnp.sum(jnp.where(lane == 2 + h, stats, 0.0), axis=1, keepdims=True)
            m = jnp.maximum(m_a, m_b)
            e_a, e_b = jnp.exp2((m_a - m) * SCALE), jnp.exp2((m_b - m) * SCALE)
            store(h, acc_s[0, h] * e_a + o_in[h] * e_b, l_a * e_a + l_b * e_b)

    remote(wt_ref.at[:, 1 - k], wt_ref.at[:, 1 - k], ws_sem.at[0], ws_sem.at[1], f, p.sib).wait_recv()

    @pl.loop(1, steps + 1)
    def _(s):
        for kind in (0, 1):
            ring(kind, s, z).wait_send()
            beside(kind, s, k).wait_send()
        wring(0, s, z).wait_send()

        @pl.when(s < steps)
        def _():
            for kind in (2, 3):
                ring(kind, s, z).wait_send()
                beside(kind, s, k).wait_send()
            wring(1, s, z).wait_send()

    for kind in (0, 1):
        beside(kind, 0, k).wait_send()
    for g in range(groups):
        for h in range(2):

            @pl.when(elsewhere(g, h))
            def _():
                to_plane(g, h).wait_send()

    across.wait_send()

    @pl.when(half == 0)
    def _():
        back[0].wait_send()
        back[1].wait_send()

    @pl.when(half == 1)
    def _():
        to_mate.wait_send()


def attend(F, C, queries, key_rows, value_rows, w_t):
    tok, width = queries.shape
    cols, wide = w_t.shape
    Z = C // 4
    per = Z // (F // 2)
    n = Z // 2 + 1
    dma = pltpu.SemaphoreType.DMA
    vmem = pl.BlockSpec(memory_space=pltpu.VMEM)
    return pl.pallas_call(
        functools.partial(attend_kernel, F, C),
        out_shape=(
            jax.ShapeDtypeStruct((tok, width), BF16),
            jax.ShapeDtypeStruct((per, 2, cols, F * wide), BF16),
        ),
        in_specs=[vmem] * 4,
        out_specs=(vmem, vmem),
        scratch_shapes=[
            pltpu.VMEM((Z, 2, tok, width), BF16),
            pltpu.VMEM((Z, 2, tok, width), BF16),
            pltpu.VMEM((Z, cols, wide), BF16),
            pltpu.VMEM((tok, width), BF16),
            pltpu.VMEM((2, 2, tok, 128), F32),
            pltpu.VMEM((2, 2, tok, 128), F32),
            pltpu.VMEM((2, 2, tok, HD), F32),
            pltpu.VMEM((2, tok, HD), F32),
            pltpu.VMEM((8, tok), F32),
            pltpu.VMEM((8, tok), F32),
            pltpu.VMEM((128, tok), F32),
            dma((4, n)), dma((4, n)), dma((4, n)), dma((4, n)), dma((2, n)), dma((2, n)),
            dma((F // 2, 2)), dma((F,)), dma((2,)), dma((2,)), dma((2,)), dma((2,)),
        ],
        compiler_params=pltpu.CompilerParams(
            collective_id=0, has_side_effects=True, vmem_limit_bytes=40 * 1024 * 1024
        ),
        name="attend",
    )(queries, key_rows, value_rows, w_t)


def head_kernel(
    F, C, att_ref, wt_ref, stream_ref, wh_ref, lat_ref, flip_ref, hg_ref,
    attbuf, strm, edge_out, edge_in, lat128, pp, rs, pall, psum, flip_out, flip_in, last_out, last_in,
    part, cbuf, ybuf, ybuf_in, zbuf, rbuf, tile, full,
    strm_sem, att_send, att_recv, edge_sem, rs_send, rs_recv, ag_send, ag_recv, flip_sem, last_sem, core_sem, half_sem,
    zs_send, zs_recv, zg_send, zg_recv, half2_sem, core2_sem,
):
    p = Place(F, C)
    f, c, z, k, half, Z = p.f, p.c, p.z, p.k, p.half, p.Z
    tok, wide = att_ref.shape
    share = wh_ref.shape[0]
    chan = lat_ref.shape[1]
    reducers = zbuf.shape[0]
    prev, nxt = lax.rem(c + C - 1, C), lax.rem(c + 1, C)
    mirror, mirror2 = C - 1 - c, lax.rem(2 * C - 2 - c, C)
    own_last = mirror2 == c

    strm_copy = pltpu.make_async_copy(
        stream_ref.at[:, pl.ds(pl.multiple_of(f * share, 128), share)], strm, strm_sem.at[0]
    )
    strm_copy.start()

    barrier = pltpu.get_barrier_semaphore()

    @pl.loop(1, F)
    def _(r):
        greet(barrier, lax.rem(f + r, F), c)

    @pl.loop(1, Z)
    def _(r):
        greet(barrier, f, p.at(half, p.zrel(r), k))

    for other in (prev, nxt, p.sib, p.mate, mirror):
        greet(barrier, f, other)

    @pl.when(jnp.logical_not(own_last))
    def _():
        greet(barrier, f, mirror2)

    mine = pl.ds(pl.multiple_of(f * wide, wide), wide)
    attbuf[:, mine] = att_ref[...]
    lat128[...] = jnp.zeros_like(lat128)
    lat128[:, :chan] = lat_ref[...]
    edge_out[...] = lat128[:8]
    pl.semaphore_wait(barrier, (F - 1) + (Z - 1) + 6 - own_last.astype(jnp.int32))

    def att_copy(r):
        return remote(
            att_ref, attbuf.at[:, mine], att_send.at[r], att_recv.at[f], lax.rem(f + r, F), c
        )

    @pl.loop(1, F)
    def _(r):
        att_copy(r).start()

    edge = remote(edge_out, edge_in, edge_sem.at[0], edge_sem.at[1], f, prev)
    edge.start()

    strm_copy.wait()
    stream_t = strm[...].astype(F32).T
    wh_t = wh_ref[...].astype(F32).T.astype(BF16)
    edge.wait_recv()
    lat_rows = lat128[...]
    row = lax.broadcasted_iota(jnp.int32, lat_rows.shape, 0)
    lat_next = jnp.where(row == tok - 1, edge_in[0:1, :], pltpu.roll(lat_rows, tok - 1, 0)).T[:chan]

    @pl.loop(1, F)
    def _(r):
        fs = lax.rem(f + r, F)
        there = pl.ds(pl.multiple_of(fs * wide, wide), wide)
        remote(att_ref, attbuf.at[:, there], att_send.at[r], att_recv.at[fs], fs, c).wait_recv()

    resid = stream_t + dot_nt(wt_ref[...], attbuf[...])
    r_hi, r_mid, r_lo = split3(resid)
    partial = jnp.dot(wh_t, r_lo, preferred_element_type=F32)
    partial += jnp.dot(wh_t, r_mid, preferred_element_type=F32)
    partial += jnp.dot(wh_t, r_hi, preferred_element_type=F32)
    pp[...] = partial.reshape(pp.shape)

    @pl.loop(1, F)
    def _(r):
        to = lax.rem(f + r, F)
        remote(pp.at[to], rs.at[f], rs_send.at[r], rs_recv.at[f], to, c).start()

    rs[f] = pp[f]

    @pl.loop(1, F)
    def _(r):
        fs = lax.rem(f + r, F)
        remote(pp.at[fs], rs.at[fs], rs_send.at[r], rs_recv.at[fs], fs, c).wait_recv()

    psum[...] = jnp.sum(rs[...], axis=0)

    @pl.loop(1, F)
    def _(r):
        remote(psum, pall.at[f], ag_send.at[r], ag_recv.at[f], lax.rem(f + r, F), c).start()

    pall[f] = psum[...]

    @pl.loop(1, F)
    def _(r):
        fs = lax.rem(f + r, F)
        remote(psum, pall.at[fs], ag_send.at[r], ag_recv.at[fs], fs, c).wait_recv()

    pred = pall[...].reshape(2 * chan, tok)
    col = lax.broadcasted_iota(jnp.int32, (chan, tok), 1)
    final = jnp.logical_and(c == C - 1, col == tok - 1)
    shift = jnp.where(final, 0.0, pred[:chan])
    log_scale = jnp.where(final, 0.0, pred[chan:])
    inverse = jnp.exp(-log_scale)
    white = (lat_next - shift) * inverse
    loss_scale = float(tok * C) ** -0.5
    d_shift = jnp.where(final, 0.0, -white * inverse * loss_scale)
    d_log = jnp.where(final, 0.0, (1.0 - white * white) * loss_scale)
    d_hi, d_mid, d_lo = split3(jnp.concatenate([d_shift, d_log], axis=0))
    grad = dot_nt(r_hi, d_lo) + dot_nt(r_lo, d_hi) + dot_nt(r_mid, d_mid)
    grad += dot_nt(r_hi, d_mid) + dot_nt(r_mid, d_hi)
    grad += dot_nt(r_hi, d_hi)
    part[...] = grad.reshape(part.shape)

    core_copy = remote(part.at[1 - k], cbuf, core_sem.at[0], core_sem.at[1], f, p.sib)
    core_copy.start()

    r_i = lax.broadcasted_iota(jnp.int32, (tok, tok), 0)
    t_i = lax.broadcasted_iota(jnp.int32, (tok, tok), 1)
    swap = jnp.logical_or(t_i == tok - 2 - r_i, jnp.logical_and(r_i == tok - 1, t_i == tok - 1))
    swap = jnp.where(swap, 1.0, 0.0).astype(BF16)
    w_hi, w_mid, w_lo = split3(jnp.concatenate([white, white], axis=0))
    turned = dot_nt(swap, w_hi) + dot_nt(swap, w_mid) + dot_nt(swap, w_lo)
    low = lax.broadcasted_iota(jnp.int32, (tok // 2, 2 * chan), 1) < chan
    flip_out[...] = jnp.where(low, turned[: tok // 2], turned[tok // 2 :])
    last_out[...] = turned[tok - 8 :]
    flip_copy = remote(flip_out, flip_in, flip_sem.at[0], flip_sem.at[1], f, mirror)
    last_copy = remote(last_out, last_in, last_sem.at[0], last_sem.at[1], f, mirror2)

    core_copy.wait_recv()
    ybuf[...] = part[k] + cbuf[...]
    half_copy = remote(ybuf.at[1 - half], ybuf_in, half_sem.at[0], half_sem.at[1], f, p.mate)
    half_copy.start()
    flip_copy.start()

    @pl.when(own_last)
    def _():
        last_in[...] = last_out[...]

    @pl.when(jnp.logical_not(own_last))
    def _():
        last_copy.start()

    half_copy.wait_recv()
    zbuf[...] = ybuf[half].reshape(zbuf.shape) + ybuf_in[...].reshape(zbuf.shape)

    @pl.loop(1, Z)
    def _(r):
        to = p.zrel(r)

        @pl.when(to < reducers)
        def _():
            remote(zbuf.at[to], rbuf.at[z], zs_send.at[r], zs_recv.at[z], f, p.at(half, to, k)).start()

    @pl.when(z < reducers)
    def _():
        rbuf[z] = zbuf[z]

        @pl.loop(1, Z)
        def _(r):
            fs = p.zrel(r)
            remote(zbuf.at[0], rbuf.at[fs], zs_send.at[r], zs_recv.at[fs], f, p.at(half, fs, k)).wait_recv()

        tile[...] = jnp.sum(rbuf[...], axis=0)

        @pl.loop(1, Z)
        def _(r):
            remote(tile, full.at[k, half, z], zg_send.at[r], zg_recv.at[z], f, p.at(half, p.zrel(r), k)).start()

        full[k, half, z] = tile[...]

    @pl.loop(1, Z)
    def _(r):
        fs = p.zrel(r)

        @pl.when(fs < reducers)
        def _():
            remote(tile, full.at[k, half, fs], zg_send.at[r], zg_recv.at[fs], f, p.at(half, fs, k)).wait_recv()

    to_half = remote(full.at[k, half], full.at[k, half], half2_sem.at[0], half2_sem.at[1], f, p.mate)
    to_half.start()

    flip_copy.wait_recv()

    @pl.when(jnp.logical_not(own_last))
    def _():
        last_copy.wait_recv()

    got = flip_in[...]
    flip_ref[: tok // 2] = got[:, :chan]
    upper = pltpu.roll(got, chan, 1)[:, :chan]
    tail = lax.broadcasted_iota(jnp.int32, upper.shape, 0) == tok // 2 - 1
    flip_ref[tok // 2 :] = jnp.where(tail, last_in[7:8, :chan], upper)

    remote(full.at[k, 1 - half], full.at[k, 1 - half], half2_sem.at[0], half2_sem.at[1], f, p.mate).wait_recv()
    to_core = remote(full.at[k], full.at[k], core2_sem.at[0], core2_sem.at[1], f, p.sib)
    to_core.start()
    remote(full.at[1 - k], full.at[1 - k], core2_sem.at[0], core2_sem.at[1], f, p.sib).wait_recv()
    hg_ref[...] = full[...].reshape(hg_ref.shape)

    @pl.loop(1, F)
    def _(r):
        att_copy(r).wait_send()
        remote(pp.at[0], rs.at[0], rs_send.at[r], rs_recv.at[0], lax.rem(f + r, F), c).wait_send()
        remote(psum, pall.at[0], ag_send.at[r], ag_recv.at[0], lax.rem(f + r, F), c).wait_send()

    @pl.loop(1, Z)
    def _(r):
        to = p.zrel(r)

        @pl.when(to < reducers)
        def _():
            remote(zbuf.at[0], rbuf.at[0], zs_send.at[r], zs_recv.at[0], f, p.at(half, to, k)).wait_send()

        @pl.when(z < reducers)
        def _():
            remote(tile, full.at[0, 0, 0], zg_send.at[r], zg_recv.at[0], f, p.at(half, to, k)).wait_send()

    for copy in (edge, core_copy, half_copy, flip_copy, to_half, to_core):
        copy.wait_send()

    @pl.when(jnp.logical_not(own_last))
    def _():
        last_copy.wait_send()


def head(F, C, attended, wt, stream, w_head, latents):
    tok, wide = attended.shape
    share, chan2 = w_head.shape
    chan = latents.shape[1]
    Z = C // 4
    tiles = share // 4 // 8
    each = -(-tiles // Z)
    reducers = tiles // each
    dma = pltpu.SemaphoreType.DMA
    vmem = pl.BlockSpec(memory_space=pltpu.VMEM)
    block = (each * 8, chan2)
    return pl.pallas_call(
        functools.partial(head_kernel, F, C),
        out_shape=(
            jax.ShapeDtypeStruct((tok, chan), F32),
            jax.ShapeDtypeStruct((share, chan2), F32),
        ),
        in_specs=[vmem, vmem, pl.BlockSpec(memory_space=pl.ANY), vmem, vmem],
        out_specs=(vmem, vmem),
        scratch_shapes=[
            pltpu.VMEM((tok, F * wide), BF16),
            pltpu.VMEM((tok, share), BF16),
            pltpu.VMEM((8, 128), F32),
            pltpu.VMEM((8, 128), F32),
            pltpu.VMEM((tok, 128), F32),
            pltpu.VMEM((F, chan2 // F, tok), F32),
            pltpu.VMEM((F, chan2 // F, tok), F32),
            pltpu.VMEM((F, chan2 // F, tok), F32),
            pltpu.VMEM((chan2 // F, tok), F32),
            pltpu.VMEM((tok // 2, chan2), F32),
            pltpu.VMEM((tok // 2, chan2), F32),
            pltpu.VMEM((8, chan2), F32),
            pltpu.VMEM((8, chan2), F32),
            pltpu.VMEM((2, 2, reducers) + block, F32),
            pltpu.VMEM((2, reducers) + block, F32),
            pltpu.VMEM((2, reducers) + block, F32),
            pltpu.VMEM((reducers,) + block, F32),
            pltpu.VMEM((reducers,) + block, F32),
            pltpu.VMEM((Z,) + block, F32),
            pltpu.VMEM(block, F32),
            pltpu.VMEM((2, 2, reducers) + block, F32),
            dma((1,)), dma((F,)), dma((F,)), dma((2,)), dma((F,)), dma((F,)), dma((F,)), dma((F,)),
            dma((2,)), dma((2,)), dma((2,)), dma((2,)),
            dma((Z,)), dma((Z,)), dma((Z,)), dma((Z,)), dma((2,)), dma((2,)),
        ],
        compiler_params=pltpu.CompilerParams(
            collective_id=1, has_side_effects=True, vmem_limit_bytes=40 * 1024 * 1024
        ),
        name="head",
    )(attended, wt, stream, w_head, latents)


def shards(F, C, latents, stream, queries, key_rows, value_rows, w_mix, w_head):
    attended, wt = attend(F, C, queries, key_rows, value_rows, w_mix.T)
    wt = wt.reshape(-1, wt.shape[-1])
    return head(F, C, attended, wt, stream, w_head, latents)


def solution(mesh):
    return jax.shard_map(
        functools.partial(shards, mesh.shape["fsdp"], mesh.shape["ctx"]),
        mesh=mesh,
        in_specs=(
            P("ctx", None),
            P("ctx", None),
            P("ctx", "fsdp"),
            P("ctx", "fsdp"),
            P("ctx", "fsdp"),
            P("fsdp", "ctx"),
            P("fsdp", None),
        ),
        out_specs=(P("ctx", None), P("fsdp", None)),
        check_vma=False,
    )
```

```python
import functools
import math

import jax
import jax.numpy as jnp
from jax import lax
from jax.experimental import pallas as pl
from jax.experimental.pallas import tpu as pltpu
from jax.sharding import PartitionSpec as P

HD = 128
MESH = pl.DeviceIdType.MESH
F32, BF16 = jnp.float32, jnp.bfloat16
NT_DIMS = (((1,), (1,)), ((), ()))
SCALE = HD**-0.5 * math.log2(math.e)


def remote(src, dst, send, recv, f, c):
    return pltpu.make_async_remote_copy(
        src_ref=src, dst_ref=dst, send_sem=send, recv_sem=recv, device_id=(f, c), device_id_type=MESH
    )


def greet(barrier, f, c):
    pl.semaphore_signal(barrier, inc=1, device_id=(f, c), device_id_type=MESH)


class Place:
    def __init__(self, F, C):
        self.F, self.C, self.Z = F, C, C // 4
        self.f, self.c = lax.axis_index("fsdp"), lax.axis_index("ctx")
        self.row = self.f // (F // 2)
        self.half = self.c // (C // 2)
        self.z = lax.rem(self.c, C // 2) // 2
        self.k = lax.rem(self.c, 2)
        self.sib = self.c + 1 - 2 * self.k
        self.mate = lax.rem(self.c + C // 2, C)
        self.prev, self.next = lax.rem(self.c + C - 1, C), lax.rem(self.c + 1, C)

    def at(self, half, z, k):
        return half * (self.C // 2) + z * 2 + k

    def plane(self, r):
        i = lax.rem(self.half * self.F + self.f + r, 2 * self.F)
        return lax.rem(i, self.F), self.at(i // self.F, self.z, self.k)

    def zrel(self, by):
        return lax.rem(self.z + by + self.Z, self.Z)


def dot_nt(a, b):
    return lax.dot_general(a, b, NT_DIMS, preferred_element_type=F32)


def split3(x):
    a = x.astype(BF16)
    rest = x - a.astype(F32)
    b = rest.astype(BF16)
    return a, b, (rest - b.astype(F32)).astype(BF16)


def entry(p, q_ref, k_ref, v_ref, w_ref, kbuf, vbuf, wbuf, qbuf, in_sem):
    z, k = p.z, p.k
    loads = [
        pltpu.make_async_copy(k_ref, kbuf.at[z, k], in_sem.at[0]),
        pltpu.make_async_copy(v_ref, vbuf.at[z, k], in_sem.at[1]),
        pltpu.make_async_copy(w_ref, wbuf.at[z], in_sem.at[2]),
        pltpu.make_async_copy(q_ref, qbuf, in_sem.at[3]),
    ]
    for load in loads:
        load.start()
    barrier = pltpu.get_barrier_semaphore()
    for c in (p.at(p.half, p.zrel(1), k), p.at(p.half, p.zrel(-1), k), p.sib, p.prev, p.next):
        greet(barrier, p.f, c)
    for r in (2, -2):
        greet(barrier, p.f, p.at(p.half, p.zrel(r), k))

    @pl.loop(1, 2 * p.F)
    def _(r):
        greet(barrier, *p.plane(r))

    for load in loads:
        load.wait()
    pl.semaphore_wait(barrier, 7 + 2 * p.F - 1)


class Weights:
    def __init__(
        self, p, wbuf, whv, stream, sp, mp, m_in, m_half, m_in2, mall,
        wh_send, wh_recv, whs_sem, ms_sem, mm_sem, mg_send, mg_recv, mx_sem,
    ):
        self.p, self.wbuf, self.whv, self.stream, self.sp = p, wbuf, whv, stream, sp
        self.mp, self.m_in, self.m_half, self.m_in2, self.mall = mp, m_in, m_half, m_in2, mall
        self.wh_sems, self.mg_sems = (wh_send, wh_recv), (mg_send, mg_recv)
        f, k = p.f, p.k
        self.whs_sem, self.mx_sem = whs_sem, mx_sem
        self.to_sib = remote(mp.at[1 - k], m_in, ms_sem.at[0], ms_sem.at[1], f, p.sib)
        self.to_mate = remote(m_half, m_in2, mm_sem.at[0], mm_sem.at[1], f, p.mate)

    def own(self, fs):
        groups = self.p.F // 2
        per = self.p.Z // groups
        return fs // groups, lax.rem(fs, groups) * per, per

    def rows(self, fs, core):
        h, at, per = self.own(fs)
        return self.whv.at[h, pl.ds(at + core * (per // 2), per // 2)]

    def head_copy(self, r, fs):
        p = self.p
        send, recv = self.wh_sems
        return remote(self.rows(fs, p.k), self.rows(fs, p.k), send.at[r], recv.at[fs], lax.rem(p.f + r, p.F), p.c)

    def beside(self, core, fs):
        return remote(
            self.rows(fs, core), self.rows(fs, core), self.whs_sem.at[0, fs], self.whs_sem.at[1, fs], self.p.f, self.p.sib
        )

    def start(self):
        @pl.loop(1, self.p.F)
        def _(r):
            self.head_copy(r, self.p.f).start()

    def share(self):
        p = self.p

        @pl.loop(1, p.F)
        def _(r):
            fs = lax.rem(p.f + r, p.F)
            self.head_copy(r, fs).wait_recv()
            self.beside(p.k, fs).start()

    def partial(self):
        p = self.p

        @pl.loop(1, p.F)
        def _(r):
            self.beside(1 - p.k, lax.rem(p.f + r, p.F)).wait_recv()

        width = self.wbuf.shape[2]
        rows = self.whv[p.half, :, p.k].reshape(-1, 128)
        pieces = self.wbuf[...].reshape(-1, width)
        out = jnp.dot(rows.astype(F32).T.astype(BF16), pieces, preferred_element_type=F32)
        self.mp[...] = out.reshape(self.mp.shape)
        self.to_sib.start()
        self.sp[...] = jnp.dot(self.stream[...], self.whv[...].reshape(-1, 128), preferred_element_type=F32).T

    def halves(self):
        self.to_sib.wait_recv()
        self.m_half[...] = self.mp[self.p.k] + self.m_in[...]
        self.to_mate.start()

    def lanes(self, fs):
        width = self.mp.shape[2]
        return pl.ds(pl.multiple_of(fs * width, width), width)

    def all_copy(self, r, fs):
        p = self.p
        send, recv = self.mg_sems
        dst = self.mall.at[p.k, :, self.lanes(fs)]
        return remote(dst, dst, send.at[r], recv.at[fs], lax.rem(p.f + r, p.F), p.c)

    def gather(self):
        p = self.p
        self.to_mate.wait_recv()
        self.mall[p.k, :, self.lanes(p.f)] = self.m_half[...] + self.m_in2[...]

        @pl.loop(1, p.F)
        def _(r):
            self.all_copy(r, p.f).start()

    def across(self, core):
        return remote(self.mall.at[core], self.mall.at[core], self.mx_sem.at[0], self.mx_sem.at[1], self.p.f, self.p.sib)

    def finish(self):
        p = self.p

        @pl.loop(1, p.F)
        def _(r):
            self.all_copy(r, lax.rem(p.f + r, p.F)).wait_recv()

        self.across(p.k).start()
        self.across(1 - p.k).wait_recv()

    def drain(self):
        p = self.p

        @pl.loop(1, p.F)
        def _(r):
            self.head_copy(r, p.f).wait_send()
            self.beside(p.k, lax.rem(p.f + r, p.F)).wait_send()
            self.all_copy(r, p.f).wait_send()

        self.to_sib.wait_send()
        self.to_mate.wait_send()
        self.across(p.k).wait_send()


def attend_phase(
    p, weights, q_ref, kbuf, vbuf, wbuf, q2, m_s, l_s, acc_s, o_in, st_out, st_in, tbuf, att_ref, wt_ref,
    ring_send, ring_recv, sib_send, sib_recv, w_send, w_recv, w2_send, w2_recv, ws_sem, q_sem, o_send, o_recv,
):
    F = p.F
    f, z, k, half, Z = p.f, p.z, p.k, p.half, p.Z
    steps, groups = Z // 2, F // 2
    per = Z // groups
    tok = q_ref.shape[0]
    wide = wbuf.shape[2]
    above, below = p.at(half, p.zrel(1), k), p.at(half, p.zrel(-1), k)
    mine = p.row == half

    m_s[...] = jnp.full_like(m_s, -1e30)
    l_s[...] = jnp.zeros_like(l_s)
    acc_s[...] = jnp.zeros_like(acc_s)

    def buf(kind):
        return kbuf if kind % 2 == 0 else vbuf

    def origin(kind, s):
        return p.zrel(-s) if kind < 2 else p.zrel(s)

    def ring(kind, s, o):
        return remote(
            buf(kind).at[o, k], buf(kind).at[o, k], ring_send.at[kind, s], ring_recv.at[kind, s],
            f, above if kind < 2 else below,
        )

    def beside(kind, s, core):
        o = origin(kind, s)
        return remote(
            buf(kind).at[o, core], buf(kind).at[o, core], sib_send.at[kind, s], sib_recv.at[kind, s], f, p.sib
        )

    def wring(up, dist, o):
        by = 2 - dist % 2 if isinstance(dist, int) else 2 - lax.rem(dist, 2)
        to = p.zrel(by) if up == 0 else p.zrel(-by)
        return remote(
            wbuf.at[o], wbuf.at[o], w_send.at[up, dist], w_recv.at[up, dist], f, p.at(half, to, k)
        )

    for kind in (0, 2, 1, 3):
        ring(kind, 1, z).start()
    for up in (0, 1):
        wring(up, 1, z).start()
        wring(up, 2, z).start()
    for kind in (0, 1):
        beside(kind, 0, k).start()
    to_mate = remote(q_ref, q2, q_sem.at[0], q_sem.at[1], f, p.mate)

    @pl.when(half == 1)
    def _():
        to_mate.start()

    weights.start()

    def fold(who, o, masked=False):
        for h in range(2):
            cols = slice(h * HD, (h + 1) * HD)
            q = (q_ref if who == 0 else q2)[:, cols]
            kk = kbuf[o, :, :, cols].reshape(2 * tok, HD)
            vv = vbuf[o, :, :, cols].reshape(2 * tok, HD)
            s = dot_nt(q, kk)
            if masked:
                row = k * tok + lax.broadcasted_iota(jnp.int32, s.shape, 0)
                s = jnp.where(lax.broadcasted_iota(jnp.int32, s.shape, 1) <= row, s, -1e30)
            s0, s1 = s[:, :tok], s[:, tok:]
            m_old = m_s[who, h]
            top = jnp.max(jnp.maximum(s0, s1), axis=1, keepdims=True)
            m_new = jnp.maximum(m_old, top)
            keep = jnp.exp2((m_old - m_new) * SCALE)
            p0 = jnp.exp2((s0 - m_new) * SCALE)
            p1 = jnp.exp2((s1 - m_new) * SCALE)
            m_s[who, h] = m_new
            l_s[who, h] = l_s[who, h] * keep + (p0 + p1)
            both = jnp.concatenate([p0.astype(BF16), p1.astype(BF16)], axis=1)
            acc_s[who, h] = acc_s[who, h] * keep + jnp.dot(both, vv, preferred_element_type=F32)

    def arrive(kind, s):
        o = origin(kind, s)
        ring(kind, s, o).wait_recv()
        last = steps if kind < 2 else steps - 1

        @pl.when(s < last)
        def _():
            ring(kind, s + 1, o).start()

        beside(kind, s, k).start()

    def w_origin(up, dist):
        return p.zrel(-dist) if up == 0 else p.zrel(dist)

    def w_arrive(s):
        for up in (0, 1):
            last = steps if up == 0 else steps - 1
            o = w_origin(up, 2 * s - 1)
            wring(up, 2 * s - 1, o).wait_recv()
            to_plane(o)

            @pl.when(2 * s <= last)
            def _():
                o = w_origin(up, 2 * s)
                wring(up, 2 * s, o).wait_recv()

                @pl.when(2 * s + 1 <= last)
                def _():
                    wring(up, 2 * s + 1, o).start()

                @pl.when(2 * s + 2 <= last)
                def _():
                    wring(up, 2 * s + 2, o).start()

                to_plane(o)

    def plane_copy(o, h):
        return remote(
            wbuf.at[o], wt_ref.at[lax.rem(o, per), k, :, pl.ds(pl.multiple_of(f * wide, wide), wide)],
            w2_send.at[o, h], w2_recv.at[f], half * groups + o // per, p.at(h, z, k),
        )

    def is_self(o, h):
        return jnp.logical_and(half * groups + o // per == f, half == h)

    def to_plane(o):
        for h in range(2):

            @pl.when(jnp.logical_not(is_self(o, h)))
            def _():
                plane_copy(o, h).start()

            @pl.when(is_self(o, h))
            def _():
                wt_ref[lax.rem(o, per), k, :, pl.ds(pl.multiple_of(f * wide, wide), wide)] = wbuf[o]

    def first_fold():
        beside(0, 0, 1 - k).wait_recv()
        beside(1, 0, 1 - k).wait_recv()

        @pl.when(half == 0)
        def _():
            to_mate.wait_recv()
            fold(1, z)

        fold(0, z, masked=True)

    def fold_step(s):
        for base in (0, 2):
            o = origin(base, s)
            beside(base, s, 1 - k).wait_recv()
            beside(base + 1, s, 1 - k).wait_recv()

            @pl.when(half == 0)
            def _():
                fold(1, o)

            seen = z >= s if base == 0 else z + s >= Z

            @pl.when(seen)
            def _():
                fold(0, o)

    to_plane(z)

    def from_plane(fs):
        return remote(
            wbuf.at[pl.ds(0, per)], wt_ref.at[:, k, :, pl.ds(fs * wide, wide)],
            w2_send.at[0, 0], w2_recv.at[fs], fs, p.at(p.row, z, k),
        )

    across = remote(wt_ref.at[:, k], wt_ref.at[:, k], ws_sem.at[0], ws_sem.at[1], f, p.sib)

    def collect():
        for fs in range(F):

            @pl.when(jnp.logical_not(jnp.logical_and(mine, fs == f)))
            def _():
                from_plane(fs).wait_recv()

        across.start()

    @pl.loop(1, steps + 1)
    def _(s):
        arrive(0, s)

        @pl.when(s < steps)
        def _():
            arrive(2, s)

        arrive(1, s)

        @pl.when(s < steps)
        def _():
            arrive(3, s)

        @pl.when(s <= steps // 2)
        def _():
            w_arrive(s)

        @pl.when(s == 3)
        def _():
            weights.share()

        @pl.when(s == steps // 2)
        def _():
            weights.partial()

        @pl.when(s == steps // 2 + 1)
        def _():
            weights.halves()

        @pl.when(s == steps - 1)
        def _():
            weights.gather()
            collect()

        @pl.when(s == 1)
        def _():
            first_fold()

        @pl.when(s > 1)
        def _():
            fold_step(s - 1)

    far = origin(0, steps)
    beside(0, steps, 1 - k).wait_recv()
    beside(1, steps, 1 - k).wait_recv()
    lane = lax.broadcasted_iota(jnp.int32, (tok, 128), 1)
    back = [
        remote(acc_s.at[1], o_in, o_send.at[0], o_recv.at[0], f, p.mate),
        remote(st_out, st_in, o_send.at[1], o_recv.at[1], f, p.mate),
    ]

    @pl.when(half == 0)
    def _():
        fold(1, far)
        back[0].start()
        stats = jnp.zeros((tok, 128), F32)
        for h in range(2):
            stats = jnp.where(lane == h, m_s[1, h], stats)
            stats = jnp.where(lane == 2 + h, jnp.sum(l_s[1, h], axis=1, keepdims=True), stats)
        st_out[...] = stats.T[:8]
        back[1].start()

    @pl.when(z >= steps)
    def _():
        fold(0, far)

    def store(h, acc, total):
        att_ref[:, h * HD : (h + 1) * HD] = (acc / total).astype(BF16)

    @pl.when(half == 0)
    def _():
        for h in range(2):
            store(h, acc_s[0, h], jnp.sum(l_s[0, h], axis=1, keepdims=True))

    @pl.when(half == 1)
    def _():
        back[0].wait_recv()
        back[1].wait_recv()
        tbuf[...] = jnp.zeros_like(tbuf)
        tbuf[:8] = st_in[...]
        stats = tbuf[...].T
        for h in range(2):
            m_a, l_a = m_s[0, h], jnp.sum(l_s[0, h], axis=1, keepdims=True)
            m_b = jnp.max(jnp.where(lane == h, stats, -3e38), axis=1, keepdims=True)
            l_b = jnp.sum(jnp.where(lane == 2 + h, stats, 0.0), axis=1, keepdims=True)
            m = jnp.maximum(m_a, m_b)
            e_a, e_b = jnp.exp2((m_a - m) * SCALE), jnp.exp2((m_b - m) * SCALE)
            store(h, acc_s[0, h] * e_a + o_in[h] * e_b, l_a * e_a + l_b * e_b)

    def early():
        weights.finish()
        remote(wt_ref.at[:, 1 - k], wt_ref.at[:, 1 - k], ws_sem.at[0], ws_sem.at[1], f, p.sib).wait_recv()

    def drain():
        attend_drain(p, ring, beside, wring, plane_copy, is_self, across, back, to_mate)

    return early, drain


def attend_drain(p, ring, beside, wring, plane_copy, is_self, across, back, to_mate):
    z, k, half, steps = p.z, p.k, p.half, p.Z // 2

    @pl.loop(1, steps + 1)
    def _(s):
        for kind in (0, 1):
            ring(kind, s, z).wait_send()
            beside(kind, s, k).wait_send()
        wring(0, s, z).wait_send()

        @pl.when(s < steps)
        def _():
            for kind in (2, 3):
                ring(kind, s, z).wait_send()
                beside(kind, s, k).wait_send()
            wring(1, s, z).wait_send()

    for kind in (0, 1):
        beside(kind, 0, k).wait_send()

    @pl.loop(0, p.Z)
    def _(o):
        for h in range(2):

            @pl.when(jnp.logical_not(is_self(o, h)))
            def _():
                plane_copy(o, h).wait_send()

    across.wait_send()

    @pl.when(half == 0)
    def _():
        back[0].wait_send()
        back[1].wait_send()

    @pl.when(half == 1)
    def _():
        to_mate.wait_send()


def head_phase(
    p, early, att_ref, wt_ref, stream, sp, mall, lat_ref, flip_ref, hg_ref,
    attbuf, edge_out, edge_in, flip_out, flip_in, last_out, last_in, part, cbuf, zbuf, rbuf, tile, full,
    att_send, att_recv, edge_sem, flip_sem, last_sem, core_sem, zs_send, zs_recv, zg_send, zg_recv, core2_sem,
):
    F, C = p.F, p.C
    f, c, z, k, half, Z = p.f, p.c, p.z, p.k, p.half, p.Z
    tok, wide = att_ref.shape
    chan = lat_ref.shape[0]
    reducers = zbuf.shape[0]
    mirror, mirror2 = C - 1 - c, lax.rem(2 * C - 2 - c, C)
    own_last = mirror2 == c
    lane = lax.broadcasted_iota(jnp.int32, (chan, tok), 1)

    def as_column(row):
        return jnp.broadcast_to(row, (tok, 128)).T

    mine = pl.ds(pl.multiple_of(f * wide, wide), wide)
    attbuf[:, mine] = att_ref[...]

    def att_copy(r):
        return remote(
            att_ref, attbuf.at[:, mine], att_send.at[r], att_recv.at[f], lax.rem(f + r, F), c
        )

    @pl.loop(1, F)
    def _(r):
        att_copy(r).start()

    lat_t = lat_ref[...]
    edge_out[...] = jnp.concatenate([lat_t, lat_t], axis=0).T[:8]
    edge = remote(edge_out, edge_in, edge_sem.at[0], edge_sem.at[1], f, p.prev)
    edge.start()
    share = hg_ref.shape[0]
    stream_t = stream[:, pl.ds(pl.multiple_of(f * share, 128), share)].astype(F32).T
    early()
    m_all = split3(mall[...].reshape(2 * chan, F * wide))
    edge.wait_recv()
    lat_next = jnp.where(lane == tok - 1, as_column(edge_in[0:1])[:chan], pltpu.roll(lat_t, tok - 1, 1))

    @pl.loop(1, F)
    def _(r):
        fs = lax.rem(f + r, F)
        there = pl.ds(pl.multiple_of(fs * wide, wide), wide)
        remote(att_ref, attbuf.at[:, there], att_send.at[r], att_recv.at[fs], fs, c).wait_recv()

    heads = attbuf[...]
    pred = sp[...] + (dot_nt(m_all[2], heads) + dot_nt(m_all[1], heads) + dot_nt(m_all[0], heads))
    resid = stream_t + dot_nt(wt_ref[...].reshape(share, F * wide), heads)
    r_hi, r_mid, r_lo = split3(resid)
    final = jnp.logical_and(c == C - 1, lane == tok - 1)
    shift = jnp.where(final, 0.0, pred[:chan])
    log_scale = jnp.where(final, 0.0, pred[chan:])
    inverse = jnp.exp(-log_scale)
    white = (lat_next - shift) * inverse
    loss_scale = float(tok * C) ** -0.5
    d_shift = jnp.where(final, 0.0, -white * inverse * loss_scale)
    d_log = jnp.where(final, 0.0, (1.0 - white * white) * loss_scale)
    d_hi, d_mid, d_lo = split3(jnp.concatenate([d_shift, d_log], axis=0))
    grad = dot_nt(r_hi, d_lo) + dot_nt(r_lo, d_hi) + dot_nt(r_mid, d_mid)
    grad += dot_nt(r_hi, d_mid) + dot_nt(r_mid, d_hi)
    grad += dot_nt(r_hi, d_hi)
    part[...] = grad.reshape(part.shape)

    core_copy = remote(part.at[1 - k], cbuf, core_sem.at[0], core_sem.at[1], f, p.sib)
    core_copy.start()

    t_i = lax.broadcasted_iota(jnp.int32, (tok, tok), 0)
    r_i = lax.broadcasted_iota(jnp.int32, (tok, tok), 1)
    swap = jnp.where(t_i == tok - 2 - r_i, 1.0, 0.0).astype(BF16)
    w_hi, w_mid, w_lo = split3(white)
    turned = jnp.dot(w_hi, swap, preferred_element_type=F32) + jnp.dot(w_mid, swap, preferred_element_type=F32)
    flip_out[...] = turned + jnp.dot(w_lo, swap, preferred_element_type=F32)
    last_out[...] = jnp.concatenate([white, white], axis=0).T[tok - 8 :]
    flip_copy = remote(flip_out, flip_in, flip_sem.at[0], flip_sem.at[1], f, mirror)
    last_copy = remote(last_out, last_in, last_sem.at[0], last_sem.at[1], f, mirror2)

    core_copy.wait_recv()
    zbuf[...] = part[k] + cbuf[...]
    ranks = 2 * Z
    me = half * Z + z

    def rank(r):
        i = lax.rem(me + r, ranks)
        return i, p.at(i // Z, lax.rem(i, Z), k)

    @pl.loop(1, ranks)
    def _(r):
        to, there = rank(r)

        @pl.when(to < reducers)
        def _():
            remote(zbuf.at[to], rbuf.at[me], zs_send.at[r], zs_recv.at[me], f, there).start()

    flip_copy.start()

    @pl.when(own_last)
    def _():
        last_in[...] = last_out[...]

    @pl.when(jnp.logical_not(own_last))
    def _():
        last_copy.start()

    @pl.when(me < reducers)
    def _():
        rbuf[me] = zbuf[me]

        @pl.loop(1, ranks)
        def _(r):
            i, there = rank(r)
            remote(zbuf.at[0], rbuf.at[i], zs_send.at[r], zs_recv.at[i], f, there).wait_recv()

        tile[...] = jnp.sum(rbuf[...], axis=0)

        @pl.loop(1, ranks)
        def _(r):
            remote(tile, full.at[k, me], zg_send.at[r], zg_recv.at[me], f, rank(r)[1]).start()

        full[k, me] = tile[...]

    flip_copy.wait_recv()

    @pl.when(jnp.logical_not(own_last))
    def _():
        last_copy.wait_recv()

    flip_ref[...] = jnp.where(lane == tok - 1, as_column(last_in[7:8])[:chan], flip_in[...])

    @pl.loop(1, ranks)
    def _(r):
        i, there = rank(r)

        @pl.when(i < reducers)
        def _():
            remote(tile, full.at[k, i], zg_send.at[r], zg_recv.at[i], f, there).wait_recv()

    to_core = remote(full.at[k], full.at[k], core2_sem.at[0], core2_sem.at[1], f, p.sib)
    to_core.start()
    remote(full.at[1 - k], full.at[1 - k], core2_sem.at[0], core2_sem.at[1], f, p.sib).wait_recv()
    hg_ref[...] = full[...].reshape(hg_ref.shape)

    @pl.loop(1, F)
    def _(r):
        att_copy(r).wait_send()

    @pl.loop(1, ranks)
    def _(r):
        i, there = rank(r)

        @pl.when(i < reducers)
        def _():
            remote(zbuf.at[0], rbuf.at[0], zs_send.at[r], zs_recv.at[0], f, there).wait_send()

        @pl.when(me < reducers)
        def _():
            remote(tile, full.at[0, 0], zg_send.at[r], zg_recv.at[0], f, there).wait_send()

    for copy in (edge, core_copy, flip_copy, to_core):
        copy.wait_send()

    @pl.when(jnp.logical_not(own_last))
    def _():
        last_copy.wait_send()


def kernel(F, C, lat_hbm, stream_hbm, q_hbm, k_hbm, v_hbm, w_hbm, wh_hbm, flip_ref, hg_ref, *scratch):
    p = Place(F, C)
    bufs = dict(zip(NAMES, scratch))
    g = bufs.__getitem__
    weights = Weights(p, *map(g, WEIGHTS))
    h, at, per = weights.own(p.f)
    early_loads = [pltpu.make_async_copy(wh_hbm, g("whv").at[h, pl.ds(at, per)], g("in_sem").at[4])]
    late = [
        pltpu.make_async_copy(stream_hbm, g("stream"), g("in_sem").at[5]),
        pltpu.make_async_copy(lat_hbm, g("lat"), g("in_sem").at[6]),
    ]
    for copy in early_loads:
        copy.start()
    entry(p, q_hbm, k_hbm, v_hbm, w_hbm, g("kbuf"), g("vbuf"), g("wbuf"), g("qbuf"), g("in_sem"))
    for copy in late:
        copy.start()
    for copy in early_loads + late:
        copy.wait()
    early, drain = attend_phase(p, weights, *map(g, ATTEND))
    head_phase(
        p, early, g("att"), g("wt"), g("stream"), g("sp"), g("mall"), g("lat"), flip_ref, hg_ref, *map(g, HEAD)
    )
    drain()
    weights.drain()


WEIGHTS = (
    "wbuf", "whv", "stream", "sp", "mp", "m_in", "m_half", "m_in2", "mall",
    "wh_send", "wh_recv", "whs_sem", "ms_sem", "mm_sem", "mg_send", "mg_recv", "mx_sem",
)
ATTEND = (
    "qbuf", "kbuf", "vbuf", "wbuf", "q2", "m_s", "l_s", "acc_s", "o_in", "st_out", "st_in", "tbuf", "att", "wt",
    "ring_send", "ring_recv", "sib_send", "sib_recv", "w_send", "w_recv", "w2_send", "w2_recv", "ws_sem", "q_sem",
    "o_send", "o_recv",
)
HEAD = (
    "attbuf", "edge_out", "edge_in", "flip_out", "flip_in", "last_out", "last_in", "part", "cbuf", "zbuf", "rbuf", "tile",
    "full", "att_send", "att_recv", "edge_sem", "flip_sem", "last_sem", "core_sem", "zs_send", "zs_recv", "zg_send",
    "zg_recv", "core2_sem",
)


def shapes(F, C, tok, width, cols, wide, chan, share):
    Z = C // 4
    per, n = Z // (F // 2), Z // 2 + 1
    tiles = share // 2 // 8
    each = -(-tiles // (2 * Z))
    reducers = tiles // each
    block = (each * 8, 2 * chan)
    dma = pltpu.SemaphoreType.DMA

    def v(*shape, dtype=F32):
        return pltpu.VMEM(shape, dtype)

    return dict(
        qbuf=v(tok, width, dtype=BF16), kbuf=v(Z, 2, tok, width, dtype=BF16), vbuf=v(Z, 2, tok, width, dtype=BF16),
        wbuf=v(Z, cols, wide, dtype=BF16), q2=v(tok, width, dtype=BF16), m_s=v(2, 2, tok, 128), l_s=v(2, 2, tok, 128),
        acc_s=v(2, 2, tok, HD), o_in=v(2, tok, HD), st_out=v(8, tok), st_in=v(8, tok), tbuf=v(128, tok),
        att=v(tok, width, dtype=BF16), wt=v(per, 2, cols, F * wide, dtype=BF16),
        ring_send=dma((4, n)), ring_recv=dma((4, n)), sib_send=dma((4, n)), sib_recv=dma((4, n)),
        w_send=dma((2, n)), w_recv=dma((2, n)), w2_send=dma((Z, 2)), w2_recv=dma((F,)), ws_sem=dma((2,)),
        q_sem=dma((2,)), o_send=dma((2,)), o_recv=dma((2,)), in_sem=dma((7,)),
        stream=v(tok, share * F, dtype=BF16), lat=v(chan, tok), whv=v(2, Z, 2, cols, 2 * chan, dtype=BF16),
        sp=v(2 * chan, tok), mp=v(2, chan, wide), m_in=v(chan, wide), m_half=v(chan, wide), m_in2=v(chan, wide),
        mall=v(2, chan, F * wide), wh_send=dma((F,)), wh_recv=dma((F,)), whs_sem=dma((2, F)), ms_sem=dma((2,)),
        mm_sem=dma((2,)), mg_send=dma((F,)), mg_recv=dma((F,)), mx_sem=dma((2,)),
        attbuf=v(tok, F * wide, dtype=BF16), edge_out=v(8, 128), edge_in=v(8, 128),
        flip_out=v(chan, tok), flip_in=v(chan, tok), last_out=v(8, 2 * chan), last_in=v(8, 2 * chan),
        part=v(2, reducers, *block), cbuf=v(reducers, *block), zbuf=v(reducers, *block), rbuf=v(2 * Z, *block),
        tile=v(*block), full=v(2, reducers, *block),
        att_send=dma((F,)), att_recv=dma((F,)), edge_sem=dma((2,)), flip_sem=dma((2,)), last_sem=dma((2,)),
        core_sem=dma((2,)), zs_send=dma((2 * Z,)), zs_recv=dma((2 * Z,)), zg_send=dma((2 * Z,)), zg_recv=dma((2 * Z,)),
        core2_sem=dma((2,)),
    )


NAMES = tuple(shapes(8, 64, 128, 256, 48, 256, 64, 384))


def shards(F, C, latents, stream, queries, key_rows, value_rows, w_mix, w_head):
    tok, chan = latents.shape
    share, chan2 = w_head.shape
    width = queries.shape[1]
    w_t = w_mix.T
    vmem = pl.BlockSpec(memory_space=pltpu.VMEM)
    flipped, grad = pl.pallas_call(
        functools.partial(kernel, F, C),
        out_shape=(
            jax.ShapeDtypeStruct((chan, tok), F32),
            jax.ShapeDtypeStruct((share, chan2), F32),
        ),
        in_specs=[pl.BlockSpec(memory_space=pl.ANY)] * 7,
        out_specs=(vmem, vmem),
        scratch_shapes=list(shapes(F, C, tok, width, *w_t.shape, chan, share).values()),
        compiler_params=pltpu.CompilerParams(
            collective_id=0, has_side_effects=True, vmem_limit_bytes=60 * 1024 * 1024
        ),
        name="coupling",
    )(latents.T, stream, queries, key_rows, value_rows, w_t, w_head.reshape(-1, 2, w_t.shape[0], chan2))
    return flipped.T, grad


def solution(mesh):
    return jax.shard_map(
        functools.partial(shards, mesh.shape["fsdp"], mesh.shape["ctx"]),
        mesh=mesh,
        in_specs=(
            P("ctx", None),
            P("ctx", None),
            P("ctx", "fsdp"),
            P("ctx", "fsdp"),
            P("ctx", "fsdp"),
            P("fsdp", "ctx"),
            P("fsdp", None),
        ),
        out_specs=(P("ctx", None), P("fsdp", None)),
        check_vma=False,
    )
```

```python
import functools
import math

import jax
import jax.numpy as jnp
from jax import lax
from jax.experimental import pallas as pl
from jax.experimental.pallas import tpu as pltpu
from jax.sharding import PartitionSpec as P

HD = 128
MESH = pl.DeviceIdType.MESH
F32, BF16 = jnp.float32, jnp.bfloat16
NT_DIMS = (((1,), (1,)), ((), ()))
SCALE = HD**-0.5 * math.log2(math.e)


def remote(src, dst, send, recv, f, c):
    return pltpu.make_async_remote_copy(
        src_ref=src, dst_ref=dst, send_sem=send, recv_sem=recv, device_id=(f, c), device_id_type=MESH
    )


def greet(barrier, f, c):
    pl.semaphore_signal(barrier, inc=1, device_id=(f, c), device_id_type=MESH)


class Place:
    def __init__(self, F, C):
        self.F, self.C, self.Z = F, C, C // 4
        self.f, self.c = lax.axis_index("fsdp"), lax.axis_index("ctx")
        self.row = self.f // (F // 2)
        self.half = self.c // (C // 2)
        self.z = lax.rem(self.c, C // 2) // 2
        self.k = lax.rem(self.c, 2)
        self.sib = self.c + 1 - 2 * self.k
        self.mate = lax.rem(self.c + C // 2, C)
        self.prev, self.next = lax.rem(self.c + C - 1, C), lax.rem(self.c + 1, C)

    def at(self, half, z, k):
        return half * (self.C // 2) + z * 2 + k

    def plane(self, r):
        i = lax.rem(self.half * self.F + self.f + r, 2 * self.F)
        return lax.rem(i, self.F), self.at(i // self.F, self.z, self.k)

    def zrel(self, by):
        return lax.rem(self.z + by + self.Z, self.Z)


def dot_nt(a, b):
    return lax.dot_general(a, b, NT_DIMS, preferred_element_type=F32)


def split3(x):
    a = x.astype(BF16)
    rest = x - a.astype(F32)
    b = rest.astype(BF16)
    return a, b, (rest - b.astype(F32)).astype(BF16)


def entry(p, q_ref, k_ref, v_ref, w_ref, kbuf, vbuf, wbuf, qbuf, in_sem):
    z, k = p.z, p.k
    loads = [
        pltpu.make_async_copy(k_ref, kbuf.at[z, k], in_sem.at[0]),
        pltpu.make_async_copy(v_ref, vbuf.at[z, k], in_sem.at[1]),
        pltpu.make_async_copy(w_ref, wbuf.at[z], in_sem.at[2]),
        pltpu.make_async_copy(q_ref, qbuf, in_sem.at[3]),
    ]
    for load in loads:
        load.start()
    barrier = pltpu.get_barrier_semaphore()
    for c in (p.at(p.half, p.zrel(1), k), p.at(p.half, p.zrel(-1), k), p.sib, p.prev, p.next):
        greet(barrier, p.f, c)
    for r in (2, -2):
        greet(barrier, p.f, p.at(p.half, p.zrel(r), k))

    @pl.loop(1, 2 * p.F)
    def _(r):
        greet(barrier, *p.plane(r))

    for load in loads:
        load.wait()
    pl.semaphore_wait(barrier, 7 + 2 * p.F - 1)


class Weights:
    def __init__(
        self, p, wbuf, whv, stream, sp, mp, m_in, m_half, m_in2, mall,
        wh_send, wh_recv, whs_sem, ms_sem, mm_sem, mg_send, mg_recv, mx_sem,
    ):
        self.p, self.wbuf, self.whv, self.stream, self.sp = p, wbuf, whv, stream, sp
        self.mp, self.m_in, self.m_half, self.m_in2, self.mall = mp, m_in, m_half, m_in2, mall
        self.wh_sems, self.mg_sems = (wh_send, wh_recv), (mg_send, mg_recv)
        f, k = p.f, p.k
        self.whs_sem, self.mx_sem = whs_sem, mx_sem
        self.to_sib = remote(mp.at[1 - k], m_in, ms_sem.at[0], ms_sem.at[1], f, p.sib)
        self.to_mate = remote(m_half, m_in2, mm_sem.at[0], mm_sem.at[1], f, p.mate)

    def own(self, fs):
        groups = self.p.F // 2
        per = self.p.Z // groups
        return fs // groups, lax.rem(fs, groups) * per, per

    def rows(self, fs, core):
        h, at, per = self.own(fs)
        return self.whv.at[h, pl.ds(at + core * (per // 2), per // 2)]

    def head_copy(self, r, fs):
        p = self.p
        send, recv = self.wh_sems
        return remote(self.rows(fs, p.k), self.rows(fs, p.k), send.at[r], recv.at[fs], lax.rem(p.f + r, p.F), p.c)

    def beside(self, core, fs):
        return remote(
            self.rows(fs, core), self.rows(fs, core), self.whs_sem.at[0, fs], self.whs_sem.at[1, fs], self.p.f, self.p.sib
        )

    def start(self):
        @pl.loop(1, self.p.F)
        def _(r):
            self.head_copy(r, self.p.f).start()

    def share(self):
        p = self.p

        @pl.loop(1, p.F)
        def _(r):
            fs = lax.rem(p.f + r, p.F)
            self.head_copy(r, fs).wait_recv()
            self.beside(p.k, fs).start()

    def partial(self):
        p = self.p

        @pl.loop(1, p.F)
        def _(r):
            self.beside(1 - p.k, lax.rem(p.f + r, p.F)).wait_recv()

        width = self.wbuf.shape[2]
        rows = self.whv[p.half, :, p.k].reshape(-1, 128)
        pieces = self.wbuf[...].reshape(-1, width)
        out = jnp.dot(rows.astype(F32).T.astype(BF16), pieces, preferred_element_type=F32)
        self.mp[...] = out.reshape(self.mp.shape)
        self.to_sib.start()

    def halves(self):
        self.to_sib.wait_recv()
        self.m_half[...] = self.mp[self.p.k] + self.m_in[...]
        self.to_mate.start()

    def lanes(self, fs):
        width = self.mp.shape[2]
        return pl.ds(pl.multiple_of(fs * width, width), width)

    def all_copy(self, r, fs):
        p = self.p
        send, recv = self.mg_sems
        dst = self.mall.at[p.k, :, self.lanes(fs)]
        return remote(dst, dst, send.at[r], recv.at[fs], lax.rem(p.f + r, p.F), p.c)

    def gather(self):
        p = self.p
        self.to_mate.wait_recv()
        self.mall[p.k, :, self.lanes(p.f)] = self.m_half[...] + self.m_in2[...]

        @pl.loop(1, p.F)
        def _(r):
            self.all_copy(r, p.f).start()

    def across(self, core):
        return remote(self.mall.at[core], self.mall.at[core], self.mx_sem.at[0], self.mx_sem.at[1], self.p.f, self.p.sib)

    def finish(self):
        p = self.p
        self.sp[...] = jnp.dot(self.stream[...], self.whv[...].reshape(-1, 128), preferred_element_type=F32).T

        @pl.loop(1, p.F)
        def _(r):
            self.all_copy(r, lax.rem(p.f + r, p.F)).wait_recv()

        self.across(p.k).start()
        self.across(1 - p.k).wait_recv()

    def drain(self):
        p = self.p

        @pl.loop(1, p.F)
        def _(r):
            self.head_copy(r, p.f).wait_send()
            self.beside(p.k, lax.rem(p.f + r, p.F)).wait_send()
            self.all_copy(r, p.f).wait_send()

        self.to_sib.wait_send()
        self.to_mate.wait_send()
        self.across(p.k).wait_send()


def attend_phase(
    p, weights, q_ref, kbuf, vbuf, wbuf, q2, m_s, l_s, acc_s, o_in, st_out, st_in, tbuf, att_ref, wt_ref,
    ring_send, ring_recv, sib_send, sib_recv, w_send, w_recv, w2_send, w2_recv, ws_sem, q_sem, o_send, o_recv,
):
    F = p.F
    f, z, k, half, Z = p.f, p.z, p.k, p.half, p.Z
    steps, groups = Z // 2, F // 2
    per = Z // groups
    tok = q_ref.shape[0]
    wide = wbuf.shape[2]
    above, below = p.at(half, p.zrel(1), k), p.at(half, p.zrel(-1), k)
    mine = p.row == half

    m_s[...] = jnp.full_like(m_s, -1e30)
    l_s[...] = jnp.zeros_like(l_s)
    acc_s[...] = jnp.zeros_like(acc_s)

    def buf(kind):
        return kbuf if kind % 2 == 0 else vbuf

    def origin(kind, s):
        return p.zrel(-s) if kind < 2 else p.zrel(s)

    def ring(kind, s, o):
        return remote(
            buf(kind).at[o, k], buf(kind).at[o, k], ring_send.at[kind, s], ring_recv.at[kind, s],
            f, above if kind < 2 else below,
        )

    def beside(kind, s, core):
        o = origin(kind, s)
        return remote(
            buf(kind).at[o, core], buf(kind).at[o, core], sib_send.at[kind, s], sib_recv.at[kind, s], f, p.sib
        )

    def wring(up, dist, o):
        by = 2 - dist % 2 if isinstance(dist, int) else 2 - lax.rem(dist, 2)
        to = p.zrel(by) if up == 0 else p.zrel(-by)
        return remote(
            wbuf.at[o], wbuf.at[o], w_send.at[up, dist], w_recv.at[up, dist], f, p.at(half, to, k)
        )

    for kind in (0, 2, 1, 3):
        ring(kind, 1, z).start()
    for up in (0, 1):
        wring(up, 1, z).start()
        wring(up, 2, z).start()
    for kind in (0, 1):
        beside(kind, 0, k).start()
    to_mate = remote(q_ref, q2, q_sem.at[0], q_sem.at[1], f, p.mate)

    @pl.when(half == 1)
    def _():
        to_mate.start()

    weights.start()

    def fold(who, blocks, masked=False):
        q = q_ref if who == 0 else q2
        heads = [slice(h * HD, (h + 1) * HD) for h in range(2)]

        def rows(ref, o, h):
            return ref[o, :, :, heads[h]].reshape(2 * tok, HD)

        scores = [[dot_nt(q[:, heads[h]], rows(kbuf, o, h)) for o in blocks] for h in range(2)]
        if masked:
            at = lax.broadcasted_iota(jnp.int32, (tok, 2 * tok), 1)
            seen = at <= k * tok + lax.broadcasted_iota(jnp.int32, (tok, 2 * tok), 0)
            scores = [[jnp.where(seen, x, -1e30) for x in per_head] for per_head in scores]
        parts, m_old, m_new = [], [], []
        for h in range(2):
            parts.append([x[:, i * tok : (i + 1) * tok] for x in scores[h] for i in range(2)])
            top = jnp.max(functools.reduce(jnp.maximum, parts[h]), axis=1, keepdims=True)
            m_old.append(m_s[who, h])
            m_new.append(jnp.maximum(m_old[h], top))
        for h in range(2):
            keep = jnp.exp2((m_old[h] - m_new[h]) * SCALE)
            e = [jnp.exp2((x - m_new[h]) * SCALE) for x in parts[h]]
            m_s[who, h] = m_new[h]
            l_s[who, h] = l_s[who, h] * keep + functools.reduce(jnp.add, e)
            acc = acc_s[who, h] * keep
            for i, o in enumerate(blocks):
                both = jnp.concatenate([e[2 * i].astype(BF16), e[2 * i + 1].astype(BF16)], axis=1)
                acc = acc + jnp.dot(both, rows(vbuf, o, h), preferred_element_type=F32)
            acc_s[who, h] = acc

    def arrive(kind, s):
        o = origin(kind, s)
        ring(kind, s, o).wait_recv()
        last = steps if kind < 2 else steps - 1

        @pl.when(s < last)
        def _():
            ring(kind, s + 1, o).start()

        beside(kind, s, k).start()

    def w_origin(up, dist):
        return p.zrel(-dist) if up == 0 else p.zrel(dist)

    def w_arrive(s):
        for up in (0, 1):
            last = steps if up == 0 else steps - 1
            o = w_origin(up, 2 * s - 1)
            wring(up, 2 * s - 1, o).wait_recv()
            to_plane(o)

            @pl.when(2 * s <= last)
            def _():
                o = w_origin(up, 2 * s)
                wring(up, 2 * s, o).wait_recv()

                @pl.when(2 * s + 1 <= last)
                def _():
                    wring(up, 2 * s + 1, o).start()

                @pl.when(2 * s + 2 <= last)
                def _():
                    wring(up, 2 * s + 2, o).start()

                to_plane(o)

    def plane_copy(o, h):
        return remote(
            wbuf.at[o], wt_ref.at[lax.rem(o, per), k, :, pl.ds(pl.multiple_of(f * wide, wide), wide)],
            w2_send.at[o, h], w2_recv.at[f], half * groups + o // per, p.at(h, z, k),
        )

    def is_self(o, h):
        return jnp.logical_and(half * groups + o // per == f, half == h)

    def to_plane(o):
        for h in range(2):

            @pl.when(jnp.logical_not(is_self(o, h)))
            def _():
                plane_copy(o, h).start()

            @pl.when(is_self(o, h))
            def _():
                wt_ref[lax.rem(o, per), k, :, pl.ds(pl.multiple_of(f * wide, wide), wide)] = wbuf[o]

    def first_fold():
        beside(0, 0, 1 - k).wait_recv()
        beside(1, 0, 1 - k).wait_recv()

        @pl.when(half == 0)
        def _():
            to_mate.wait_recv()
            fold(1, (z,))

        fold(0, (z,), masked=True)

    def fold_step(s):
        low, high = origin(0, s), origin(2, s)
        for kind in range(4):
            beside(kind, s, 1 - k).wait_recv()
        from_low, from_high = z >= s, z + s >= Z

        @pl.when(half == 0)
        def _():
            fold(1, (low, high))

        @pl.when(jnp.logical_and(from_low, from_high))
        def _():
            fold(0, (low, high))

        @pl.when(jnp.logical_and(from_low, jnp.logical_not(from_high)))
        def _():
            fold(0, (low,))

        @pl.when(jnp.logical_and(from_high, jnp.logical_not(from_low)))
        def _():
            fold(0, (high,))

    to_plane(z)

    def from_plane(fs):
        return remote(
            wbuf.at[pl.ds(0, per)], wt_ref.at[:, k, :, pl.ds(fs * wide, wide)],
            w2_send.at[0, 0], w2_recv.at[fs], fs, p.at(p.row, z, k),
        )

    across = remote(wt_ref.at[:, k], wt_ref.at[:, k], ws_sem.at[0], ws_sem.at[1], f, p.sib)

    def collect():
        for fs in range(F):

            @pl.when(jnp.logical_not(jnp.logical_and(mine, fs == f)))
            def _():
                from_plane(fs).wait_recv()

        across.start()

    @pl.loop(1, steps + 1)
    def _(s):
        arrive(0, s)

        @pl.when(s < steps)
        def _():
            arrive(2, s)

        arrive(1, s)

        @pl.when(s < steps)
        def _():
            arrive(3, s)

        @pl.when(jnp.logical_and(s > 1, s <= steps // 2 + 1))
        def _():
            w_arrive(s - 1)

        @pl.when(s == 3)
        def _():
            weights.share()

        @pl.when(s == steps // 2 + 1)
        def _():
            weights.partial()

        @pl.when(s == steps // 2 + 2)
        def _():
            weights.halves()

        @pl.when(s == steps)
        def _():
            weights.gather()

        @pl.when(s == 1)
        def _():
            first_fold()

        @pl.when(s > 1)
        def _():
            fold_step(s - 1)

    far = origin(0, steps)
    beside(0, steps, 1 - k).wait_recv()
    beside(1, steps, 1 - k).wait_recv()
    lane = lax.broadcasted_iota(jnp.int32, (tok, 128), 1)
    back = [
        remote(acc_s.at[1], o_in, o_send.at[0], o_recv.at[0], f, p.mate),
        remote(st_out, st_in, o_send.at[1], o_recv.at[1], f, p.mate),
    ]

    @pl.when(half == 0)
    def _():
        fold(1, (far,))
        back[0].start()
        stats = jnp.zeros((tok, 128), F32)
        for h in range(2):
            stats = jnp.where(lane == h, m_s[1, h], stats)
            stats = jnp.where(lane == 2 + h, jnp.sum(l_s[1, h], axis=1, keepdims=True), stats)
        st_out[...] = stats.T[:8]
        back[1].start()

    @pl.when(z >= steps)
    def _():
        fold(0, (far,))

    collect()

    def store(h, acc, total):
        att_ref[:, h * HD : (h + 1) * HD] = (acc / total).astype(BF16)

    @pl.when(half == 0)
    def _():
        for h in range(2):
            store(h, acc_s[0, h], jnp.sum(l_s[0, h], axis=1, keepdims=True))

    @pl.when(half == 1)
    def _():
        back[0].wait_recv()
        back[1].wait_recv()
        tbuf[...] = jnp.zeros_like(tbuf)
        tbuf[:8] = st_in[...]
        stats = tbuf[...].T
        for h in range(2):
            m_a, l_a = m_s[0, h], jnp.sum(l_s[0, h], axis=1, keepdims=True)
            m_b = jnp.max(jnp.where(lane == h, stats, -3e38), axis=1, keepdims=True)
            l_b = jnp.sum(jnp.where(lane == 2 + h, stats, 0.0), axis=1, keepdims=True)
            m = jnp.maximum(m_a, m_b)
            e_a, e_b = jnp.exp2((m_a - m) * SCALE), jnp.exp2((m_b - m) * SCALE)
            store(h, acc_s[0, h] * e_a + o_in[h] * e_b, l_a * e_a + l_b * e_b)

    def early():
        weights.finish()
        remote(wt_ref.at[:, 1 - k], wt_ref.at[:, 1 - k], ws_sem.at[0], ws_sem.at[1], f, p.sib).wait_recv()

    def drain():
        attend_drain(p, ring, beside, wring, plane_copy, is_self, across, back, to_mate)

    return early, drain


def attend_drain(p, ring, beside, wring, plane_copy, is_self, across, back, to_mate):
    z, k, half, steps = p.z, p.k, p.half, p.Z // 2

    @pl.loop(1, steps + 1)
    def _(s):
        for kind in (0, 1):
            ring(kind, s, z).wait_send()
            beside(kind, s, k).wait_send()
        wring(0, s, z).wait_send()

        @pl.when(s < steps)
        def _():
            for kind in (2, 3):
                ring(kind, s, z).wait_send()
                beside(kind, s, k).wait_send()
            wring(1, s, z).wait_send()

    for kind in (0, 1):
        beside(kind, 0, k).wait_send()

    @pl.loop(0, p.Z)
    def _(o):
        for h in range(2):

            @pl.when(jnp.logical_not(is_self(o, h)))
            def _():
                plane_copy(o, h).wait_send()

    across.wait_send()

    @pl.when(half == 0)
    def _():
        back[0].wait_send()
        back[1].wait_send()

    @pl.when(half == 1)
    def _():
        to_mate.wait_send()


def head_phase(
    p, early, att_ref, wt_ref, stream, sp, mall, lat_ref, flip_ref, hg_ref,
    attbuf, edge_out, edge_in, flip_out, flip_in, last_out, last_in, part, cbuf, zbuf, rbuf, tile, full,
    att_send, att_recv, edge_sem, flip_sem, last_sem, core_sem, zs_send, zs_recv, zg_send, zg_recv, core2_sem,
):
    F, C = p.F, p.C
    f, c, z, k, half, Z = p.f, p.c, p.z, p.k, p.half, p.Z
    tok, wide = att_ref.shape
    chan = lat_ref.shape[0]
    reducers = zbuf.shape[0]
    mirror, mirror2 = C - 1 - c, lax.rem(2 * C - 2 - c, C)
    own_last = mirror2 == c
    lane = lax.broadcasted_iota(jnp.int32, (chan, tok), 1)

    def as_column(row):
        return jnp.broadcast_to(row, (tok, 128)).T

    mine = pl.ds(pl.multiple_of(f * wide, wide), wide)
    attbuf[:, mine] = att_ref[...]

    def att_copy(r):
        return remote(
            att_ref, attbuf.at[:, mine], att_send.at[r], att_recv.at[f], lax.rem(f + r, F), c
        )

    @pl.loop(1, F)
    def _(r):
        att_copy(r).start()

    lat_t = lat_ref[...]
    edge_out[...] = jnp.concatenate([lat_t, lat_t], axis=0).T[:8]
    edge = remote(edge_out, edge_in, edge_sem.at[0], edge_sem.at[1], f, p.prev)
    edge.start()
    share = hg_ref.shape[0]
    stream_t = stream[:, pl.ds(pl.multiple_of(f * share, 128), share)].astype(F32).T
    early()
    m_all = split3(mall[...].reshape(2 * chan, F * wide))
    edge.wait_recv()
    lat_next = jnp.where(lane == tok - 1, as_column(edge_in[0:1])[:chan], pltpu.roll(lat_t, tok - 1, 1))

    @pl.loop(1, F)
    def _(r):
        fs = lax.rem(f + r, F)
        there = pl.ds(pl.multiple_of(fs * wide, wide), wide)
        remote(att_ref, attbuf.at[:, there], att_send.at[r], att_recv.at[fs], fs, c).wait_recv()

    heads = attbuf[...]
    pred = sp[...] + (dot_nt(m_all[2], heads) + dot_nt(m_all[1], heads) + dot_nt(m_all[0], heads))
    resid = stream_t + dot_nt(wt_ref[...].reshape(share, F * wide), heads)
    r_hi, r_mid, r_lo = split3(resid)
    final = jnp.logical_and(c == C - 1, lane == tok - 1)
    shift = jnp.where(final, 0.0, pred[:chan])
    log_scale = jnp.where(final, 0.0, pred[chan:])
    inverse = jnp.exp(-log_scale)
    white = (lat_next - shift) * inverse
    loss_scale = float(tok * C) ** -0.5
    d_shift = jnp.where(final, 0.0, -white * inverse * loss_scale)
    d_log = jnp.where(final, 0.0, (1.0 - white * white) * loss_scale)
    d_hi, d_mid, d_lo = split3(jnp.concatenate([d_shift, d_log], axis=0))
    grad = dot_nt(r_hi, d_lo) + dot_nt(r_lo, d_hi) + dot_nt(r_mid, d_mid)
    grad += dot_nt(r_hi, d_mid) + dot_nt(r_mid, d_hi)
    grad += dot_nt(r_hi, d_hi)
    part[...] = grad.reshape(part.shape)

    core_copy = remote(part.at[1 - k], cbuf, core_sem.at[0], core_sem.at[1], f, p.sib)
    core_copy.start()

    t_i = lax.broadcasted_iota(jnp.int32, (tok, tok), 0)
    r_i = lax.broadcasted_iota(jnp.int32, (tok, tok), 1)
    swap = jnp.where(t_i == tok - 2 - r_i, 1.0, 0.0).astype(BF16)
    w_hi, w_mid, w_lo = split3(white)
    turned = jnp.dot(w_hi, swap, preferred_element_type=F32) + jnp.dot(w_mid, swap, preferred_element_type=F32)
    flip_out[...] = turned + jnp.dot(w_lo, swap, preferred_element_type=F32)
    last_out[...] = jnp.concatenate([white, white], axis=0).T[tok - 8 :]
    flip_copy = remote(flip_out, flip_in, flip_sem.at[0], flip_sem.at[1], f, mirror)
    last_copy = remote(last_out, last_in, last_sem.at[0], last_sem.at[1], f, mirror2)

    core_copy.wait_recv()
    zbuf[...] = part[k] + cbuf[...]
    ranks = 2 * Z
    me = half * Z + z

    def rank(r):
        i = lax.rem(me + r, ranks)
        return i, p.at(i // Z, lax.rem(i, Z), k)

    @pl.loop(1, ranks)
    def _(r):
        to, there = rank(r)

        @pl.when(to < reducers)
        def _():
            remote(zbuf.at[to], rbuf.at[me], zs_send.at[r], zs_recv.at[me], f, there).start()

    @pl.when(me < reducers)
    def _():
        rbuf[me] = zbuf[me]

        @pl.loop(1, ranks)
        def _(r):
            i, there = rank(r)
            remote(zbuf.at[0], rbuf.at[i], zs_send.at[r], zs_recv.at[i], f, there).wait_recv()

        tile[...] = jnp.sum(rbuf[...], axis=0)

        @pl.loop(1, ranks)
        def _(r):
            remote(tile, full.at[k, me], zg_send.at[r], zg_recv.at[me], f, rank(r)[1]).start()

        full[k, me] = tile[...]

    flip_copy.start()

    @pl.when(own_last)
    def _():
        last_in[...] = last_out[...]

    @pl.when(jnp.logical_not(own_last))
    def _():
        last_copy.start()

    flip_copy.wait_recv()

    @pl.when(jnp.logical_not(own_last))
    def _():
        last_copy.wait_recv()

    flip_ref[...] = jnp.where(lane == tok - 1, as_column(last_in[7:8])[:chan], flip_in[...])

    @pl.loop(1, ranks)
    def _(r):
        i, there = rank(r)

        @pl.when(i < reducers)
        def _():
            remote(tile, full.at[k, i], zg_send.at[r], zg_recv.at[i], f, there).wait_recv()

    to_core = remote(full.at[k], full.at[k], core2_sem.at[0], core2_sem.at[1], f, p.sib)
    to_core.start()
    remote(full.at[1 - k], full.at[1 - k], core2_sem.at[0], core2_sem.at[1], f, p.sib).wait_recv()
    hg_ref[...] = full[...].reshape(hg_ref.shape)

    @pl.loop(1, F)
    def _(r):
        att_copy(r).wait_send()

    @pl.loop(1, ranks)
    def _(r):
        i, there = rank(r)

        @pl.when(i < reducers)
        def _():
            remote(zbuf.at[0], rbuf.at[0], zs_send.at[r], zs_recv.at[0], f, there).wait_send()

        @pl.when(me < reducers)
        def _():
            remote(tile, full.at[0, 0], zg_send.at[r], zg_recv.at[0], f, there).wait_send()

    for copy in (edge, core_copy, flip_copy, to_core):
        copy.wait_send()

    @pl.when(jnp.logical_not(own_last))
    def _():
        last_copy.wait_send()


def kernel(F, C, lat_hbm, stream_hbm, q_hbm, k_hbm, v_hbm, w_hbm, wh_hbm, flip_ref, hg_ref, *scratch):
    p = Place(F, C)
    bufs = dict(zip(NAMES, scratch))
    g = bufs.__getitem__
    weights = Weights(p, *map(g, WEIGHTS))
    h, at, per = weights.own(p.f)
    early_loads = [pltpu.make_async_copy(wh_hbm, g("whv").at[h, pl.ds(at, per)], g("in_sem").at[4])]
    late = [
        pltpu.make_async_copy(stream_hbm, g("stream"), g("in_sem").at[5]),
        pltpu.make_async_copy(lat_hbm, g("lat"), g("in_sem").at[6]),
    ]
    for copy in early_loads:
        copy.start()
    entry(p, q_hbm, k_hbm, v_hbm, w_hbm, g("kbuf"), g("vbuf"), g("wbuf"), g("qbuf"), g("in_sem"))
    for copy in late:
        copy.start()
    for copy in early_loads + late:
        copy.wait()
    early, drain = attend_phase(p, weights, *map(g, ATTEND))
    head_phase(
        p, early, g("att"), g("wt"), g("stream"), g("sp"), g("mall"), g("lat"), flip_ref, hg_ref, *map(g, HEAD)
    )
    drain()
    weights.drain()


WEIGHTS = (
    "wbuf", "whv", "stream", "sp", "mp", "m_in", "m_half", "m_in2", "mall",
    "wh_send", "wh_recv", "whs_sem", "ms_sem", "mm_sem", "mg_send", "mg_recv", "mx_sem",
)
ATTEND = (
    "qbuf", "kbuf", "vbuf", "wbuf", "q2", "m_s", "l_s", "acc_s", "o_in", "st_out", "st_in", "tbuf", "att", "wt",
    "ring_send", "ring_recv", "sib_send", "sib_recv", "w_send", "w_recv", "w2_send", "w2_recv", "ws_sem", "q_sem",
    "o_send", "o_recv",
)
HEAD = (
    "attbuf", "edge_out", "edge_in", "flip_out", "flip_in", "last_out", "last_in", "part", "cbuf", "zbuf", "rbuf", "tile",
    "full", "att_send", "att_recv", "edge_sem", "flip_sem", "last_sem", "core_sem", "zs_send", "zs_recv", "zg_send",
    "zg_recv", "core2_sem",
)


def shapes(F, C, tok, width, cols, wide, chan, share):
    Z = C // 4
    per, n = Z // (F // 2), Z // 2 + 1
    tiles = share // 2 // 8
    each = -(-tiles // (2 * Z))
    reducers = tiles // each
    block = (each * 8, 2 * chan)
    dma = pltpu.SemaphoreType.DMA

    def v(*shape, dtype=F32):
        return pltpu.VMEM(shape, dtype)

    return dict(
        qbuf=v(tok, width, dtype=BF16), kbuf=v(Z, 2, tok, width, dtype=BF16), vbuf=v(Z, 2, tok, width, dtype=BF16),
        wbuf=v(Z, cols, wide, dtype=BF16), q2=v(tok, width, dtype=BF16), m_s=v(2, 2, tok, 128), l_s=v(2, 2, tok, 128),
        acc_s=v(2, 2, tok, HD), o_in=v(2, tok, HD), st_out=v(8, tok), st_in=v(8, tok), tbuf=v(128, tok),
        att=v(tok, width, dtype=BF16), wt=v(per, 2, cols, F * wide, dtype=BF16),
        ring_send=dma((4, n)), ring_recv=dma((4, n)), sib_send=dma((4, n)), sib_recv=dma((4, n)),
        w_send=dma((2, n)), w_recv=dma((2, n)), w2_send=dma((Z, 2)), w2_recv=dma((F,)), ws_sem=dma((2,)),
        q_sem=dma((2,)), o_send=dma((2,)), o_recv=dma((2,)), in_sem=dma((7,)),
        stream=v(tok, share * F, dtype=BF16), lat=v(chan, tok), whv=v(2, Z, 2, cols, 2 * chan, dtype=BF16),
        sp=v(2 * chan, tok), mp=v(2, chan, wide), m_in=v(chan, wide), m_half=v(chan, wide), m_in2=v(chan, wide),
        mall=v(2, chan, F * wide), wh_send=dma((F,)), wh_recv=dma((F,)), whs_sem=dma((2, F)), ms_sem=dma((2,)),
        mm_sem=dma((2,)), mg_send=dma((F,)), mg_recv=dma((F,)), mx_sem=dma((2,)),
        attbuf=v(tok, F * wide, dtype=BF16), edge_out=v(8, 128), edge_in=v(8, 128),
        flip_out=v(chan, tok), flip_in=v(chan, tok), last_out=v(8, 2 * chan), last_in=v(8, 2 * chan),
        part=v(2, reducers, *block), cbuf=v(reducers, *block), zbuf=v(reducers, *block), rbuf=v(2 * Z, *block),
        tile=v(*block), full=v(2, reducers, *block),
        att_send=dma((F,)), att_recv=dma((F,)), edge_sem=dma((2,)), flip_sem=dma((2,)), last_sem=dma((2,)),
        core_sem=dma((2,)), zs_send=dma((2 * Z,)), zs_recv=dma((2 * Z,)), zg_send=dma((2 * Z,)), zg_recv=dma((2 * Z,)),
        core2_sem=dma((2,)),
    )


NAMES = tuple(shapes(8, 64, 128, 256, 48, 256, 64, 384))


def shards(F, C, latents, stream, queries, key_rows, value_rows, w_mix, w_head):
    tok, chan = latents.shape
    share, chan2 = w_head.shape
    width = queries.shape[1]
    w_t = w_mix.T
    vmem = pl.BlockSpec(memory_space=pltpu.VMEM)
    flipped, grad = pl.pallas_call(
        functools.partial(kernel, F, C),
        out_shape=(
            jax.ShapeDtypeStruct((chan, tok), F32),
            jax.ShapeDtypeStruct((share, chan2), F32),
        ),
        in_specs=[pl.BlockSpec(memory_space=pl.ANY)] * 7,
        out_specs=(vmem, vmem),
        scratch_shapes=list(shapes(F, C, tok, width, *w_t.shape, chan, share).values()),
        compiler_params=pltpu.CompilerParams(
            collective_id=0, has_side_effects=True, vmem_limit_bytes=60 * 1024 * 1024
        ),
        name="coupling",
    )(latents.T, stream, queries, key_rows, value_rows, w_t, w_head.reshape(-1, 2, w_t.shape[0], chan2))
    return flipped.T, grad


def solution(mesh):
    return jax.shard_map(
        functools.partial(shards, mesh.shape["fsdp"], mesh.shape["ctx"]),
        mesh=mesh,
        in_specs=(
            P("ctx", None),
            P("ctx", None),
            P("ctx", "fsdp"),
            P("ctx", "fsdp"),
            P("ctx", "fsdp"),
            P("fsdp", "ctx"),
            P("fsdp", None),
        ),
        out_specs=(P("ctx", None), P("fsdp", None)),
        check_vma=False,
    )
```

```python
import functools
import math

import jax
import jax.numpy as jnp
from jax import lax
from jax.experimental import pallas as pl
from jax.experimental.pallas import tpu as pltpu
from jax.sharding import PartitionSpec as P

HD = 128
MESH = pl.DeviceIdType.MESH
F32, BF16 = jnp.float32, jnp.bfloat16
NT_DIMS = (((1,), (1,)), ((), ()))
SCALE = HD**-0.5 * math.log2(math.e)


def remote(src, dst, send, recv, f, c):
    return pltpu.make_async_remote_copy(
        src_ref=src, dst_ref=dst, send_sem=send, recv_sem=recv, device_id=(f, c), device_id_type=MESH
    )


def greet(barrier, f, c):
    pl.semaphore_signal(barrier, inc=1, device_id=(f, c), device_id_type=MESH)


class Place:
    def __init__(self, F, C):
        self.F, self.C, self.Z = F, C, C // 4
        self.f, self.c = lax.axis_index("fsdp"), lax.axis_index("ctx")
        self.row = self.f // (F // 2)
        self.half = self.c // (C // 2)
        self.z = lax.rem(self.c, C // 2) // 2
        self.k = lax.rem(self.c, 2)
        self.sib = self.c + 1 - 2 * self.k
        self.mate = lax.rem(self.c + C // 2, C)
        self.prev, self.next = lax.rem(self.c + C - 1, C), lax.rem(self.c + 1, C)

    def at(self, half, z, k):
        return half * (self.C // 2) + z * 2 + k

    def plane(self, r):
        i = lax.rem(self.half * self.F + self.f + r, 2 * self.F)
        return lax.rem(i, self.F), self.at(i // self.F, self.z, self.k)

    def zrel(self, by):
        return lax.rem(self.z + by + self.Z, self.Z)


def dot_nt(a, b):
    return lax.dot_general(a, b, NT_DIMS, preferred_element_type=F32)


def split3(x):
    a = x.astype(BF16)
    rest = x - a.astype(F32)
    b = rest.astype(BF16)
    return a, b, (rest - b.astype(F32)).astype(BF16)


def entry(p, q_ref, k_ref, v_ref, w_ref, kbuf, vbuf, wbuf, qbuf, in_sem):
    z, k = p.z, p.k
    loads = [
        pltpu.make_async_copy(k_ref, kbuf.at[z, k], in_sem.at[0]),
        pltpu.make_async_copy(v_ref, vbuf.at[z, k], in_sem.at[1]),
        pltpu.make_async_copy(w_ref, wbuf.at[z], in_sem.at[2]),
        pltpu.make_async_copy(q_ref, qbuf, in_sem.at[3]),
    ]
    for load in loads:
        load.start()
    barrier = pltpu.get_barrier_semaphore()
    for c in (p.at(p.half, p.zrel(1), k), p.at(p.half, p.zrel(-1), k), p.sib, p.prev, p.next):
        greet(barrier, p.f, c)
    for r in (2, -2):
        greet(barrier, p.f, p.at(p.half, p.zrel(r), k))

    @pl.loop(1, 2 * p.F)
    def _(r):
        greet(barrier, *p.plane(r))

    for load in loads:
        load.wait()
    pl.semaphore_wait(barrier, 7 + 2 * p.F - 1)


class Weights:
    def __init__(
        self, p, wbuf, whv, stream, sp, mp, m_in, m_half, m_in2, mall,
        wh_send, wh_recv, whs_sem, ms_sem, mm_sem, mg_send, mg_recv, mx_sem,
    ):
        self.p, self.wbuf, self.whv, self.stream, self.sp = p, wbuf, whv, stream, sp
        self.mp, self.m_in, self.m_half, self.m_in2, self.mall = mp, m_in, m_half, m_in2, mall
        self.wh_sems, self.mg_sems = (wh_send, wh_recv), (mg_send, mg_recv)
        f, k = p.f, p.k
        self.whs_sem, self.mx_sem = whs_sem, mx_sem
        self.to_sib = remote(mp.at[1 - k], m_in, ms_sem.at[0], ms_sem.at[1], f, p.sib)
        self.to_mate = remote(m_half, m_in2, mm_sem.at[0], mm_sem.at[1], f, p.mate)

    def own(self, fs):
        groups = self.p.F // 2
        per = self.p.Z // groups
        return fs // groups, lax.rem(fs, groups) * per, per

    def rows(self, fs, core):
        h, at, per = self.own(fs)
        return self.whv.at[h, pl.ds(at + core * (per // 2), per // 2)]

    def head_copy(self, r, fs):
        p = self.p
        send, recv = self.wh_sems
        return remote(self.rows(fs, p.k), self.rows(fs, p.k), send.at[r], recv.at[fs], lax.rem(p.f + r, p.F), p.c)

    def beside(self, core, fs):
        return remote(
            self.rows(fs, core), self.rows(fs, core), self.whs_sem.at[0, fs], self.whs_sem.at[1, fs], self.p.f, self.p.sib
        )

    def start(self):
        @pl.loop(1, self.p.F)
        def _(r):
            self.head_copy(r, self.p.f).start()

    def share(self):
        p = self.p

        @pl.loop(1, p.F)
        def _(r):
            fs = lax.rem(p.f + r, p.F)
            self.head_copy(r, fs).wait_recv()
            self.beside(p.k, fs).start()

    def partial(self):
        p = self.p

        @pl.loop(1, p.F)
        def _(r):
            self.beside(1 - p.k, lax.rem(p.f + r, p.F)).wait_recv()

        width = self.wbuf.shape[2]
        rows = self.whv[p.half, :, p.k].reshape(-1, 128)
        pieces = self.wbuf[...].reshape(-1, width)
        out = jnp.dot(rows.astype(F32).T.astype(BF16), pieces, preferred_element_type=F32)
        self.mp[...] = out.reshape(self.mp.shape)
        self.to_sib.start()

    def halves(self):
        self.to_sib.wait_recv()
        self.m_half[...] = self.mp[self.p.k] + self.m_in[...]
        self.to_mate.start()

    def lanes(self, fs):
        width = self.mp.shape[2]
        return pl.ds(pl.multiple_of(fs * width, width), width)

    def all_copy(self, r, fs):
        p = self.p
        send, recv = self.mg_sems
        dst = self.mall.at[p.k, :, self.lanes(fs)]
        return remote(dst, dst, send.at[r], recv.at[fs], lax.rem(p.f + r, p.F), p.c)

    def gather(self):
        p = self.p
        self.to_mate.wait_recv()
        self.mall[p.k, :, self.lanes(p.f)] = self.m_half[...] + self.m_in2[...]

        @pl.loop(1, p.F)
        def _(r):
            self.all_copy(r, p.f).start()

    def across(self, core):
        return remote(self.mall.at[core], self.mall.at[core], self.mx_sem.at[0], self.mx_sem.at[1], self.p.f, self.p.sib)

    def finish(self):
        p = self.p
        self.sp[...] = jnp.dot(self.stream[...], self.whv[...].reshape(-1, 128), preferred_element_type=F32).T

        @pl.loop(1, p.F)
        def _(r):
            self.all_copy(r, lax.rem(p.f + r, p.F)).wait_recv()

        self.across(p.k).start()
        self.across(1 - p.k).wait_recv()

    def drain(self):
        p = self.p

        @pl.loop(1, p.F)
        def _(r):
            self.head_copy(r, p.f).wait_send()
            self.beside(p.k, lax.rem(p.f + r, p.F)).wait_send()
            self.all_copy(r, p.f).wait_send()

        self.to_sib.wait_send()
        self.to_mate.wait_send()
        self.across(p.k).wait_send()


def attend_phase(
    p, weights, q_ref, kbuf, vbuf, wbuf, q2, m_s, l_s, acc_s, o_in, st_out, st_in, tbuf, att_ref, wt_ref,
    ring_send, ring_recv, sib_send, sib_recv, w_send, w_recv, w2_send, w2_recv, ws_sem, q_sem, o_send, o_recv,
):
    F = p.F
    f, z, k, half, Z = p.f, p.z, p.k, p.half, p.Z
    steps, groups = Z // 2, F // 2
    per = Z // groups
    tok = q_ref.shape[0]
    wide = wbuf.shape[2]
    above, below = p.at(half, p.zrel(1), k), p.at(half, p.zrel(-1), k)
    mine = p.row == half

    m_s[...] = jnp.full_like(m_s, -1e30)
    l_s[...] = jnp.zeros_like(l_s)
    acc_s[...] = jnp.zeros_like(acc_s)

    def buf(kind):
        return kbuf if kind % 2 == 0 else vbuf

    def origin(kind, s):
        return p.zrel(-s) if kind < 2 else p.zrel(s)

    def ring(kind, s, o):
        return remote(
            buf(kind).at[o, k], buf(kind).at[o, k], ring_send.at[kind, s], ring_recv.at[kind, s],
            f, above if kind < 2 else below,
        )

    def beside(kind, s, core):
        o = origin(kind, s)
        return remote(
            buf(kind).at[o, core], buf(kind).at[o, core], sib_send.at[kind, s], sib_recv.at[kind, s], f, p.sib
        )

    def wring(up, dist, o):
        by = 2 - dist % 2 if isinstance(dist, int) else 2 - lax.rem(dist, 2)
        to = p.zrel(by) if up == 0 else p.zrel(-by)
        return remote(
            wbuf.at[o], wbuf.at[o], w_send.at[up, dist], w_recv.at[up, dist], f, p.at(half, to, k)
        )

    for kind in (0, 2, 1, 3):
        ring(kind, 1, z).start()
    for up in (0, 1):
        wring(up, 1, z).start()
        wring(up, 2, z).start()
    for kind in (0, 1):
        beside(kind, 0, k).start()
    to_mate = remote(q_ref, q2, q_sem.at[0], q_sem.at[1], f, p.mate)

    @pl.when(half == 1)
    def _():
        to_mate.start()

    weights.start()

    def fold(who, blocks, masked=False):
        q = q_ref if who == 0 else q2
        heads = [slice(h * HD, (h + 1) * HD) for h in range(2)]

        def rows(ref, o, h):
            return ref[o, :, :, heads[h]].reshape(2 * tok, HD)

        scores = [[dot_nt(q[:, heads[h]], rows(kbuf, o, h)) for o in blocks] for h in range(2)]
        if masked:
            at = lax.broadcasted_iota(jnp.int32, (tok, 2 * tok), 1)
            seen = at <= k * tok + lax.broadcasted_iota(jnp.int32, (tok, 2 * tok), 0)
            scores = [[jnp.where(seen, x, -1e30) for x in per_head] for per_head in scores]
        parts, m_old, m_new = [], [], []
        for h in range(2):
            parts.append([x[:, i * tok : (i + 1) * tok] for x in scores[h] for i in range(2)])
            top = jnp.max(functools.reduce(jnp.maximum, parts[h]), axis=1, keepdims=True)
            m_old.append(m_s[who, h])
            m_new.append(jnp.maximum(m_old[h], top))
        for h in range(2):
            keep = jnp.exp2((m_old[h] - m_new[h]) * SCALE)
            e = [jnp.exp2((x - m_new[h]) * SCALE) for x in parts[h]]
            m_s[who, h] = m_new[h]
            l_s[who, h] = l_s[who, h] * keep + functools.reduce(jnp.add, e)
            acc = acc_s[who, h] * keep
            for i, o in enumerate(blocks):
                both = jnp.concatenate([e[2 * i].astype(BF16), e[2 * i + 1].astype(BF16)], axis=1)
                acc = acc + jnp.dot(both, rows(vbuf, o, h), preferred_element_type=F32)
            acc_s[who, h] = acc

    def arrive(kind, s):
        o = origin(kind, s)
        ring(kind, s, o).wait_recv()
        last = steps if kind < 2 else steps - 1

        @pl.when(s < last)
        def _():
            ring(kind, s + 1, o).start()

        beside(kind, s, k).start()

    def w_origin(up, dist):
        return p.zrel(-dist) if up == 0 else p.zrel(dist)

    def w_arrive(s):
        for up in (0, 1):
            last = steps if up == 0 else steps - 1
            o = w_origin(up, 2 * s - 1)
            wring(up, 2 * s - 1, o).wait_recv()
            to_plane(o)

            @pl.when(2 * s <= last)
            def _():
                o = w_origin(up, 2 * s)
                wring(up, 2 * s, o).wait_recv()

                @pl.when(2 * s + 1 <= last)
                def _():
                    wring(up, 2 * s + 1, o).start()

                @pl.when(2 * s + 2 <= last)
                def _():
                    wring(up, 2 * s + 2, o).start()

                to_plane(o)

    def plane_copy(o, h):
        return remote(
            wbuf.at[o], wt_ref.at[lax.rem(o, per), k, :, pl.ds(pl.multiple_of(f * wide, wide), wide)],
            w2_send.at[o, h], w2_recv.at[f], half * groups + o // per, p.at(h, z, k),
        )

    def is_self(o, h):
        return jnp.logical_and(half * groups + o // per == f, half == h)

    def to_plane(o):
        for h in range(2):

            @pl.when(jnp.logical_not(is_self(o, h)))
            def _():
                plane_copy(o, h).start()

            @pl.when(is_self(o, h))
            def _():
                wt_ref[lax.rem(o, per), k, :, pl.ds(pl.multiple_of(f * wide, wide), wide)] = wbuf[o]

    def first_fold():
        beside(0, 0, 1 - k).wait_recv()
        beside(1, 0, 1 - k).wait_recv()

        @pl.when(half == 0)
        def _():
            to_mate.wait_recv()
            fold(1, (z,))

        fold(0, (z,), masked=True)

    def fold_step(s):
        low, high = origin(0, s), origin(2, s)
        for kind in range(4):
            beside(kind, s, 1 - k).wait_recv()
        from_low, from_high = z >= s, z + s >= Z

        @pl.when(half == 0)
        def _():
            fold(1, (low, high))

        @pl.when(jnp.logical_and(from_low, from_high))
        def _():
            fold(0, (low, high))

        @pl.when(jnp.logical_and(from_low, jnp.logical_not(from_high)))
        def _():
            fold(0, (low,))

        @pl.when(jnp.logical_and(from_high, jnp.logical_not(from_low)))
        def _():
            fold(0, (high,))

    to_plane(z)

    def from_plane(fs):
        return remote(
            wbuf.at[pl.ds(0, per)], wt_ref.at[:, k, :, pl.ds(fs * wide, wide)],
            w2_send.at[0, 0], w2_recv.at[fs], fs, p.at(p.row, z, k),
        )

    across = remote(wt_ref.at[:, k], wt_ref.at[:, k], ws_sem.at[0], ws_sem.at[1], f, p.sib)

    def collect():
        for fs in range(F):

            @pl.when(jnp.logical_not(jnp.logical_and(mine, fs == f)))
            def _():
                from_plane(fs).wait_recv()

        across.start()

    @pl.loop(1, steps + 1)
    def _(s):
        arrive(0, s)

        @pl.when(s < steps)
        def _():
            arrive(2, s)

        arrive(1, s)

        @pl.when(s < steps)
        def _():
            arrive(3, s)

        @pl.when(jnp.logical_and(s > 1, s <= steps // 2 + 1))
        def _():
            w_arrive(s - 1)

        @pl.when(s == 3)
        def _():
            weights.share()

        @pl.when(s == steps // 2 + 1)
        def _():
            weights.partial()

        @pl.when(s == steps // 2 + 2)
        def _():
            weights.halves()

        @pl.when(s == steps)
        def _():
            weights.gather()

        @pl.when(s == 1)
        def _():
            first_fold()

        @pl.when(s > 1)
        def _():
            fold_step(s - 1)

    far = origin(0, steps)
    beside(0, steps, 1 - k).wait_recv()
    beside(1, steps, 1 - k).wait_recv()
    lane = lax.broadcasted_iota(jnp.int32, (tok, 128), 1)
    back = [
        remote(acc_s.at[1], o_in, o_send.at[0], o_recv.at[0], f, p.mate),
        remote(st_out, st_in, o_send.at[1], o_recv.at[1], f, p.mate),
    ]

    @pl.when(half == 0)
    def _():
        fold(1, (far,))
        back[0].start()
        stats = jnp.zeros((tok, 128), F32)
        for h in range(2):
            stats = jnp.where(lane == h, m_s[1, h], stats)
            stats = jnp.where(lane == 2 + h, jnp.sum(l_s[1, h], axis=1, keepdims=True), stats)
        st_out[...] = stats.T[:8]
        back[1].start()

    @pl.when(z >= steps)
    def _():
        fold(0, (far,))

    collect()

    def store(h, acc, total):
        att_ref[:, h * HD : (h + 1) * HD] = (acc / total).astype(BF16)

    @pl.when(half == 0)
    def _():
        for h in range(2):
            store(h, acc_s[0, h], jnp.sum(l_s[0, h], axis=1, keepdims=True))

    @pl.when(half == 1)
    def _():
        back[0].wait_recv()
        back[1].wait_recv()
        tbuf[...] = jnp.zeros_like(tbuf)
        tbuf[:8] = st_in[...]
        stats = tbuf[...].T
        for h in range(2):
            m_a, l_a = m_s[0, h], jnp.sum(l_s[0, h], axis=1, keepdims=True)
            m_b = jnp.max(jnp.where(lane == h, stats, -3e38), axis=1, keepdims=True)
            l_b = jnp.sum(jnp.where(lane == 2 + h, stats, 0.0), axis=1, keepdims=True)
            m = jnp.maximum(m_a, m_b)
            e_a, e_b = jnp.exp2((m_a - m) * SCALE), jnp.exp2((m_b - m) * SCALE)
            store(h, acc_s[0, h] * e_a + o_in[h] * e_b, l_a * e_a + l_b * e_b)

    def early():
        weights.finish()
        remote(wt_ref.at[:, 1 - k], wt_ref.at[:, 1 - k], ws_sem.at[0], ws_sem.at[1], f, p.sib).wait_recv()

    def drain():
        attend_drain(p, ring, beside, wring, plane_copy, is_self, across, back, to_mate)

    return early, drain


def attend_drain(p, ring, beside, wring, plane_copy, is_self, across, back, to_mate):
    z, k, half, steps = p.z, p.k, p.half, p.Z // 2

    @pl.loop(1, steps + 1)
    def _(s):
        for kind in (0, 1):
            ring(kind, s, z).wait_send()
            beside(kind, s, k).wait_send()
        wring(0, s, z).wait_send()

        @pl.when(s < steps)
        def _():
            for kind in (2, 3):
                ring(kind, s, z).wait_send()
                beside(kind, s, k).wait_send()
            wring(1, s, z).wait_send()

    for kind in (0, 1):
        beside(kind, 0, k).wait_send()

    @pl.loop(0, p.Z)
    def _(o):
        for h in range(2):

            @pl.when(jnp.logical_not(is_self(o, h)))
            def _():
                plane_copy(o, h).wait_send()

    across.wait_send()

    @pl.when(half == 0)
    def _():
        back[0].wait_send()
        back[1].wait_send()

    @pl.when(half == 1)
    def _():
        to_mate.wait_send()


def head_phase(
    p, early, att_ref, wt_ref, stream, sp, mall, lat_ref, flip_ref, hg_ref,
    attbuf, edge_out, edge_in, flip_out, flip_in, last_out, last_in, part, cbuf, zbuf, nbuf, hbuf, hbuf_in, qbuf, full,
    att_send, att_recv, edge_sem, flip_sem, last_sem, core_sem, half_sem, zs_send, zs_recv, zq_send, zq_recv,
    zg_send, zg_recv, core2_sem,
):
    F, C = p.F, p.C
    f, c, z, k, half, Z = p.f, p.c, p.z, p.k, p.half, p.Z
    tok, wide = att_ref.shape
    chan = lat_ref.shape[0]
    mirror, mirror2 = C - 1 - c, lax.rem(2 * C - 2 - c, C)
    own_last = mirror2 == c
    lane = lax.broadcasted_iota(jnp.int32, (chan, tok), 1)

    def as_column(row):
        return jnp.broadcast_to(row, (tok, 128)).T

    mine = pl.ds(pl.multiple_of(f * wide, wide), wide)
    attbuf[:, mine] = att_ref[...]

    def att_copy(r):
        return remote(
            att_ref, attbuf.at[:, mine], att_send.at[r], att_recv.at[f], lax.rem(f + r, F), c
        )

    @pl.loop(1, F)
    def _(r):
        att_copy(r).start()

    lat_t = lat_ref[...]
    edge_out[...] = jnp.concatenate([lat_t, lat_t], axis=0).T[:8]
    edge = remote(edge_out, edge_in, edge_sem.at[0], edge_sem.at[1], f, p.prev)
    edge.start()
    share = hg_ref.shape[0]
    stream_t = stream[:, pl.ds(pl.multiple_of(f * share, 128), share)].astype(F32).T
    early()
    m_all = split3(mall[...].reshape(2 * chan, F * wide))
    edge.wait_recv()
    lat_next = jnp.where(lane == tok - 1, as_column(edge_in[0:1])[:chan], pltpu.roll(lat_t, tok - 1, 1))

    @pl.loop(1, F)
    def _(r):
        fs = lax.rem(f + r, F)
        there = pl.ds(pl.multiple_of(fs * wide, wide), wide)
        remote(att_ref, attbuf.at[:, there], att_send.at[r], att_recv.at[fs], fs, c).wait_recv()

    heads = attbuf[...]
    pred = sp[...] + (dot_nt(m_all[2], heads) + dot_nt(m_all[1], heads) + dot_nt(m_all[0], heads))
    resid = stream_t + dot_nt(wt_ref[...].reshape(share, F * wide), heads)
    r_hi, r_mid, r_lo = split3(resid)
    final = jnp.logical_and(c == C - 1, lane == tok - 1)
    shift = jnp.where(final, 0.0, pred[:chan])
    log_scale = jnp.where(final, 0.0, pred[chan:])
    inverse = jnp.exp(-log_scale)
    white = (lat_next - shift) * inverse
    loss_scale = float(tok * C) ** -0.5
    d_shift = jnp.where(final, 0.0, -white * inverse * loss_scale)
    d_log = jnp.where(final, 0.0, (1.0 - white * white) * loss_scale)
    d_hi, d_mid, d_lo = split3(jnp.concatenate([d_shift, d_log], axis=0))
    grad = dot_nt(r_hi, d_lo) + dot_nt(r_lo, d_hi) + dot_nt(r_mid, d_mid)
    grad += dot_nt(r_hi, d_mid) + dot_nt(r_mid, d_hi)
    grad += dot_nt(r_hi, d_hi)
    part[...] = grad.reshape(part.shape)

    core_copy = remote(part.at[1 - k], cbuf, core_sem.at[0], core_sem.at[1], f, p.sib)
    core_copy.start()

    t_i = lax.broadcasted_iota(jnp.int32, (tok, tok), 0)
    r_i = lax.broadcasted_iota(jnp.int32, (tok, tok), 1)
    swap = jnp.where(t_i == tok - 2 - r_i, 1.0, 0.0).astype(BF16)
    w_hi, w_mid, w_lo = split3(white)
    turned = jnp.dot(w_hi, swap, preferred_element_type=F32) + jnp.dot(w_mid, swap, preferred_element_type=F32)
    flip_out[...] = turned + jnp.dot(w_lo, swap, preferred_element_type=F32)
    last_out[...] = jnp.concatenate([white, white], axis=0).T[tok - 8 :]
    flip_copy = remote(flip_out, flip_in, flip_sem.at[0], flip_sem.at[1], f, mirror)
    last_copy = remote(last_out, last_in, last_sem.at[0], last_sem.at[1], f, mirror2)

    core_copy.wait_recv()
    zbuf[...] = part[k] + cbuf[...]
    g, q = lax.rem(z, 4), z // 4
    quads = Z // 4

    def near(r):
        i = lax.rem(g + r, 4)
        return i, p.at(half, q * 4 + i, k)

    def far(r):
        i = lax.rem(q + r, quads)
        return i, p.at(half, i * 4 + g, k)

    for r in range(1, 4):
        i, there = near(r)
        remote(zbuf.at[i], nbuf.at[g], zs_send.at[r], zs_recv.at[g], f, there).start()
    nbuf[g] = zbuf[g]
    for r in range(1, 4):
        i, there = near(r)
        remote(zbuf.at[i], nbuf.at[i], zs_send.at[r], zs_recv.at[i], f, there).wait_recv()
    hbuf[...] = nbuf[0] + nbuf[1] + nbuf[2] + nbuf[3]
    half_copy = remote(hbuf, hbuf_in, half_sem.at[0], half_sem.at[1], f, p.mate)
    half_copy.start()
    half_copy.wait_recv()
    qbuf[q] = hbuf[...] + hbuf_in[...]
    for r in range(1, quads):
        i, there = far(r)
        remote(qbuf.at[q], qbuf.at[q], zq_send.at[r], zq_recv.at[q], f, there).start()
    flip_copy.start()

    @pl.when(own_last)
    def _():
        last_in[...] = last_out[...]

    @pl.when(jnp.logical_not(own_last))
    def _():
        last_copy.start()

    for r in range(1, quads):
        i, there = far(r)
        remote(qbuf.at[i], qbuf.at[i], zq_send.at[r], zq_recv.at[i], f, there).wait_recv()
    full[k, g] = functools.reduce(jnp.add, [qbuf[i] for i in range(quads)])
    for r in range(1, 4):
        i, there = near(r)
        remote(full.at[k, g], full.at[k, g], zg_send.at[r], zg_recv.at[g], f, there).start()

    flip_copy.wait_recv()

    @pl.when(jnp.logical_not(own_last))
    def _():
        last_copy.wait_recv()

    flip_ref[...] = jnp.where(lane == tok - 1, as_column(last_in[7:8])[:chan], flip_in[...])

    for r in range(1, 4):
        i, there = near(r)
        remote(full.at[k, i], full.at[k, i], zg_send.at[r], zg_recv.at[i], f, there).wait_recv()
    to_core = remote(full.at[k], full.at[k], core2_sem.at[0], core2_sem.at[1], f, p.sib)
    to_core.start()
    remote(full.at[1 - k], full.at[1 - k], core2_sem.at[0], core2_sem.at[1], f, p.sib).wait_recv()
    hg_ref[...] = full[...].reshape(hg_ref.shape)

    @pl.loop(1, F)
    def _(r):
        att_copy(r).wait_send()

    for r in range(1, 4):
        i, there = near(r)
        remote(zbuf.at[i], nbuf.at[0], zs_send.at[r], zs_recv.at[0], f, there).wait_send()
        remote(full.at[k, g], full.at[k, g], zg_send.at[r], zg_recv.at[0], f, there).wait_send()
    for r in range(1, quads):
        i, there = far(r)
        remote(qbuf.at[q], qbuf.at[q], zq_send.at[r], zq_recv.at[0], f, there).wait_send()

    for copy in (edge, core_copy, half_copy, flip_copy, to_core):
        copy.wait_send()

    @pl.when(jnp.logical_not(own_last))
    def _():
        last_copy.wait_send()


def kernel(F, C, lat_hbm, stream_hbm, q_hbm, k_hbm, v_hbm, w_hbm, wh_hbm, flip_ref, hg_ref, *scratch):
    p = Place(F, C)
    bufs = dict(zip(NAMES, scratch))
    g = bufs.__getitem__
    weights = Weights(p, *map(g, WEIGHTS))
    h, at, per = weights.own(p.f)
    early_loads = [pltpu.make_async_copy(wh_hbm, g("whv").at[h, pl.ds(at, per)], g("in_sem").at[4])]
    late = [
        pltpu.make_async_copy(stream_hbm, g("stream"), g("in_sem").at[5]),
        pltpu.make_async_copy(lat_hbm, g("lat"), g("in_sem").at[6]),
    ]
    for copy in early_loads:
        copy.start()
    entry(p, q_hbm, k_hbm, v_hbm, w_hbm, g("kbuf"), g("vbuf"), g("wbuf"), g("qbuf"), g("in_sem"))
    for copy in late:
        copy.start()
    for copy in early_loads + late:
        copy.wait()
    early, drain = attend_phase(p, weights, *map(g, ATTEND))
    head_phase(
        p, early, g("att"), g("wt"), g("stream"), g("sp"), g("mall"), g("lat"), flip_ref, hg_ref, *map(g, HEAD)
    )
    drain()
    weights.drain()


WEIGHTS = (
    "wbuf", "whv", "stream", "sp", "mp", "m_in", "m_half", "m_in2", "mall",
    "wh_send", "wh_recv", "whs_sem", "ms_sem", "mm_sem", "mg_send", "mg_recv", "mx_sem",
)
ATTEND = (
    "qbuf", "kbuf", "vbuf", "wbuf", "q2", "m_s", "l_s", "acc_s", "o_in", "st_out", "st_in", "tbuf", "att", "wt",
    "ring_send", "ring_recv", "sib_send", "sib_recv", "w_send", "w_recv", "w2_send", "w2_recv", "ws_sem", "q_sem",
    "o_send", "o_recv",
)
HEAD = (
    "attbuf", "edge_out", "edge_in", "flip_out", "flip_in", "last_out", "last_in", "part", "cbuf", "zbuf", "nbuf", "hbuf",
    "hbuf_in", "quart", "full", "att_send", "att_recv", "edge_sem", "flip_sem", "last_sem", "core_sem", "half_sem",
    "zs_send", "zs_recv", "zq_send", "zq_recv", "zg_send", "zg_recv", "core2_sem",
)


def shapes(F, C, tok, width, cols, wide, chan, share):
    Z = C // 4
    per, n = Z // (F // 2), Z // 2 + 1
    block = (share // 8, 2 * chan)
    dma = pltpu.SemaphoreType.DMA

    def v(*shape, dtype=F32):
        return pltpu.VMEM(shape, dtype)

    return dict(
        qbuf=v(tok, width, dtype=BF16), kbuf=v(Z, 2, tok, width, dtype=BF16), vbuf=v(Z, 2, tok, width, dtype=BF16),
        wbuf=v(Z, cols, wide, dtype=BF16), q2=v(tok, width, dtype=BF16), m_s=v(2, 2, tok, 128), l_s=v(2, 2, tok, 128),
        acc_s=v(2, 2, tok, HD), o_in=v(2, tok, HD), st_out=v(8, tok), st_in=v(8, tok), tbuf=v(128, tok),
        att=v(tok, width, dtype=BF16), wt=v(per, 2, cols, F * wide, dtype=BF16),
        ring_send=dma((4, n)), ring_recv=dma((4, n)), sib_send=dma((4, n)), sib_recv=dma((4, n)),
        w_send=dma((2, n)), w_recv=dma((2, n)), w2_send=dma((Z, 2)), w2_recv=dma((F,)), ws_sem=dma((2,)),
        q_sem=dma((2,)), o_send=dma((2,)), o_recv=dma((2,)), in_sem=dma((7,)),
        stream=v(tok, share * F, dtype=BF16), lat=v(chan, tok), whv=v(2, Z, 2, cols, 2 * chan, dtype=BF16),
        sp=v(2 * chan, tok), mp=v(2, chan, wide), m_in=v(chan, wide), m_half=v(chan, wide), m_in2=v(chan, wide),
        mall=v(2, chan, F * wide), wh_send=dma((F,)), wh_recv=dma((F,)), whs_sem=dma((2, F)), ms_sem=dma((2,)),
        mm_sem=dma((2,)), mg_send=dma((F,)), mg_recv=dma((F,)), mx_sem=dma((2,)),
        attbuf=v(tok, F * wide, dtype=BF16), edge_out=v(8, 128), edge_in=v(8, 128),
        flip_out=v(chan, tok), flip_in=v(chan, tok), last_out=v(8, 2 * chan), last_in=v(8, 2 * chan),
        part=v(2, 4, *block), cbuf=v(4, *block), zbuf=v(4, *block), nbuf=v(4, *block), hbuf=v(*block), hbuf_in=v(*block),
        quart=v(Z // 4, *block), full=v(2, 4, *block),
        att_send=dma((F,)), att_recv=dma((F,)), edge_sem=dma((2,)), flip_sem=dma((2,)), last_sem=dma((2,)),
        core_sem=dma((2,)), half_sem=dma((2,)), zs_send=dma((4,)), zs_recv=dma((4,)), zq_send=dma((Z // 4,)),
        zq_recv=dma((Z // 4,)), zg_send=dma((4,)), zg_recv=dma((4,)), core2_sem=dma((2,)),
    )


NAMES = tuple(shapes(8, 64, 128, 256, 48, 256, 64, 384))


def shards(F, C, latents, stream, queries, key_rows, value_rows, w_mix, w_head):
    tok, chan = latents.shape
    share, chan2 = w_head.shape
    width = queries.shape[1]
    w_t = w_mix.T
    vmem = pl.BlockSpec(memory_space=pltpu.VMEM)
    flipped, grad = pl.pallas_call(
        functools.partial(kernel, F, C),
        out_shape=(
            jax.ShapeDtypeStruct((chan, tok), F32),
            jax.ShapeDtypeStruct((share, chan2), F32),
        ),
        in_specs=[pl.BlockSpec(memory_space=pl.ANY)] * 7,
        out_specs=(vmem, vmem),
        scratch_shapes=list(shapes(F, C, tok, width, *w_t.shape, chan, share).values()),
        compiler_params=pltpu.CompilerParams(
            collective_id=0, has_side_effects=True, vmem_limit_bytes=60 * 1024 * 1024
        ),
        name="coupling",
    )(latents.T, stream, queries, key_rows, value_rows, w_t, w_head.reshape(-1, 2, w_t.shape[0], chan2))
    return flipped.T, grad


def solution(mesh):
    return jax.shard_map(
        functools.partial(shards, mesh.shape["fsdp"], mesh.shape["ctx"]),
        mesh=mesh,
        in_specs=(
            P("ctx", None),
            P("ctx", None),
            P("ctx", "fsdp"),
            P("ctx", "fsdp"),
            P("ctx", "fsdp"),
            P("fsdp", "ctx"),
            P("fsdp", None),
        ),
        out_specs=(P("ctx", None), P("fsdp", None)),
        check_vma=False,
    )
```

```python
import functools
import math

import jax
import jax.numpy as jnp
from jax import lax
from jax.experimental import pallas as pl
from jax.experimental.pallas import tpu as pltpu
from jax.sharding import PartitionSpec as P

HD = 128
MESH = pl.DeviceIdType.MESH
F32, BF16 = jnp.float32, jnp.bfloat16
NT_DIMS = (((1,), (1,)), ((), ()))
SCALE = HD**-0.5 * math.log2(math.e)


def remote(src, dst, send, recv, f, c):
    return pltpu.make_async_remote_copy(
        src_ref=src, dst_ref=dst, send_sem=send, recv_sem=recv, device_id=(f, c), device_id_type=MESH
    )


def greet(barrier, f, c):
    pl.semaphore_signal(barrier, inc=1, device_id=(f, c), device_id_type=MESH)


class Place:
    def __init__(self, F, C):
        self.F, self.C, self.Z = F, C, C // 4
        self.f, self.c = lax.axis_index("fsdp"), lax.axis_index("ctx")
        self.row = self.f // (F // 2)
        self.half = self.c // (C // 2)
        self.z = lax.rem(self.c, C // 2) // 2
        self.k = lax.rem(self.c, 2)
        self.sib = self.c + 1 - 2 * self.k
        self.mate = lax.rem(self.c + C // 2, C)
        self.prev, self.next = lax.rem(self.c + C - 1, C), lax.rem(self.c + 1, C)

    def at(self, half, z, k):
        return half * (self.C // 2) + z * 2 + k

    def plane(self, r):
        i = lax.rem(self.half * self.F + self.f + r, 2 * self.F)
        return lax.rem(i, self.F), self.at(i // self.F, self.z, self.k)

    def zrel(self, by):
        return lax.rem(self.z + by + self.Z, self.Z)


def dot_nt(a, b):
    return lax.dot_general(a, b, NT_DIMS, preferred_element_type=F32)


def split3(x):
    a = x.astype(BF16)
    rest = x - a.astype(F32)
    b = rest.astype(BF16)
    return a, b, (rest - b.astype(F32)).astype(BF16)


def entry(p, q_ref, k_ref, v_ref, w_ref, kbuf, vbuf, wbuf, qbuf, in_sem):
    z, k = p.z, p.k
    loads = [
        pltpu.make_async_copy(k_ref, kbuf.at[z, k], in_sem.at[0]),
        pltpu.make_async_copy(v_ref, vbuf.at[z, k], in_sem.at[1]),
        pltpu.make_async_copy(w_ref, wbuf.at[z], in_sem.at[2]),
        pltpu.make_async_copy(q_ref, qbuf, in_sem.at[3]),
    ]
    for load in loads:
        load.start()
    barrier = pltpu.get_barrier_semaphore()
    for c in (p.at(p.half, p.zrel(1), k), p.at(p.half, p.zrel(-1), k), p.sib, p.prev, p.next):
        greet(barrier, p.f, c)
    for r in (2, -2):
        greet(barrier, p.f, p.at(p.half, p.zrel(r), k))

    @pl.loop(1, 2 * p.F)
    def _(r):
        greet(barrier, *p.plane(r))

    for load in loads:
        load.wait()
    pl.semaphore_wait(barrier, 7 + 2 * p.F - 1)


class Weights:
    def __init__(
        self, p, wbuf, whv, stream, sp, mp, m_in, m_half, m_in2, mall, m3,
        wh_send, wh_recv, whs_sem, ms_sem, mm_sem, mx_sem,
    ):
        self.p, self.wbuf, self.whv, self.stream, self.sp = p, wbuf, whv, stream, sp
        self.mp, self.m_in, self.m_half, self.m_in2, self.mall = mp, m_in, m_half, m_in2, mall
        self.m3 = m3
        self.wh_sems = (wh_send, wh_recv)
        f, k = p.f, p.k
        self.whs_sem, self.mx_sem = whs_sem, mx_sem
        self.to_sib = remote(mp.at[1 - k], m_in, ms_sem.at[0], ms_sem.at[1], f, p.sib)
        self.to_mate = remote(m_half, m_in2, mm_sem.at[0], mm_sem.at[1], f, p.mate)

    def own(self, fs):
        groups = self.p.F // 2
        per = self.p.Z // groups
        return fs // groups, lax.rem(fs, groups) * per, per

    def rows(self, fs, core):
        h, at, per = self.own(fs)
        return self.whv.at[h, pl.ds(at + core * (per // 2), per // 2)]

    def head_copy(self, r, fs):
        p = self.p
        send, recv = self.wh_sems
        return remote(self.rows(fs, p.k), self.rows(fs, p.k), send.at[r], recv.at[fs], lax.rem(p.f + r, p.F), p.c)

    def beside(self, core, fs):
        return remote(
            self.rows(fs, core), self.rows(fs, core), self.whs_sem.at[0, fs], self.whs_sem.at[1, fs], self.p.f, self.p.sib
        )

    def start(self):
        @pl.loop(1, self.p.F)
        def _(r):
            self.head_copy(r, self.p.f).start()

    def share(self):
        p = self.p

        @pl.loop(1, p.F)
        def _(r):
            fs = lax.rem(p.f + r, p.F)
            self.head_copy(r, fs).wait_recv()
            self.beside(p.k, fs).start()

    def partial(self):
        p = self.p

        @pl.loop(1, p.F)
        def _(r):
            self.beside(1 - p.k, lax.rem(p.f + r, p.F)).wait_recv()

        width = self.wbuf.shape[2]
        rows = self.whv[p.half, :, p.k].reshape(-1, 128)
        pieces = self.wbuf[...].reshape(-1, width)
        out = jnp.dot(rows.astype(F32).T.astype(BF16), pieces, preferred_element_type=F32)
        self.mp[...] = out.reshape(self.mp.shape)
        self.to_sib.start()

    def halves(self):
        self.to_sib.wait_recv()
        self.m_half[...] = self.mp[self.p.k] + self.m_in[...]
        self.to_mate.start()

    def whole(self):
        self.to_mate.wait_recv()
        self.mall[self.p.k] = self.m_half[...] + self.m_in2[...]
        self.across(self.p.k).start()

    def across(self, core):
        return remote(self.mall.at[core], self.mall.at[core], self.mx_sem.at[0], self.mx_sem.at[1], self.p.f, self.p.sib)

    def settle(self):
        self.across(1 - self.p.k).wait_recv()
        for i, part in enumerate(split3(self.mall[...].reshape(self.m3.shape[1:]))):
            self.m3[i] = part

    def stream_part(self):
        self.sp[...] = jnp.dot(self.stream[...], self.whv[...].reshape(-1, 128), preferred_element_type=F32).T

    def drain(self):
        p = self.p

        @pl.loop(1, p.F)
        def _(r):
            self.head_copy(r, p.f).wait_send()
            self.beside(p.k, lax.rem(p.f + r, p.F)).wait_send()

        self.to_sib.wait_send()
        self.to_mate.wait_send()
        self.across(p.k).wait_send()


def attend_phase(
    p, weights, q_ref, kbuf, vbuf, wbuf, q2, m_s, l_s, acc_s, o_in, st_out, st_in, tbuf, att_ref, wt_ref,
    ring_send, ring_recv, sib_send, sib_recv, w_send, w_recv, w2_send, w2_recv, ws_sem, q_sem, o_send, o_recv,
):
    F = p.F
    f, z, k, half, Z = p.f, p.z, p.k, p.half, p.Z
    steps, groups = Z // 2, F // 2
    per = Z // groups
    tok = q_ref.shape[0]
    wide = wbuf.shape[2]
    above, below = p.at(half, p.zrel(1), k), p.at(half, p.zrel(-1), k)
    mine = p.row == half

    m_s[...] = jnp.full_like(m_s, -1e30)
    l_s[...] = jnp.zeros_like(l_s)
    acc_s[...] = jnp.zeros_like(acc_s)

    def buf(kind):
        return kbuf if kind % 2 == 0 else vbuf

    def origin(kind, s):
        return p.zrel(-s) if kind < 2 else p.zrel(s)

    def ring(kind, s, o):
        return remote(
            buf(kind).at[o, k], buf(kind).at[o, k], ring_send.at[kind, s], ring_recv.at[kind, s],
            f, above if kind < 2 else below,
        )

    def beside(kind, s, core):
        o = origin(kind, s)
        return remote(
            buf(kind).at[o, core], buf(kind).at[o, core], sib_send.at[kind, s], sib_recv.at[kind, s], f, p.sib
        )

    def wring(up, dist, o):
        by = 2 - dist % 2 if isinstance(dist, int) else 2 - lax.rem(dist, 2)
        to = p.zrel(by) if up == 0 else p.zrel(-by)
        return remote(
            wbuf.at[o], wbuf.at[o], w_send.at[up, dist], w_recv.at[up, dist], f, p.at(half, to, k)
        )

    for kind in (0, 2, 1, 3):
        ring(kind, 1, z).start()
    for up in (0, 1):
        wring(up, 1, z).start()
        wring(up, 2, z).start()
    for kind in (0, 1):
        beside(kind, 0, k).start()
    to_mate = remote(q_ref, q2, q_sem.at[0], q_sem.at[1], f, p.mate)

    @pl.when(half == 1)
    def _():
        to_mate.start()

    weights.start()

    def fold(who, blocks, masked=False):
        q = q_ref if who == 0 else q2
        heads = [slice(h * HD, (h + 1) * HD) for h in range(2)]

        def rows(ref, o, h):
            return ref[o, :, :, heads[h]].reshape(2 * tok, HD)

        scores = [[dot_nt(q[:, heads[h]], rows(kbuf, o, h)) for o in blocks] for h in range(2)]
        if masked:
            at = lax.broadcasted_iota(jnp.int32, (tok, 2 * tok), 1)
            seen = at <= k * tok + lax.broadcasted_iota(jnp.int32, (tok, 2 * tok), 0)
            scores = [[jnp.where(seen, x, -1e30) for x in per_head] for per_head in scores]
        parts, m_old, m_new = [], [], []
        for h in range(2):
            parts.append([x[:, i * tok : (i + 1) * tok] for x in scores[h] for i in range(2)])
            top = jnp.max(functools.reduce(jnp.maximum, parts[h]), axis=1, keepdims=True)
            m_old.append(m_s[who, h])
            m_new.append(jnp.maximum(m_old[h], top))
        for h in range(2):
            keep = jnp.exp2((m_old[h] - m_new[h]) * SCALE)
            e = [jnp.exp2((x - m_new[h]) * SCALE) for x in parts[h]]
            m_s[who, h] = m_new[h]
            l_s[who, h] = l_s[who, h] * keep + functools.reduce(jnp.add, e)
            acc = acc_s[who, h] * keep
            for i, o in enumerate(blocks):
                both = jnp.concatenate([e[2 * i].astype(BF16), e[2 * i + 1].astype(BF16)], axis=1)
                acc = acc + jnp.dot(both, rows(vbuf, o, h), preferred_element_type=F32)
            acc_s[who, h] = acc

    def arrive(kind, s):
        o = origin(kind, s)
        ring(kind, s, o).wait_recv()
        last = steps if kind < 2 else steps - 1

        @pl.when(s < last)
        def _():
            ring(kind, s + 1, o).start()

        beside(kind, s, k).start()

    def w_origin(up, dist):
        return p.zrel(-dist) if up == 0 else p.zrel(dist)

    def w_arrive(s):
        for up in (0, 1):
            last = steps if up == 0 else steps - 1
            o = w_origin(up, 2 * s - 1)
            wring(up, 2 * s - 1, o).wait_recv()
            to_plane(o)

            @pl.when(2 * s <= last)
            def _():
                o = w_origin(up, 2 * s)
                wring(up, 2 * s, o).wait_recv()

                @pl.when(2 * s + 1 <= last)
                def _():
                    wring(up, 2 * s + 1, o).start()

                @pl.when(2 * s + 2 <= last)
                def _():
                    wring(up, 2 * s + 2, o).start()

                to_plane(o)

    def plane_copy(o, h):
        return remote(
            wbuf.at[o], wt_ref.at[lax.rem(o, per), k, :, pl.ds(pl.multiple_of(f * wide, wide), wide)],
            w2_send.at[o, h], w2_recv.at[f], half * groups + o // per, p.at(h, z, k),
        )

    def is_self(o, h):
        return jnp.logical_and(half * groups + o // per == f, half == h)

    def to_plane(o):
        for h in range(2):

            @pl.when(jnp.logical_not(is_self(o, h)))
            def _():
                plane_copy(o, h).start()

            @pl.when(is_self(o, h))
            def _():
                wt_ref[lax.rem(o, per), k, :, pl.ds(pl.multiple_of(f * wide, wide), wide)] = wbuf[o]

    def first_fold():
        beside(0, 0, 1 - k).wait_recv()
        beside(1, 0, 1 - k).wait_recv()

        @pl.when(half == 0)
        def _():
            to_mate.wait_recv()
            fold(1, (z,))

        fold(0, (z,), masked=True)

    def fold_step(s):
        low, high = origin(0, s), origin(2, s)
        for kind in range(4):
            beside(kind, s, 1 - k).wait_recv()
        from_low, from_high = z >= s, z + s >= Z

        @pl.when(half == 0)
        def _():
            fold(1, (low, high))

        @pl.when(jnp.logical_and(from_low, from_high))
        def _():
            fold(0, (low, high))

        @pl.when(jnp.logical_and(from_low, jnp.logical_not(from_high)))
        def _():
            fold(0, (low,))

        @pl.when(jnp.logical_and(from_high, jnp.logical_not(from_low)))
        def _():
            fold(0, (high,))

    to_plane(z)

    def from_plane(fs):
        return remote(
            wbuf.at[pl.ds(0, per)], wt_ref.at[:, k, :, pl.ds(fs * wide, wide)],
            w2_send.at[0, 0], w2_recv.at[fs], fs, p.at(p.row, z, k),
        )

    across = remote(wt_ref.at[:, k], wt_ref.at[:, k], ws_sem.at[0], ws_sem.at[1], f, p.sib)

    def collect():
        for fs in range(F):

            @pl.when(jnp.logical_not(jnp.logical_and(mine, fs == f)))
            def _():
                from_plane(fs).wait_recv()

        across.start()

    @pl.loop(1, steps + 1)
    def _(s):
        arrive(0, s)

        @pl.when(s < steps)
        def _():
            arrive(2, s)

        arrive(1, s)

        @pl.when(s < steps)
        def _():
            arrive(3, s)

        @pl.when(jnp.logical_and(s > 1, s <= steps // 2 + 1))
        def _():
            w_arrive(s - 1)

        @pl.when(s == 3)
        def _():
            weights.share()

        @pl.when(s == steps // 2 + 1)
        def _():
            weights.partial()

        @pl.when(s == steps // 2 + 2)
        def _():
            weights.halves()

        @pl.when(s == steps)
        def _():
            weights.whole()

        @pl.when(s == 1)
        def _():
            first_fold()

        @pl.when(s > 1)
        def _():
            fold_step(s - 1)

    far = origin(0, steps)
    beside(0, steps, 1 - k).wait_recv()
    beside(1, steps, 1 - k).wait_recv()
    lane = lax.broadcasted_iota(jnp.int32, (tok, 128), 1)
    back = [
        remote(acc_s.at[1], o_in, o_send.at[0], o_recv.at[0], f, p.mate),
        remote(st_out, st_in, o_send.at[1], o_recv.at[1], f, p.mate),
    ]

    @pl.when(half == 0)
    def _():
        fold(1, (far,))
        back[0].start()
        stats = jnp.zeros((tok, 128), F32)
        for h in range(2):
            stats = jnp.where(lane == h, m_s[1, h], stats)
            stats = jnp.where(lane == 2 + h, jnp.sum(l_s[1, h], axis=1, keepdims=True), stats)
        st_out[...] = stats.T[:8]
        back[1].start()

    @pl.when(z >= steps)
    def _():
        fold(0, (far,))

    weights.settle()
    collect()

    def store(h, acc, total):
        att_ref[:, h * HD : (h + 1) * HD] = (acc / total).astype(BF16)

    @pl.when(half == 0)
    def _():
        for h in range(2):
            store(h, acc_s[0, h], jnp.sum(l_s[0, h], axis=1, keepdims=True))

    @pl.when(half == 1)
    def _():
        back[0].wait_recv()
        back[1].wait_recv()
        tbuf[...] = jnp.zeros_like(tbuf)
        tbuf[:8] = st_in[...]
        stats = tbuf[...].T
        for h in range(2):
            m_a, l_a = m_s[0, h], jnp.sum(l_s[0, h], axis=1, keepdims=True)
            m_b = jnp.max(jnp.where(lane == h, stats, -3e38), axis=1, keepdims=True)
            l_b = jnp.sum(jnp.where(lane == 2 + h, stats, 0.0), axis=1, keepdims=True)
            m = jnp.maximum(m_a, m_b)
            e_a, e_b = jnp.exp2((m_a - m) * SCALE), jnp.exp2((m_b - m) * SCALE)
            store(h, acc_s[0, h] * e_a + o_in[h] * e_b, l_a * e_a + l_b * e_b)

    def early():
        weights.stream_part()
        remote(wt_ref.at[:, 1 - k], wt_ref.at[:, 1 - k], ws_sem.at[0], ws_sem.at[1], f, p.sib).wait_recv()

    def drain():
        attend_drain(p, ring, beside, wring, plane_copy, is_self, across, back, to_mate)

    return early, drain


def attend_drain(p, ring, beside, wring, plane_copy, is_self, across, back, to_mate):
    z, k, half, steps = p.z, p.k, p.half, p.Z // 2

    @pl.loop(1, steps + 1)
    def _(s):
        for kind in (0, 1):
            ring(kind, s, z).wait_send()
            beside(kind, s, k).wait_send()
        wring(0, s, z).wait_send()

        @pl.when(s < steps)
        def _():
            for kind in (2, 3):
                ring(kind, s, z).wait_send()
                beside(kind, s, k).wait_send()
            wring(1, s, z).wait_send()

    for kind in (0, 1):
        beside(kind, 0, k).wait_send()

    @pl.loop(0, p.Z)
    def _(o):
        for h in range(2):

            @pl.when(jnp.logical_not(is_self(o, h)))
            def _():
                plane_copy(o, h).wait_send()

    across.wait_send()

    @pl.when(half == 0)
    def _():
        back[0].wait_send()
        back[1].wait_send()

    @pl.when(half == 1)
    def _():
        to_mate.wait_send()


def head_phase(
    p, early, att_ref, wt_ref, stream, sp, m3, lat_ref, flip_ref, hg_ref, pp, rs, pall, psum,
    attbuf, edge_out, edge_in, flip_out, flip_in, last_out, last_in, part, cbuf, zbuf, nbuf, hbuf, hbuf_in, qbuf, full,
    rs_send, rs_recv, ag_send, ag_recv, att_send, att_recv, edge_sem, flip_sem, last_sem, core_sem, half_sem, zs_send, zs_recv, zq_send, zq_recv,
    zg_send, zg_recv, core2_sem,
):
    F, C = p.F, p.C
    f, c, z, k, half, Z = p.f, p.c, p.z, p.k, p.half, p.Z
    tok, wide = att_ref.shape
    chan = lat_ref.shape[0]
    mirror, mirror2 = C - 1 - c, lax.rem(2 * C - 2 - c, C)
    own_last = mirror2 == c
    lane = lax.broadcasted_iota(jnp.int32, (chan, tok), 1)

    def as_column(row):
        return jnp.broadcast_to(row, (tok, 128)).T

    mine = pl.ds(pl.multiple_of(f * wide, wide), wide)
    own = att_ref[...]
    pp[...] = (dot_nt(m3[2], own) + dot_nt(m3[1], own) + dot_nt(m3[0], own)).reshape(pp.shape)

    @pl.loop(1, F)
    def _(r):
        to = lax.rem(f + r, F)
        remote(pp.at[to], rs.at[f], rs_send.at[r], rs_recv.at[f], to, c).start()

    attbuf[:, mine] = att_ref[...]

    def att_copy(r):
        return remote(
            att_ref, attbuf.at[:, mine], att_send.at[r], att_recv.at[f], lax.rem(f + r, F), c
        )

    @pl.loop(1, F)
    def _(r):
        att_copy(r).start()

    lat_t = lat_ref[...]
    edge_out[...] = jnp.concatenate([lat_t, lat_t], axis=0).T[:8]
    edge = remote(edge_out, edge_in, edge_sem.at[0], edge_sem.at[1], f, p.prev)
    edge.start()
    share = hg_ref.shape[0]
    rs[f] = pp[f]

    @pl.loop(1, F)
    def _(r):
        fs = lax.rem(f + r, F)
        remote(pp.at[fs], rs.at[fs], rs_send.at[r], rs_recv.at[fs], fs, c).wait_recv()

    psum[...] = jnp.sum(rs[...], axis=0)

    @pl.loop(1, F)
    def _(r):
        remote(psum, pall.at[f], ag_send.at[r], ag_recv.at[f], lax.rem(f + r, F), c).start()

    pall[f] = psum[...]
    stream_t = stream[:, pl.ds(pl.multiple_of(f * share, 128), share)].astype(F32).T
    early()
    edge.wait_recv()
    lat_next = jnp.where(lane == tok - 1, as_column(edge_in[0:1])[:chan], pltpu.roll(lat_t, tok - 1, 1))

    @pl.loop(1, F)
    def _(r):
        fs = lax.rem(f + r, F)
        there = pl.ds(pl.multiple_of(fs * wide, wide), wide)
        remote(att_ref, attbuf.at[:, there], att_send.at[r], att_recv.at[fs], fs, c).wait_recv()

    heads = attbuf[...]
    resid = stream_t + dot_nt(wt_ref[...].reshape(share, F * wide), heads)
    r_hi, r_mid, r_lo = split3(resid)

    @pl.loop(1, F)
    def _(r):
        fs = lax.rem(f + r, F)
        remote(psum, pall.at[fs], ag_send.at[r], ag_recv.at[fs], fs, c).wait_recv()

    pred = sp[...] + pall[...].reshape(2 * chan, tok)
    final = jnp.logical_and(c == C - 1, lane == tok - 1)
    shift = jnp.where(final, 0.0, pred[:chan])
    log_scale = jnp.where(final, 0.0, pred[chan:])
    inverse = jnp.exp(-log_scale)
    white = (lat_next - shift) * inverse
    loss_scale = float(tok * C) ** -0.5
    d_shift = jnp.where(final, 0.0, -white * inverse * loss_scale)
    d_log = jnp.where(final, 0.0, (1.0 - white * white) * loss_scale)
    d_hi, d_mid, d_lo = split3(jnp.concatenate([d_shift, d_log], axis=0))
    grad = dot_nt(r_hi, d_lo) + dot_nt(r_lo, d_hi) + dot_nt(r_mid, d_mid)
    grad += dot_nt(r_hi, d_mid) + dot_nt(r_mid, d_hi)
    grad += dot_nt(r_hi, d_hi)
    part[...] = grad.reshape(part.shape)

    core_copy = remote(part.at[1 - k], cbuf, core_sem.at[0], core_sem.at[1], f, p.sib)
    core_copy.start()

    t_i = lax.broadcasted_iota(jnp.int32, (tok, tok), 0)
    r_i = lax.broadcasted_iota(jnp.int32, (tok, tok), 1)
    swap = jnp.where(t_i == tok - 2 - r_i, 1.0, 0.0).astype(BF16)
    w_hi, w_mid, w_lo = split3(white)
    turned = jnp.dot(w_hi, swap, preferred_element_type=F32) + jnp.dot(w_mid, swap, preferred_element_type=F32)
    flip_out[...] = turned + jnp.dot(w_lo, swap, preferred_element_type=F32)
    last_out[...] = jnp.concatenate([white, white], axis=0).T[tok - 8 :]
    flip_copy = remote(flip_out, flip_in, flip_sem.at[0], flip_sem.at[1], f, mirror)
    last_copy = remote(last_out, last_in, last_sem.at[0], last_sem.at[1], f, mirror2)

    core_copy.wait_recv()
    zbuf[...] = part[k] + cbuf[...]
    g, q = lax.rem(z, 4), z // 4
    quads = Z // 4

    def near(r):
        i = lax.rem(g + r, 4)
        return i, p.at(half, q * 4 + i, k)

    def far(r):
        i = lax.rem(q + r, quads)
        return i, p.at(half, i * 4 + g, k)

    for r in range(1, 4):
        i, there = near(r)
        remote(zbuf.at[i], nbuf.at[g], zs_send.at[r], zs_recv.at[g], f, there).start()
    nbuf[g] = zbuf[g]
    for r in range(1, 4):
        i, there = near(r)
        remote(zbuf.at[i], nbuf.at[i], zs_send.at[r], zs_recv.at[i], f, there).wait_recv()
    hbuf[...] = nbuf[0] + nbuf[1] + nbuf[2] + nbuf[3]
    half_copy = remote(hbuf, hbuf_in, half_sem.at[0], half_sem.at[1], f, p.mate)
    half_copy.start()
    half_copy.wait_recv()
    qbuf[q] = hbuf[...] + hbuf_in[...]
    for r in range(1, quads):
        i, there = far(r)
        remote(qbuf.at[q], qbuf.at[q], zq_send.at[r], zq_recv.at[q], f, there).start()
    flip_copy.start()

    @pl.when(own_last)
    def _():
        last_in[...] = last_out[...]

    @pl.when(jnp.logical_not(own_last))
    def _():
        last_copy.start()

    for r in range(1, quads):
        i, there = far(r)
        remote(qbuf.at[i], qbuf.at[i], zq_send.at[r], zq_recv.at[i], f, there).wait_recv()
    full[k, g] = functools.reduce(jnp.add, [qbuf[i] for i in range(quads)])
    for r in range(1, 4):
        i, there = near(r)
        remote(full.at[k, g], full.at[k, g], zg_send.at[r], zg_recv.at[g], f, there).start()

    flip_copy.wait_recv()

    @pl.when(jnp.logical_not(own_last))
    def _():
        last_copy.wait_recv()

    flip_ref[...] = jnp.where(lane == tok - 1, as_column(last_in[7:8])[:chan], flip_in[...])

    for r in range(1, 4):
        i, there = near(r)
        remote(full.at[k, i], full.at[k, i], zg_send.at[r], zg_recv.at[i], f, there).wait_recv()
    to_core = remote(full.at[k], full.at[k], core2_sem.at[0], core2_sem.at[1], f, p.sib)
    to_core.start()
    remote(full.at[1 - k], full.at[1 - k], core2_sem.at[0], core2_sem.at[1], f, p.sib).wait_recv()
    hg_ref[...] = full[...].reshape(hg_ref.shape)

    @pl.loop(1, F)
    def _(r):
        att_copy(r).wait_send()
        remote(pp.at[0], rs.at[0], rs_send.at[r], rs_recv.at[0], lax.rem(f + r, F), c).wait_send()
        remote(psum, pall.at[0], ag_send.at[r], ag_recv.at[0], lax.rem(f + r, F), c).wait_send()

    for r in range(1, 4):
        i, there = near(r)
        remote(zbuf.at[i], nbuf.at[0], zs_send.at[r], zs_recv.at[0], f, there).wait_send()
        remote(full.at[k, g], full.at[k, g], zg_send.at[r], zg_recv.at[0], f, there).wait_send()
    for r in range(1, quads):
        i, there = far(r)
        remote(qbuf.at[q], qbuf.at[q], zq_send.at[r], zq_recv.at[0], f, there).wait_send()

    for copy in (edge, core_copy, half_copy, flip_copy, to_core):
        copy.wait_send()

    @pl.when(jnp.logical_not(own_last))
    def _():
        last_copy.wait_send()


def kernel(F, C, lat_hbm, stream_hbm, q_hbm, k_hbm, v_hbm, w_hbm, wh_hbm, flip_ref, hg_ref, *scratch):
    p = Place(F, C)
    bufs = dict(zip(NAMES, scratch))
    g = bufs.__getitem__
    weights = Weights(p, *map(g, WEIGHTS))
    h, at, per = weights.own(p.f)
    early_loads = [pltpu.make_async_copy(wh_hbm, g("whv").at[h, pl.ds(at, per)], g("in_sem").at[4])]
    late = [
        pltpu.make_async_copy(stream_hbm, g("stream"), g("in_sem").at[5]),
        pltpu.make_async_copy(lat_hbm, g("lat"), g("in_sem").at[6]),
    ]
    for copy in early_loads:
        copy.start()
    entry(p, q_hbm, k_hbm, v_hbm, w_hbm, g("kbuf"), g("vbuf"), g("wbuf"), g("qbuf"), g("in_sem"))
    for copy in late:
        copy.start()
    for copy in early_loads + late:
        copy.wait()
    early, drain = attend_phase(p, weights, *map(g, ATTEND))
    head_phase(
        p, early, g("att"), g("wt"), g("stream"), g("sp"), g("m3"), g("lat"), flip_ref, hg_ref, *map(g, HEAD)
    )
    drain()
    weights.drain()


WEIGHTS = (
    "wbuf", "whv", "stream", "sp", "mp", "m_in", "m_half", "m_in2", "mall", "m3",
    "wh_send", "wh_recv", "whs_sem", "ms_sem", "mm_sem", "mx_sem",
)
ATTEND = (
    "qbuf", "kbuf", "vbuf", "wbuf", "q2", "m_s", "l_s", "acc_s", "o_in", "st_out", "st_in", "tbuf", "att", "wt",
    "ring_send", "ring_recv", "sib_send", "sib_recv", "w_send", "w_recv", "w2_send", "w2_recv", "ws_sem", "q_sem",
    "o_send", "o_recv",
)
HEAD = (
    "pp", "rs", "pall", "psum", "attbuf", "edge_out", "edge_in", "flip_out", "flip_in", "last_out", "last_in", "part", "cbuf", "zbuf", "nbuf", "hbuf",
    "hbuf_in", "quart", "full", "rs_send", "rs_recv", "ag_send", "ag_recv", "att_send", "att_recv", "edge_sem", "flip_sem", "last_sem", "core_sem", "half_sem",
    "zs_send", "zs_recv", "zq_send", "zq_recv", "zg_send", "zg_recv", "core2_sem",
)


def shapes(F, C, tok, width, cols, wide, chan, share):
    Z = C // 4
    per, n = Z // (F // 2), Z // 2 + 1
    block = (share // 8, 2 * chan)
    dma = pltpu.SemaphoreType.DMA

    def v(*shape, dtype=F32):
        return pltpu.VMEM(shape, dtype)

    return dict(
        qbuf=v(tok, width, dtype=BF16), kbuf=v(Z, 2, tok, width, dtype=BF16), vbuf=v(Z, 2, tok, width, dtype=BF16),
        wbuf=v(Z, cols, wide, dtype=BF16), q2=v(tok, width, dtype=BF16), m_s=v(2, 2, tok, 128), l_s=v(2, 2, tok, 128),
        acc_s=v(2, 2, tok, HD), o_in=v(2, tok, HD), st_out=v(8, tok), st_in=v(8, tok), tbuf=v(128, tok),
        att=v(tok, width, dtype=BF16), wt=v(per, 2, cols, F * wide, dtype=BF16),
        ring_send=dma((4, n)), ring_recv=dma((4, n)), sib_send=dma((4, n)), sib_recv=dma((4, n)),
        w_send=dma((2, n)), w_recv=dma((2, n)), w2_send=dma((Z, 2)), w2_recv=dma((F,)), ws_sem=dma((2,)),
        q_sem=dma((2,)), o_send=dma((2,)), o_recv=dma((2,)), in_sem=dma((7,)),
        stream=v(tok, share * F, dtype=BF16), lat=v(chan, tok), whv=v(2, Z, 2, cols, 2 * chan, dtype=BF16),
        sp=v(2 * chan, tok), mp=v(2, chan, wide), m_in=v(chan, wide), m_half=v(chan, wide), m_in2=v(chan, wide),
        mall=v(2, chan, wide), m3=v(3, 2 * chan, wide, dtype=BF16), pp=v(F, 2 * chan // F, tok),
        rs=v(F, 2 * chan // F, tok), pall=v(F, 2 * chan // F, tok), psum=v(2 * chan // F, tok),
        rs_send=dma((F,)), rs_recv=dma((F,)), ag_send=dma((F,)), ag_recv=dma((F,)), wh_send=dma((F,)), wh_recv=dma((F,)), whs_sem=dma((2, F)), ms_sem=dma((2,)),
        mm_sem=dma((2,)), mx_sem=dma((2,)),
        attbuf=v(tok, F * wide, dtype=BF16), edge_out=v(8, 128), edge_in=v(8, 128),
        flip_out=v(chan, tok), flip_in=v(chan, tok), last_out=v(8, 2 * chan), last_in=v(8, 2 * chan),
        part=v(2, 4, *block), cbuf=v(4, *block), zbuf=v(4, *block), nbuf=v(4, *block), hbuf=v(*block), hbuf_in=v(*block),
        quart=v(Z // 4, *block), full=v(2, 4, *block),
        att_send=dma((F,)), att_recv=dma((F,)), edge_sem=dma((2,)), flip_sem=dma((2,)), last_sem=dma((2,)),
        core_sem=dma((2,)), half_sem=dma((2,)), zs_send=dma((4,)), zs_recv=dma((4,)), zq_send=dma((Z // 4,)),
        zq_recv=dma((Z // 4,)), zg_send=dma((4,)), zg_recv=dma((4,)), core2_sem=dma((2,)),
    )


NAMES = tuple(shapes(8, 64, 128, 256, 48, 256, 64, 384))


def shards(F, C, latents, stream, queries, key_rows, value_rows, w_mix, w_head):
    tok, chan = latents.shape
    share, chan2 = w_head.shape
    width = queries.shape[1]
    w_t = w_mix.T
    vmem = pl.BlockSpec(memory_space=pltpu.VMEM)
    flipped, grad = pl.pallas_call(
        functools.partial(kernel, F, C),
        out_shape=(
            jax.ShapeDtypeStruct((chan, tok), F32),
            jax.ShapeDtypeStruct((share, chan2), F32),
        ),
        in_specs=[pl.BlockSpec(memory_space=pl.ANY)] * 7,
        out_specs=(vmem, vmem),
        scratch_shapes=list(shapes(F, C, tok, width, *w_t.shape, chan, share).values()),
        compiler_params=pltpu.CompilerParams(
            collective_id=0, has_side_effects=True, vmem_limit_bytes=60 * 1024 * 1024
        ),
        name="coupling",
    )(latents.T, stream, queries, key_rows, value_rows, w_t, w_head.reshape(-1, 2, w_t.shape[0], chan2))
    return flipped.T, grad


def solution(mesh):
    return jax.shard_map(
        functools.partial(shards, mesh.shape["fsdp"], mesh.shape["ctx"]),
        mesh=mesh,
        in_specs=(
            P("ctx", None),
            P("ctx", None),
            P("ctx", "fsdp"),
            P("ctx", "fsdp"),
            P("ctx", "fsdp"),
            P("fsdp", "ctx"),
            P("fsdp", None),
        ),
        out_specs=(P("ctx", None), P("fsdp", None)),
        check_vma=False,
    )
```

```python
import functools
import math

import jax
import jax.numpy as jnp
from jax import lax
from jax.experimental import pallas as pl
from jax.experimental.pallas import tpu as pltpu
from jax.sharding import PartitionSpec as P

HD = 128
MESH = pl.DeviceIdType.MESH
F32, BF16 = jnp.float32, jnp.bfloat16
NT_DIMS = (((1,), (1,)), ((), ()))
SCALE = HD**-0.5 * math.log2(math.e)


def remote(src, dst, send, recv, f, c):
    return pltpu.make_async_remote_copy(
        src_ref=src, dst_ref=dst, send_sem=send, recv_sem=recv, device_id=(f, c), device_id_type=MESH
    )


def greet(barrier, f, c):
    pl.semaphore_signal(barrier, inc=1, device_id=(f, c), device_id_type=MESH)


class Place:
    def __init__(self, F, C):
        self.F, self.C, self.Z = F, C, C // 4
        self.f, self.c = lax.axis_index("fsdp"), lax.axis_index("ctx")
        self.row = self.f // (F // 2)
        self.half = self.c // (C // 2)
        self.z = lax.rem(self.c, C // 2) // 2
        self.k = lax.rem(self.c, 2)
        self.sib = self.c + 1 - 2 * self.k
        self.mate = lax.rem(self.c + C // 2, C)
        self.prev, self.next = lax.rem(self.c + C - 1, C), lax.rem(self.c + 1, C)

    def at(self, half, z, k):
        return half * (self.C // 2) + z * 2 + k

    def plane(self, r):
        i = lax.rem(self.half * self.F + self.f + r, 2 * self.F)
        return lax.rem(i, self.F), self.at(i // self.F, self.z, self.k)

    def zrel(self, by):
        return lax.rem(self.z + by + self.Z, self.Z)


def dot_nt(a, b):
    return lax.dot_general(a, b, NT_DIMS, preferred_element_type=F32)


def split3(x):
    a = x.astype(BF16)
    rest = x - a.astype(F32)
    b = rest.astype(BF16)
    return a, b, (rest - b.astype(F32)).astype(BF16)


def entry(p, q_ref, k_ref, v_ref, w_ref, kbuf, vbuf, wbuf, qbuf, in_sem):
    z, k = p.z, p.k
    loads = [
        pltpu.make_async_copy(k_ref, kbuf.at[z, k], in_sem.at[0]),
        pltpu.make_async_copy(v_ref, vbuf.at[z, k], in_sem.at[1]),
        pltpu.make_async_copy(w_ref, wbuf.at[z], in_sem.at[2]),
        pltpu.make_async_copy(q_ref, qbuf, in_sem.at[3]),
    ]
    for load in loads:
        load.start()
    barrier = pltpu.get_barrier_semaphore()
    for c in (p.at(p.half, p.zrel(1), k), p.at(p.half, p.zrel(-1), k), p.sib, p.prev, p.next):
        greet(barrier, p.f, c)
    for r in (2, -2):
        greet(barrier, p.f, p.at(p.half, p.zrel(r), k))

    @pl.loop(1, 2 * p.F)
    def _(r):
        greet(barrier, *p.plane(r))

    for load in loads:
        load.wait()
    pl.semaphore_wait(barrier, 7 + 2 * p.F - 1)


class Weights:
    def __init__(
        self, p, wbuf, whv, stream, sp, mp, m_in, m_half, m_in2, mall, m3,
        wh_send, wh_recv, whs_sem, ms_sem, mm_sem, mx_sem,
    ):
        self.p, self.wbuf, self.whv, self.stream, self.sp = p, wbuf, whv, stream, sp
        self.mp, self.m_in, self.m_half, self.m_in2, self.mall = mp, m_in, m_half, m_in2, mall
        self.m3 = m3
        self.wh_sems = (wh_send, wh_recv)
        f, k = p.f, p.k
        self.whs_sem, self.mx_sem = whs_sem, mx_sem
        self.to_sib = remote(mp.at[1 - k], m_in, ms_sem.at[0], ms_sem.at[1], f, p.sib)
        self.to_mate = remote(m_half, m_in2, mm_sem.at[0], mm_sem.at[1], f, p.mate)

    def own(self, fs):
        groups = self.p.F // 2
        per = self.p.Z // groups
        return fs // groups, lax.rem(fs, groups) * per, per

    def rows(self, fs, core):
        h, at, per = self.own(fs)
        return self.whv.at[h, pl.ds(at + core * (per // 2), per // 2)]

    def head_copy(self, r, fs):
        p = self.p
        send, recv = self.wh_sems
        return remote(self.rows(fs, p.k), self.rows(fs, p.k), send.at[r], recv.at[fs], lax.rem(p.f + r, p.F), p.c)

    def beside(self, core, fs):
        return remote(
            self.rows(fs, core), self.rows(fs, core), self.whs_sem.at[0, fs], self.whs_sem.at[1, fs], self.p.f, self.p.sib
        )

    def start(self):
        @pl.loop(1, self.p.F)
        def _(r):
            self.head_copy(r, self.p.f).start()

    def share(self):
        p = self.p

        @pl.loop(1, p.F)
        def _(r):
            fs = lax.rem(p.f + r, p.F)
            self.head_copy(r, fs).wait_recv()
            self.beside(p.k, fs).start()

    def partial(self):
        p = self.p

        @pl.loop(1, p.F)
        def _(r):
            self.beside(1 - p.k, lax.rem(p.f + r, p.F)).wait_recv()

        width = self.wbuf.shape[2]
        rows = self.whv[p.half, :, p.k].reshape(-1, 128)
        pieces = self.wbuf[...].reshape(-1, width)
        out = jnp.dot(rows.astype(F32).T.astype(BF16), pieces, preferred_element_type=F32)
        self.mp[...] = out.reshape(self.mp.shape)
        self.to_sib.start()

    def halves(self):
        self.to_sib.wait_recv()
        self.m_half[...] = self.mp[self.p.k] + self.m_in[...]
        self.to_mate.start()

    def whole(self):
        self.to_mate.wait_recv()
        self.mall[self.p.k] = self.m_half[...] + self.m_in2[...]
        self.across(self.p.k).start()

    def across(self, core):
        return remote(self.mall.at[core], self.mall.at[core], self.mx_sem.at[0], self.mx_sem.at[1], self.p.f, self.p.sib)

    def settle(self):
        self.across(1 - self.p.k).wait_recv()
        for i, part in enumerate(split3(self.mall[...].reshape(self.m3.shape[1:]))):
            self.m3[i] = part

    def stream_part(self):
        self.sp[...] = jnp.dot(self.stream[...], self.whv[...].reshape(-1, 128), preferred_element_type=F32).T

    def drain(self):
        p = self.p

        @pl.loop(1, p.F)
        def _(r):
            self.head_copy(r, p.f).wait_send()
            self.beside(p.k, lax.rem(p.f + r, p.F)).wait_send()

        self.to_sib.wait_send()
        self.to_mate.wait_send()
        self.across(p.k).wait_send()


def attend_phase(
    p, weights, q_ref, kbuf, vbuf, wbuf, q2, m_s, l_s, acc_s, o_in, st_out, st_in, tbuf, att_ref, wt_ref,
    ring_send, ring_recv, sib_send, sib_recv, w_send, w_recv, w2_send, w2_recv, ws_sem, q_sem, o_send, o_recv,
):
    F = p.F
    f, z, k, half, Z = p.f, p.z, p.k, p.half, p.Z
    steps, groups = Z // 2, F // 2
    per = Z // groups
    tok = q_ref.shape[0]
    wide = wbuf.shape[2]
    above, below = p.at(half, p.zrel(1), k), p.at(half, p.zrel(-1), k)
    mine = p.row == half

    m_s[...] = jnp.full_like(m_s, -1e30)
    l_s[...] = jnp.zeros_like(l_s)
    acc_s[...] = jnp.zeros_like(acc_s)

    def buf(kind):
        return kbuf if kind % 2 == 0 else vbuf

    def origin(kind, s):
        return p.zrel(-s) if kind < 2 else p.zrel(s)

    def ring(kind, s, o):
        return remote(
            buf(kind).at[o, k], buf(kind).at[o, k], ring_send.at[kind, s], ring_recv.at[kind, s],
            f, above if kind < 2 else below,
        )

    def beside(kind, s, core):
        o = origin(kind, s)
        return remote(
            buf(kind).at[o, core], buf(kind).at[o, core], sib_send.at[kind, s], sib_recv.at[kind, s], f, p.sib
        )

    def wring(up, dist, o):
        by = 2 - dist % 2 if isinstance(dist, int) else 2 - lax.rem(dist, 2)
        to = p.zrel(by) if up == 0 else p.zrel(-by)
        return remote(
            wbuf.at[o], wbuf.at[o], w_send.at[up, dist], w_recv.at[up, dist], f, p.at(half, to, k)
        )

    for kind in (0, 2, 1, 3):
        ring(kind, 1, z).start()
    for up in (0, 1):
        wring(up, 1, z).start()
        wring(up, 2, z).start()
    for kind in (0, 1):
        beside(kind, 0, k).start()
    to_mate = remote(q_ref, q2, q_sem.at[0], q_sem.at[1], f, p.mate)

    @pl.when(half == 1)
    def _():
        to_mate.start()

    weights.start()

    def fold(who, blocks, masked=False):
        q = q_ref if who == 0 else q2
        heads = [slice(h * HD, (h + 1) * HD) for h in range(2)]

        def rows(ref, o, h):
            return ref[o, :, :, heads[h]].reshape(2 * tok, HD)

        scores = [[dot_nt(q[:, heads[h]], rows(kbuf, o, h)) for o in blocks] for h in range(2)]
        if masked:
            at = lax.broadcasted_iota(jnp.int32, (tok, 2 * tok), 1)
            seen = at <= k * tok + lax.broadcasted_iota(jnp.int32, (tok, 2 * tok), 0)
            scores = [[jnp.where(seen, x, -1e30) for x in per_head] for per_head in scores]
        parts, m_old, m_new = [], [], []
        for h in range(2):
            parts.append([x[:, i * tok : (i + 1) * tok] for x in scores[h] for i in range(2)])
            top = jnp.max(functools.reduce(jnp.maximum, parts[h]), axis=1, keepdims=True)
            m_old.append(m_s[who, h])
            m_new.append(jnp.maximum(m_old[h], top))
        for h in range(2):
            keep = jnp.exp2((m_old[h] - m_new[h]) * SCALE)
            e = [jnp.exp2((x - m_new[h]) * SCALE) for x in parts[h]]
            m_s[who, h] = m_new[h]
            l_s[who, h] = l_s[who, h] * keep + functools.reduce(jnp.add, e)
            acc = acc_s[who, h] * keep
            for i, o in enumerate(blocks):
                both = jnp.concatenate([e[2 * i].astype(BF16), e[2 * i + 1].astype(BF16)], axis=1)
                acc = acc + jnp.dot(both, rows(vbuf, o, h), preferred_element_type=F32)
            acc_s[who, h] = acc

    def arrive(kind, s):
        o = origin(kind, s)
        ring(kind, s, o).wait_recv()
        last = steps if kind < 2 else steps - 1

        @pl.when(s < last)
        def _():
            ring(kind, s + 1, o).start()

        beside(kind, s, k).start()

    def w_origin(up, dist):
        return p.zrel(-dist) if up == 0 else p.zrel(dist)

    def w_arrive(s):
        for up in (0, 1):
            last = steps if up == 0 else steps - 1
            o = w_origin(up, 2 * s - 1)
            wring(up, 2 * s - 1, o).wait_recv()
            to_plane(o)

            @pl.when(2 * s <= last)
            def _():
                o = w_origin(up, 2 * s)
                wring(up, 2 * s, o).wait_recv()

                @pl.when(2 * s + 1 <= last)
                def _():
                    wring(up, 2 * s + 1, o).start()

                @pl.when(2 * s + 2 <= last)
                def _():
                    wring(up, 2 * s + 2, o).start()

                to_plane(o)

    def plane_copy(o, h):
        return remote(
            wbuf.at[o], wt_ref.at[lax.rem(o, per), k, :, pl.ds(pl.multiple_of(f * wide, wide), wide)],
            w2_send.at[o, h], w2_recv.at[f], half * groups + o // per, p.at(h, z, k),
        )

    def is_self(o, h):
        return jnp.logical_and(half * groups + o // per == f, half == h)

    def to_plane(o):
        for h in range(2):

            @pl.when(jnp.logical_not(is_self(o, h)))
            def _():
                plane_copy(o, h).start()

            @pl.when(is_self(o, h))
            def _():
                wt_ref[lax.rem(o, per), k, :, pl.ds(pl.multiple_of(f * wide, wide), wide)] = wbuf[o]

    def first_fold():
        beside(0, 0, 1 - k).wait_recv()
        beside(1, 0, 1 - k).wait_recv()

        @pl.when(half == 0)
        def _():
            to_mate.wait_recv()
            fold(1, (z,))

        fold(0, (z,), masked=True)

    def fold_step(s):
        low, high = origin(0, s), origin(2, s)
        for kind in range(4):
            beside(kind, s, 1 - k).wait_recv()
        from_low, from_high = z >= s, z + s >= Z

        @pl.when(half == 0)
        def _():
            fold(1, (low, high))

        @pl.when(jnp.logical_and(from_low, from_high))
        def _():
            fold(0, (low, high))

        @pl.when(jnp.logical_and(from_low, jnp.logical_not(from_high)))
        def _():
            fold(0, (low,))

        @pl.when(jnp.logical_and(from_high, jnp.logical_not(from_low)))
        def _():
            fold(0, (high,))

    to_plane(z)

    def from_plane(fs):
        return remote(
            wbuf.at[pl.ds(0, per)], wt_ref.at[:, k, :, pl.ds(fs * wide, wide)],
            w2_send.at[0, 0], w2_recv.at[fs], fs, p.at(p.row, z, k),
        )

    across = remote(wt_ref.at[:, k], wt_ref.at[:, k], ws_sem.at[0], ws_sem.at[1], f, p.sib)

    def collect():
        for fs in range(F):

            @pl.when(jnp.logical_not(jnp.logical_and(mine, fs == f)))
            def _():
                from_plane(fs).wait_recv()

        across.start()

    @pl.loop(1, steps + 1)
    def _(s):
        arrive(0, s)

        @pl.when(s < steps)
        def _():
            arrive(2, s)

        arrive(1, s)

        @pl.when(s < steps)
        def _():
            arrive(3, s)

        @pl.when(jnp.logical_and(s > 1, s <= steps // 2 + 1))
        def _():
            w_arrive(s - 1)

        @pl.when(s == 3)
        def _():
            weights.share()

        @pl.when(s == steps // 2 + 1)
        def _():
            weights.partial()

        @pl.when(s == steps // 2 + 2)
        def _():
            weights.halves()

        @pl.when(s == steps)
        def _():
            weights.whole()

        @pl.when(s == 1)
        def _():
            first_fold()

        @pl.when(s > 1)
        def _():
            fold_step(s - 1)

    far = origin(0, steps)
    beside(0, steps, 1 - k).wait_recv()
    beside(1, steps, 1 - k).wait_recv()
    lane = lax.broadcasted_iota(jnp.int32, (tok, 128), 1)
    back = [
        remote(acc_s.at[1], o_in, o_send.at[0], o_recv.at[0], f, p.mate),
        remote(st_out, st_in, o_send.at[1], o_recv.at[1], f, p.mate),
    ]

    @pl.when(half == 0)
    def _():
        fold(1, (far,))
        back[0].start()
        stats = jnp.zeros((tok, 128), F32)
        for h in range(2):
            stats = jnp.where(lane == h, m_s[1, h], stats)
            stats = jnp.where(lane == 2 + h, jnp.sum(l_s[1, h], axis=1, keepdims=True), stats)
        st_out[...] = stats.T[:8]
        back[1].start()

    @pl.when(z >= steps)
    def _():
        fold(0, (far,))

    weights.settle()
    collect()

    def store(h, acc, total):
        att_ref[:, h * HD : (h + 1) * HD] = (acc / total).astype(BF16)

    @pl.when(half == 0)
    def _():
        for h in range(2):
            store(h, acc_s[0, h], jnp.sum(l_s[0, h], axis=1, keepdims=True))

    @pl.when(half == 1)
    def _():
        back[0].wait_recv()
        back[1].wait_recv()
        tbuf[...] = jnp.zeros_like(tbuf)
        tbuf[:8] = st_in[...]
        stats = tbuf[...].T
        for h in range(2):
            m_a, l_a = m_s[0, h], jnp.sum(l_s[0, h], axis=1, keepdims=True)
            m_b = jnp.max(jnp.where(lane == h, stats, -3e38), axis=1, keepdims=True)
            l_b = jnp.sum(jnp.where(lane == 2 + h, stats, 0.0), axis=1, keepdims=True)
            m = jnp.maximum(m_a, m_b)
            e_a, e_b = jnp.exp2((m_a - m) * SCALE), jnp.exp2((m_b - m) * SCALE)
            store(h, acc_s[0, h] * e_a + o_in[h] * e_b, l_a * e_a + l_b * e_b)

    def early():
        weights.stream_part()
        remote(wt_ref.at[:, 1 - k], wt_ref.at[:, 1 - k], ws_sem.at[0], ws_sem.at[1], f, p.sib).wait_recv()

    def drain():
        attend_drain(p, ring, beside, wring, plane_copy, is_self, across, back, to_mate)

    return early, drain


def attend_drain(p, ring, beside, wring, plane_copy, is_self, across, back, to_mate):
    z, k, half, steps = p.z, p.k, p.half, p.Z // 2

    @pl.loop(1, steps + 1)
    def _(s):
        for kind in (0, 1):
            ring(kind, s, z).wait_send()
            beside(kind, s, k).wait_send()
        wring(0, s, z).wait_send()

        @pl.when(s < steps)
        def _():
            for kind in (2, 3):
                ring(kind, s, z).wait_send()
                beside(kind, s, k).wait_send()
            wring(1, s, z).wait_send()

    for kind in (0, 1):
        beside(kind, 0, k).wait_send()

    @pl.loop(0, p.Z)
    def _(o):
        for h in range(2):

            @pl.when(jnp.logical_not(is_self(o, h)))
            def _():
                plane_copy(o, h).wait_send()

    across.wait_send()

    @pl.when(half == 0)
    def _():
        back[0].wait_send()
        back[1].wait_send()

    @pl.when(half == 1)
    def _():
        to_mate.wait_send()


def head_phase(
    p, early, drain, att_ref, wt_ref, stream, sp, m3, lat_ref, flip_ref, hg_ref, pp, rs, pall, psum,
    attbuf, edge_out, edge_in, flip_out, flip_in, last_out, last_in, part, cbuf, zbuf, nbuf, hbuf, hbuf_in, qbuf, full,
    rs_send, rs_recv, ag_send, ag_recv, att_send, att_recv, edge_sem, flip_sem, last_sem, core_sem, half_sem, zs_send, zs_recv, zq_send, zq_recv,
    zg_send, zg_recv, core2_sem,
):
    F, C = p.F, p.C
    f, c, z, k, half, Z = p.f, p.c, p.z, p.k, p.half, p.Z
    tok, wide = att_ref.shape
    chan = lat_ref.shape[0]
    mirror, mirror2 = C - 1 - c, lax.rem(2 * C - 2 - c, C)
    own_last = mirror2 == c
    lane = lax.broadcasted_iota(jnp.int32, (chan, tok), 1)

    def as_column(row):
        return jnp.broadcast_to(row, (tok, 128)).T

    mine = pl.ds(pl.multiple_of(f * wide, wide), wide)
    own = att_ref[...]
    pp[...] = (dot_nt(m3[2], own) + dot_nt(m3[1], own) + dot_nt(m3[0], own)).reshape(pp.shape)

    @pl.loop(1, F)
    def _(r):
        to = lax.rem(f + r, F)
        remote(pp.at[to], rs.at[f], rs_send.at[r], rs_recv.at[f], to, c).start()

    attbuf[:, mine] = att_ref[...]

    def att_copy(r):
        return remote(
            att_ref, attbuf.at[:, mine], att_send.at[r], att_recv.at[f], lax.rem(f + r, F), c
        )

    @pl.loop(1, F)
    def _(r):
        att_copy(r).start()

    lat_t = lat_ref[...]
    edge_out[...] = jnp.concatenate([lat_t, lat_t], axis=0).T[:8]
    edge = remote(edge_out, edge_in, edge_sem.at[0], edge_sem.at[1], f, p.prev)
    edge.start()
    share = hg_ref.shape[0]
    rs[f] = pp[f]

    @pl.loop(1, F)
    def _(r):
        fs = lax.rem(f + r, F)
        remote(pp.at[fs], rs.at[fs], rs_send.at[r], rs_recv.at[fs], fs, c).wait_recv()

    psum[...] = jnp.sum(rs[...], axis=0)

    @pl.loop(1, F)
    def _(r):
        remote(psum, pall.at[f], ag_send.at[r], ag_recv.at[f], lax.rem(f + r, F), c).start()

    pall[f] = psum[...]
    stream_t = stream[:, pl.ds(pl.multiple_of(f * share, 128), share)].astype(F32).T
    early()
    edge.wait_recv()
    lat_next = jnp.where(lane == tok - 1, as_column(edge_in[0:1])[:chan], pltpu.roll(lat_t, tok - 1, 1))

    @pl.loop(1, F)
    def _(r):
        fs = lax.rem(f + r, F)
        there = pl.ds(pl.multiple_of(fs * wide, wide), wide)
        remote(att_ref, attbuf.at[:, there], att_send.at[r], att_recv.at[fs], fs, c).wait_recv()

    heads = attbuf[...]
    resid = stream_t + dot_nt(wt_ref[...].reshape(share, F * wide), heads)
    r_hi, r_mid, r_lo = split3(resid)

    @pl.loop(1, F)
    def _(r):
        fs = lax.rem(f + r, F)
        remote(psum, pall.at[fs], ag_send.at[r], ag_recv.at[fs], fs, c).wait_recv()

    pred = sp[...] + pall[...].reshape(2 * chan, tok)
    final = jnp.logical_and(c == C - 1, lane == tok - 1)
    shift = jnp.where(final, 0.0, pred[:chan])
    log_scale = jnp.where(final, 0.0, pred[chan:])
    inverse = jnp.exp(-log_scale)
    white = (lat_next - shift) * inverse
    loss_scale = float(tok * C) ** -0.5
    d_shift = jnp.where(final, 0.0, -white * inverse * loss_scale)
    d_log = jnp.where(final, 0.0, (1.0 - white * white) * loss_scale)
    d_hi, d_mid, d_lo = split3(jnp.concatenate([d_shift, d_log], axis=0))
    grad = dot_nt(r_hi, d_lo) + dot_nt(r_lo, d_hi) + dot_nt(r_mid, d_mid)
    grad += dot_nt(r_hi, d_mid) + dot_nt(r_mid, d_hi)
    grad += dot_nt(r_hi, d_hi)
    part[...] = grad.reshape(part.shape)

    core_copy = remote(part.at[1 - k], cbuf, core_sem.at[0], core_sem.at[1], f, p.sib)
    core_copy.start()

    t_i = lax.broadcasted_iota(jnp.int32, (tok, tok), 0)
    r_i = lax.broadcasted_iota(jnp.int32, (tok, tok), 1)
    swap = jnp.where(t_i == tok - 2 - r_i, 1.0, 0.0).astype(BF16)
    w_hi, w_mid, w_lo = split3(white)
    turned = jnp.dot(w_hi, swap, preferred_element_type=F32) + jnp.dot(w_mid, swap, preferred_element_type=F32)
    flip_out[...] = turned + jnp.dot(w_lo, swap, preferred_element_type=F32)
    last_out[...] = jnp.concatenate([white, white], axis=0).T[tok - 8 :]
    flip_copy = remote(flip_out, flip_in, flip_sem.at[0], flip_sem.at[1], f, mirror)
    last_copy = remote(last_out, last_in, last_sem.at[0], last_sem.at[1], f, mirror2)

    core_copy.wait_recv()
    zbuf[...] = part[k] + cbuf[...]
    g, q = lax.rem(z, 4), z // 4
    quads = Z // 4

    def near(r):
        i = lax.rem(g + r, 4)
        return i, p.at(half, q * 4 + i, k)

    def far(r):
        i = lax.rem(q + r, quads)
        return i, p.at(half, i * 4 + g, k)

    for r in range(1, 4):
        i, there = near(r)
        remote(zbuf.at[i], nbuf.at[g], zs_send.at[r], zs_recv.at[g], f, there).start()
    nbuf[g] = zbuf[g]
    for r in range(1, 4):
        i, there = near(r)
        remote(zbuf.at[i], nbuf.at[i], zs_send.at[r], zs_recv.at[i], f, there).wait_recv()
    hbuf[...] = nbuf[0] + nbuf[1] + nbuf[2] + nbuf[3]
    half_copy = remote(hbuf, hbuf_in, half_sem.at[0], half_sem.at[1], f, p.mate)
    half_copy.start()
    flip_copy.start()

    @pl.when(own_last)
    def _():
        last_in[...] = last_out[...]

    @pl.when(jnp.logical_not(own_last))
    def _():
        last_copy.start()

    half_copy.wait_recv()
    qbuf[q] = hbuf[...] + hbuf_in[...]
    for r in range(1, quads):
        i, there = far(r)
        remote(qbuf.at[q], qbuf.at[q], zq_send.at[r], zq_recv.at[q], f, there).start()
    drain()

    @pl.loop(1, F)
    def _(r):
        att_copy(r).wait_send()
        remote(pp.at[0], rs.at[0], rs_send.at[r], rs_recv.at[0], lax.rem(f + r, F), c).wait_send()
        remote(psum, pall.at[0], ag_send.at[r], ag_recv.at[0], lax.rem(f + r, F), c).wait_send()

    for r in range(1, quads):
        i, there = far(r)
        remote(qbuf.at[i], qbuf.at[i], zq_send.at[r], zq_recv.at[i], f, there).wait_recv()
    full[k, g] = functools.reduce(jnp.add, [qbuf[i] for i in range(quads)])
    for r in range(1, 4):
        i, there = near(r)
        remote(full.at[k, g], full.at[k, g], zg_send.at[r], zg_recv.at[g], f, there).start()

    flip_copy.wait_recv()

    @pl.when(jnp.logical_not(own_last))
    def _():
        last_copy.wait_recv()

    flip_ref[...] = jnp.where(lane == tok - 1, as_column(last_in[7:8])[:chan], flip_in[...])

    for r in range(1, 4):
        i, there = near(r)
        remote(full.at[k, i], full.at[k, i], zg_send.at[r], zg_recv.at[i], f, there).wait_recv()
    to_core = remote(full.at[k], full.at[k], core2_sem.at[0], core2_sem.at[1], f, p.sib)
    to_core.start()
    remote(full.at[1 - k], full.at[1 - k], core2_sem.at[0], core2_sem.at[1], f, p.sib).wait_recv()
    hg_ref[...] = full[...].reshape(hg_ref.shape)

    for r in range(1, 4):
        i, there = near(r)
        remote(zbuf.at[i], nbuf.at[0], zs_send.at[r], zs_recv.at[0], f, there).wait_send()
        remote(full.at[k, g], full.at[k, g], zg_send.at[r], zg_recv.at[0], f, there).wait_send()
    for r in range(1, quads):
        i, there = far(r)
        remote(qbuf.at[q], qbuf.at[q], zq_send.at[r], zq_recv.at[0], f, there).wait_send()

    for copy in (edge, core_copy, half_copy, flip_copy, to_core):
        copy.wait_send()

    @pl.when(jnp.logical_not(own_last))
    def _():
        last_copy.wait_send()


def kernel(F, C, lat_hbm, stream_hbm, q_hbm, k_hbm, v_hbm, w_hbm, wh_hbm, flip_ref, hg_ref, *scratch):
    p = Place(F, C)
    bufs = dict(zip(NAMES, scratch))
    g = bufs.__getitem__
    weights = Weights(p, *map(g, WEIGHTS))
    h, at, per = weights.own(p.f)
    early_loads = [pltpu.make_async_copy(wh_hbm, g("whv").at[h, pl.ds(at, per)], g("in_sem").at[4])]
    late = [
        pltpu.make_async_copy(stream_hbm, g("stream"), g("in_sem").at[5]),
        pltpu.make_async_copy(lat_hbm, g("lat"), g("in_sem").at[6]),
    ]
    for copy in early_loads:
        copy.start()
    entry(p, q_hbm, k_hbm, v_hbm, w_hbm, g("kbuf"), g("vbuf"), g("wbuf"), g("qbuf"), g("in_sem"))
    for copy in late:
        copy.start()
    for copy in early_loads + late:
        copy.wait()
    early, drain = attend_phase(p, weights, *map(g, ATTEND))
    head_phase(
        p, early, lambda: (drain(), weights.drain()), g("att"), g("wt"), g("stream"), g("sp"), g("m3"), g("lat"), flip_ref, hg_ref, *map(g, HEAD)
    )


WEIGHTS = (
    "wbuf", "whv", "stream", "sp", "mp", "m_in", "m_half", "m_in2", "mall", "m3",
    "wh_send", "wh_recv", "whs_sem", "ms_sem", "mm_sem", "mx_sem",
)
ATTEND = (
    "qbuf", "kbuf", "vbuf", "wbuf", "q2", "m_s", "l_s", "acc_s", "o_in", "st_out", "st_in", "tbuf", "att", "wt",
    "ring_send", "ring_recv", "sib_send", "sib_recv", "w_send", "w_recv", "w2_send", "w2_recv", "ws_sem", "q_sem",
    "o_send", "o_recv",
)
HEAD = (
    "pp", "rs", "pall", "psum", "attbuf", "edge_out", "edge_in", "flip_out", "flip_in", "last_out", "last_in", "part", "cbuf", "zbuf", "nbuf", "hbuf",
    "hbuf_in", "quart", "full", "rs_send", "rs_recv", "ag_send", "ag_recv", "att_send", "att_recv", "edge_sem", "flip_sem", "last_sem", "core_sem", "half_sem",
    "zs_send", "zs_recv", "zq_send", "zq_recv", "zg_send", "zg_recv", "core2_sem",
)


def shapes(F, C, tok, width, cols, wide, chan, share):
    Z = C // 4
    per, n = Z // (F // 2), Z // 2 + 1
    block = (share // 8, 2 * chan)
    dma = pltpu.SemaphoreType.DMA

    def v(*shape, dtype=F32):
        return pltpu.VMEM(shape, dtype)

    return dict(
        qbuf=v(tok, width, dtype=BF16), kbuf=v(Z, 2, tok, width, dtype=BF16), vbuf=v(Z, 2, tok, width, dtype=BF16),
        wbuf=v(Z, cols, wide, dtype=BF16), q2=v(tok, width, dtype=BF16), m_s=v(2, 2, tok, 128), l_s=v(2, 2, tok, 128),
        acc_s=v(2, 2, tok, HD), o_in=v(2, tok, HD), st_out=v(8, tok), st_in=v(8, tok), tbuf=v(128, tok),
        att=v(tok, width, dtype=BF16), wt=v(per, 2, cols, F * wide, dtype=BF16),
        ring_send=dma((4, n)), ring_recv=dma((4, n)), sib_send=dma((4, n)), sib_recv=dma((4, n)),
        w_send=dma((2, n)), w_recv=dma((2, n)), w2_send=dma((Z, 2)), w2_recv=dma((F,)), ws_sem=dma((2,)),
        q_sem=dma((2,)), o_send=dma((2,)), o_recv=dma((2,)), in_sem=dma((7,)),
        stream=v(tok, share * F, dtype=BF16), lat=v(chan, tok), whv=v(2, Z, 2, cols, 2 * chan, dtype=BF16),
        sp=v(2 * chan, tok), mp=v(2, chan, wide), m_in=v(chan, wide), m_half=v(chan, wide), m_in2=v(chan, wide),
        mall=v(2, chan, wide), m3=v(3, 2 * chan, wide, dtype=BF16), pp=v(F, 2 * chan // F, tok),
        rs=v(F, 2 * chan // F, tok), pall=v(F, 2 * chan // F, tok), psum=v(2 * chan // F, tok),
        rs_send=dma((F,)), rs_recv=dma((F,)), ag_send=dma((F,)), ag_recv=dma((F,)), wh_send=dma((F,)), wh_recv=dma((F,)), whs_sem=dma((2, F)), ms_sem=dma((2,)),
        mm_sem=dma((2,)), mx_sem=dma((2,)),
        attbuf=v(tok, F * wide, dtype=BF16), edge_out=v(8, 128), edge_in=v(8, 128),
        flip_out=v(chan, tok), flip_in=v(chan, tok), last_out=v(8, 2 * chan), last_in=v(8, 2 * chan),
        part=v(2, 4, *block), cbuf=v(4, *block), zbuf=v(4, *block), nbuf=v(4, *block), hbuf=v(*block), hbuf_in=v(*block),
        quart=v(Z // 4, *block), full=v(2, 4, *block),
        att_send=dma((F,)), att_recv=dma((F,)), edge_sem=dma((2,)), flip_sem=dma((2,)), last_sem=dma((2,)),
        core_sem=dma((2,)), half_sem=dma((2,)), zs_send=dma((4,)), zs_recv=dma((4,)), zq_send=dma((Z // 4,)),
        zq_recv=dma((Z // 4,)), zg_send=dma((4,)), zg_recv=dma((4,)), core2_sem=dma((2,)),
    )


NAMES = tuple(shapes(8, 64, 128, 256, 48, 256, 64, 384))


def shards(F, C, latents, stream, queries, key_rows, value_rows, w_mix, w_head):
    tok, chan = latents.shape
    share, chan2 = w_head.shape
    width = queries.shape[1]
    w_t = w_mix.T
    vmem = pl.BlockSpec(memory_space=pltpu.VMEM)
    flipped, grad = pl.pallas_call(
        functools.partial(kernel, F, C),
        out_shape=(
            jax.ShapeDtypeStruct((chan, tok), F32),
            jax.ShapeDtypeStruct((share, chan2), F32),
        ),
        in_specs=[pl.BlockSpec(memory_space=pl.ANY)] * 7,
        out_specs=(vmem, vmem),
        scratch_shapes=list(shapes(F, C, tok, width, *w_t.shape, chan, share).values()),
        compiler_params=pltpu.CompilerParams(
            collective_id=0, has_side_effects=True, vmem_limit_bytes=60 * 1024 * 1024
        ),
        name="coupling",
    )(latents.T, stream, queries, key_rows, value_rows, w_t, w_head.reshape(-1, 2, w_t.shape[0], chan2))
    return flipped.T, grad


def solution(mesh):
    return jax.shard_map(
        functools.partial(shards, mesh.shape["fsdp"], mesh.shape["ctx"]),
        mesh=mesh,
        in_specs=(
            P("ctx", None),
            P("ctx", None),
            P("ctx", "fsdp"),
            P("ctx", "fsdp"),
            P("ctx", "fsdp"),
            P("fsdp", "ctx"),
            P("fsdp", None),
        ),
        out_specs=(P("ctx", None), P("fsdp", None)),
        check_vma=False,
    )
```
